32 devices in a mesh: dp: 8 (over z, y), fsdp: 4 (over x, core).
Axes of the slice: x: 2, y: 2, z: 4, core: 2. Of those that a mesh axis runs over, the one named last changes fastest.
Arguments:
- tokens: bfloat16 [16, 1024, 1536], P('dp', 'fsdp'), may hold values from -6 to 6
- seq_lengths: int32 [16], P('dp'), may hold values from 256 to 1024, as said below
- seq_buckets: int32 [16], P('dp'), may hold values from 0 to 3, as said below
- bucket_widths: int32 [4], replicated, may hold values from 768 to 6144, as said below
- norm_one_gain: bfloat16 [1536], P(('dp', 'fsdp')), may hold values from 0.099609375 to 1.8984375
- norm_one_bias: bfloat16 [1536], P(('dp', 'fsdp')), may hold values from -3 to 3
- qkv_weight: bfloat16 [1536, 4608], P(('dp', 'fsdp')), may hold values from -0.21875 to 0.21875
- out_weight: bfloat16 [1536, 1536], P(('dp', 'fsdp')), may hold values from -0.4375 to 0.4375
- norm_two_gain: bfloat16 [1536], P(('dp', 'fsdp')), may hold values from 0.099609375 to 1.8984375
- norm_two_bias: bfloat16 [1536], P(('dp', 'fsdp')), may hold values from -3 to 3
- ffn_in_weight: bfloat16 [1536, 6144], P(('dp', 'fsdp')), may hold values from -0.15625 to 0.15625
- ffn_out_weight: bfloat16 [6144, 1536], P(('dp', 'fsdp')), may hold values from -0.15625 to 0.15625
- cotangent: bfloat16 [16, 1024, 1536], P('dp', 'fsdp'), may hold values from -6 to 6
Outputs:
- layer_output: bfloat16 [16, 1024, 1536], P('dp', 'fsdp')
- input_grad: float32 [16, 1024, 1536], P('dp', 'fsdp')
- norm_one_gain_grad: float32 [1536], P(('dp', 'fsdp'))
- norm_one_bias_grad: float32 [1536], P(('dp', 'fsdp'))
- qkv_weight_grad: float32 [1536, 4608], P(('dp', 'fsdp'))
- out_weight_grad: float32 [1536, 1536], P(('dp', 'fsdp'))
- norm_two_gain_grad: float32 [1536], P(('dp', 'fsdp'))
- norm_two_bias_grad: float32 [1536], P(('dp', 'fsdp'))
- ffn_in_weight_grad: float32 [1536, 6144], P(('dp', 'fsdp'))
- ffn_out_weight_grad: float32 [6144, 1536], P(('dp', 'fsdp'))
The draws below stay inside these ranges and needn't reach their ends.
Inputs may be any that keep to these rules, and one draw needn't show every extreme that they name: `seq_lengths`: one sequence has exactly 1024 live positions and one exactly 256. `seq_buckets`: every micro-batch holds at least one sequence. `bucket_widths`: the widths are 768, 1536, 3072 and 6144, each once, in some order.
All inputs are finite; a program needn't handle non-finite values.
Results may differ from the reference program's by a relative error of at most 0.012.
The reference program's roundings to bfloat16 on the way count: a program that leaves them out, or rounds other values in their place, can miss the bound.
Values may be sent and summed in bfloat16 or wider, within the bound.
No kernel may reach another device: no remote copies, remote signals or barrier semaphores. Data moves between devices by JAX's collectives and lax.ppermute only.
A program may use at most 320 MiB of HBM per device.

```python
import jax
import jax.numpy as jnp
from jax import lax

D = 1536
HEADS = 12
HEAD_DIM = 128
FF = 6144
BUCKETS = 4
SEQ = 1024
NSEQ = 16


def draw_seq_lengths(key, part):
    first_key, second_key = jax.random.split(key)
    drawn_lengths = jax.random.randint(first_key, (NSEQ,), SEQ // 4, SEQ + 1)
    longest = jax.random.randint(second_key, (), 0, NSEQ)
    shortest = (longest + 1) % NSEQ
    return drawn_lengths.at[longest].set(SEQ).at[shortest].set(SEQ // 4).astype(jnp.int32)


def draw_seq_buckets(key, part):
    first_key, second_key = jax.random.split(key)
    drawn_buckets = jax.random.randint(first_key, (NSEQ,), 0, BUCKETS)
    placed = jax.random.permutation(second_key, NSEQ)[:BUCKETS]
    return drawn_buckets.at[placed].set(jnp.arange(BUCKETS).astype(jnp.int32)).astype(jnp.int32)


def draw_bucket_widths(key, part):
    order_list = jax.random.permutation(key, BUCKETS).astype(jnp.int32)
    return (FF // 8 * jnp.left_shift(jnp.ones((BUCKETS,), jnp.int32), order_list)).astype(jnp.int32)


def steps_of(key, dims, cuts, smallest, high):
    gain, own = 1.0, jax.random.fold_in(key, 6)
    for axis_at, shards_of in cuts:
        heights = jnp.exp(jax.random.uniform(jax.random.fold_in(own, axis_at), (shards_of,), jnp.float32, smallest / len(cuts), high / len(cuts)))
        gain = gain * jnp.repeat(heights, dims[axis_at] // shards_of).reshape([-1 if axis == axis_at else 1 for axis in range(len(dims))])
    return gain


def noise(rng, dims, scale, reach, pieces=(), kind=jnp.bfloat16):
    level = steps_of(rng, dims, pieces, -0.22, 0.18) if pieces else 1.0
    array = jax.random.normal(rng, dims, jnp.float32) * scale * level
    return jnp.minimum(jnp.maximum(array, -reach), reach).astype(kind)


def setup_inputs(seed: int = 0) -> dict:
    splits = jax.random.split(jax.random.key(seed), 14)
    return {
        "tokens": noise(splits[0], (NSEQ, SEQ, D), 1.0, 6.0, ((0, 8), (1, 4))),
        "seq_lengths": draw_seq_lengths(jax.random.fold_in(splits[13], 71), 0),
        "seq_buckets": draw_seq_buckets(jax.random.fold_in(splits[13], 71), 0),
        "bucket_widths": draw_bucket_widths(jax.random.fold_in(splits[13], 71), 0),
        "norm_one_gain": jnp.clip(1.0 + 0.18 * jax.random.normal(splits[4], (D,), jnp.float32), 0.099609375, 1.8984375).astype(jnp.bfloat16),
        "norm_one_bias": noise(splits[5], (D,), 0.5, 3.0, ((0, 32),)),
        "qkv_weight": noise(splits[6], (D, 3 * D), (D // 2) ** -0.5, 0.21875, ((0, 32),)),
        "out_weight": noise(splits[7], (D, D), (D // 8) ** -0.5, 0.4375, ((0, 32),)),
        "norm_two_gain": jnp.clip(1.0 + 0.18 * jax.random.normal(splits[8], (D,), jnp.float32), 0.099609375, 1.8984375).astype(jnp.bfloat16),
        "norm_two_bias": noise(splits[9], (D,), 0.5, 3.0, ((0, 32),)),
        "ffn_in_weight": noise(splits[10], (D, FF), D ** -0.5, 0.15625, ((0, 32),)),
        "ffn_out_weight": noise(splits[11], (FF, D), (FF // 4) ** -0.5, 0.15625, ((0, 32),)),
        "cotangent": noise(splits[12], (NSEQ, SEQ, D), 1.0, 6.0, ((0, 8), (1, 4))),
    }


@jax.custom_vjp
def low(v):
    return lax.optimization_barrier(v.astype(jnp.bfloat16)).astype(jnp.float32)

@jax.custom_vjp
def low_back(v):
    return v

def low_keep(v):
    return (low(v), None)

def low_pass(kept, grad):
    return (grad,)

def back_keep(v):
    return (v, None)

def back_low(kept, grad):
    return (low(grad),)
low.defvjp(low_keep, low_pass)
low_back.defvjp(back_keep, back_low)

def product(lhs_matrix, rhs_matrix):
    return jnp.dot(lhs_matrix, rhs_matrix, precision=lax.Precision.HIGHEST, preferred_element_type=jnp.float32)

def layer_norm(values, gain_vec, shift_vec):
    center = values - lax.optimization_barrier(jnp.mean(values, axis=-1, keepdims=True))
    spread = lax.optimization_barrier(jnp.mean(center * center, axis=-1, keepdims=True))
    return center * lax.rsqrt(spread + 1e-05) * gain_vec + shift_vec

def rotary(values, cosine, sine_table):
    half_dim = values.shape[-1] // 2
    first_half = values[..., :half_dim]
    second = values[..., half_dim:]
    return jnp.concatenate([first_half * cosine - second * sine_table, second * cosine + first_half * sine_table], axis=-1)

def rotary_tables(positions):
    half_dim = HEAD_DIM // 2
    inverse = 10000.0 ** (-(jnp.arange(half_dim).astype(jnp.float32) * 2.0) / HEAD_DIM)
    angles = positions.astype(jnp.float32)[:, None] * inverse[None, :]
    return (jnp.cos(angles)[:, None, :], jnp.sin(angles)[:, None, :])

def sequence_forward(inputs, weight_set, live_rows, width_mask, cosine, sine_table, allowed):
    gain_one, bias_one, qkv_mat, out_mat, gain_two, bias_two, in_mat, down_mat = weight_set
    seq_rows = inputs.shape[0]
    inv_root = HEAD_DIM ** (-0.5)
    normed = low(layer_norm(inputs, gain_one, bias_one))
    mixed_qkv = low_back(product(normed, qkv_mat))
    queries = low(rotary(mixed_qkv[:, :D].reshape(seq_rows, HEADS, HEAD_DIM), cosine, sine_table))
    key_heads = low(rotary(mixed_qkv[:, D:2 * D].reshape(seq_rows, HEADS, HEAD_DIM), cosine, sine_table))
    values = low(mixed_qkv[:, 2 * D:].reshape(seq_rows, HEADS, HEAD_DIM))
    scores = jnp.einsum('qhd,khd->hqk', queries, key_heads, precision=lax.Precision.HIGHEST) * inv_root
    scores = low_back(scores)
    scores = jnp.where(allowed[None], scores, -1e+30)
    shifted = scores - lax.optimization_barrier(jnp.max(scores, axis=-1, keepdims=True))
    expo = jnp.exp(shifted)
    weights = expo / lax.optimization_barrier(jnp.sum(expo, axis=-1, keepdims=True))
    attended = jnp.einsum('hqk,khd->qhd', low(weights), values, precision=lax.Precision.HIGHEST).reshape(seq_rows, D)
    attended = low(low_back(attended))
    branch = low_back(product(attended, out_mat))
    middle = inputs + branch
    normed_two = low(layer_norm(middle, gain_two, bias_two))
    hidden = low_back(product(normed_two, in_mat))
    active = low(jnp.where(width_mask[None, :], jax.nn.gelu(hidden), 0.0))
    feed_out = low_back(product(active, down_mat))
    return jnp.where(live_rows[:, None], middle + feed_out, 0.0)

def reference(tokens, seq_lengths, seq_buckets, bucket_widths, norm_one_gain, norm_one_bias, qkv_weight, out_weight, norm_two_gain, norm_two_bias, ffn_in_weight, ffn_out_weight, cotangent):
    weight_set = tuple((piece.astype(jnp.float32) for piece in (norm_one_gain, norm_one_bias, qkv_weight, out_weight, norm_two_gain, norm_two_bias, ffn_in_weight, ffn_out_weight)))
    positions = jnp.arange(SEQ).astype(jnp.int32)
    cosine, sine_table = rotary_tables(positions)
    causal = positions[None, :] <= positions[:, None]

    def one_sequence(totals, seq_items):
        inputs, seq_length, seq_bucket, seq_cot = seq_items
        live_rows = positions < seq_length
        prefix_width = jnp.sum(jnp.where(jnp.arange(BUCKETS).astype(jnp.int32) == seq_bucket, bucket_widths, 0))
        width_mask = jnp.arange(FF).astype(jnp.int32) < prefix_width
        allowed = causal & (positions[None, :] < seq_length)

        def forward(inputs_f, weights_f):
            return sequence_forward(inputs_f, weights_f, live_rows, width_mask, cosine, sine_table, allowed)
        result, pullback = jax.vjp(forward, inputs.astype(jnp.float32), weight_set)
        input_part, weight_part = pullback(seq_cot.astype(jnp.float32))
        totals = tuple((total + part_grad for total, part_grad in zip(totals, weight_part)))
        return (totals, (result.astype(jnp.bfloat16), input_part))
    starting = tuple((jnp.zeros(piece.shape, jnp.float32) for piece in weight_set))
    totals, (outputs, input_grads) = lax.scan(one_sequence, starting, (tokens, seq_lengths, seq_buckets, cotangent))
    return (outputs, input_grads, totals[0], totals[1], totals[2], totals[3], totals[4], totals[5], totals[6], totals[7])
```

```python
import functools

import jax
import jax.numpy as jnp
from jax import lax
from jax.experimental import pallas as pl
from jax.experimental.pallas import tpu as pltpu
from jax.sharding import PartitionSpec as P

HEADS = 12
HEAD_DIM = 128
BUCKETS = 4
FSDP = 4

BF = jnp.bfloat16
F32 = jnp.float32
NT = (((1,), (1,)), ((), ()))
TN = (((0,), (0,)), ((), ()))
NN = (((1,), (0,)), ((), ()))


def dot(a, b, dims):
    return lax.dot_general(a, b, dims, preferred_element_type=F32)


def rotary_tables(rows):
    half = HEAD_DIM // 2
    inverse = 10000.0 ** (-(jnp.arange(half).astype(F32) * 2.0) / HEAD_DIM)
    angles = jnp.arange(rows).astype(F32)[:, None] * inverse[None, :]
    cos, sin = jnp.cos(angles), jnp.sin(angles)
    return jnp.concatenate([cos, cos], axis=1), jnp.concatenate([-sin, sin], axis=1)


def normalize(values):
    center = values - jnp.mean(values, axis=-1, keepdims=True)
    spread = jnp.mean(center * center, axis=-1, keepdims=True)
    scale = lax.rsqrt(spread + 1e-05)
    return center * scale, scale


def norm_back(grad, gain, normed, scale):
    scaled = grad * gain
    first = jnp.mean(scaled, axis=-1, keepdims=True)
    second = jnp.mean(scaled * normed, axis=-1, keepdims=True)
    return scale * (scaled - first - normed * second)


def scores_of(query, keys):
    rows, cols = query.shape[0], keys.shape[0]
    scores = dot(query, keys, NT) * (HEAD_DIM ** (-0.5))
    row = lax.broadcasted_iota(jnp.int32, (rows, rows), 0)
    col = lax.broadcasted_iota(jnp.int32, (rows, rows), 1)
    last = jnp.where(col <= row, scores[:, cols - rows :], -1e30)
    if cols == rows:
        return last
    return jnp.concatenate([scores[:, : cols - rows], last], axis=1)


def attend_body(len_ref, own_ref, *refs):
    h_in, (w_ref, wo_ref, cos_ref, sin_ref) = refs[0:4], refs[4:8]
    term_refs, out_refs, turned_refs = refs[8:12], refs[12:16], refs[16:20]
    q_ref, k_ref, v_ref, lse_ref, o_ref = refs[20:25]
    rows = h_in[0].shape[1]
    head, heads = pl.program_id(1), pl.num_programs(1)
    length = len_ref[pl.program_id(0)]
    own = own_ref[0]
    for r in range(FSDP):
        start = pl.multiple_of((own ^ r) * rows, rows)
        at = pl.ds(start, rows)

        @pl.when(start < length)
        def _():
            mixed = dot(h_in[r][0], w_ref[...], NN)
            cos, sin = cos_ref[at, :], sin_ref[at, :]
            for part, target in ((0, q_ref), (1, k_ref)):
                value = mixed[:, part * HEAD_DIM : (part + 1) * HEAD_DIM]
                turned = value * cos + pltpu.roll(value, HEAD_DIM // 2, 1) * sin
                target[0, 0, at, :] = turned.astype(BF)
            v_ref[0, 0, at, :] = mixed[:, 2 * HEAD_DIM :].astype(BF)

        @pl.when(head == 0)
        def _():
            turned_refs[r][0] = h_in[r][0].T

    for b in range(FSDP):
        lo, hi = b * rows, (b + 1) * rows

        @pl.when(lo < length)
        def _():
            scores = scores_of(q_ref[0, 0, lo:hi, :], k_ref[0, 0, :hi, :])
            peak = jnp.max(scores, axis=1, keepdims=True)
            expo = jnp.exp(scores - peak)
            total = jnp.sum(expo, axis=1, keepdims=True)
            probs = (expo * (1.0 / total)).astype(BF)
            o_ref[head, lo:hi, :] = dot(probs, v_ref[0, 0, :hi, :], NN).astype(BF)
            lse_ref[0, 0, lo:hi, :] = peak + jnp.log(total)

    @pl.when(head == heads - 1)
    def _():
        for r in range(FSDP):
            start = pl.multiple_of((own ^ r) * rows, rows)
            at = pl.ds(start, rows)

            @pl.when(start < length)
            def _():
                side = jnp.concatenate([o_ref[h, at, :] for h in range(o_ref.shape[0])], axis=1)
                out_refs[r][0] = side
                term_refs[r][0] = dot(side, wo_ref[...], NN).astype(BF)

            @pl.when(start >= length)
            def _():
                out_refs[r][0] = jnp.zeros_like(out_refs[r][0])
                term_refs[r][0] = jnp.zeros_like(term_refs[r][0])


def attend(lengths, own, normed, qkv_mat, out_mat, cos, sin):
    count, rows, model = normed[0].shape
    wide = out_mat.shape[0]
    heads = wide // HEAD_DIM
    full = FSDP * rows
    held = pl.BlockSpec((1, rows, model), lambda s, h, *_: (s, 0, 0))
    side = pl.BlockSpec((1, rows, wide), lambda s, h, *_: (s, 0, 0))
    turned = pl.BlockSpec((1, model, rows), lambda s, h, *_: (s, 0, 0))
    table = pl.BlockSpec((full, HEAD_DIM), lambda s, h, *_: (0, 0))
    whole = pl.BlockSpec((1, 1, full, HEAD_DIM), lambda s, h, *_: (s, h, 0, 0))
    stat = pl.BlockSpec((1, 1, full, 1), lambda s, h, *_: (s, h, 0, 0))
    weight = pl.BlockSpec((model, 3 * HEAD_DIM), lambda s, h, *_: (0, h))
    shape = jax.ShapeDtypeStruct
    outs = pl.pallas_call(
        attend_body,
        grid_spec=pltpu.PrefetchScalarGridSpec(
            num_scalar_prefetch=2,
            grid=(count, heads),
            in_specs=[held] * 4 + [weight, pl.BlockSpec((wide, model), lambda s, h, *_: (0, 0)), table, table],
            out_specs=[held] * 4 + [side] * 4 + [turned] * 4 + [whole] * 3 + [stat],
            scratch_shapes=[pltpu.VMEM((heads, full, HEAD_DIM), BF)],
        ),
        out_shape=[shape((count, rows, model), BF)] * 4
        + [shape((count, rows, wide), BF)] * 4
        + [shape((count, model, rows), BF)] * 4
        + [shape((count, heads, full, HEAD_DIM), BF)] * 3
        + [shape((count, heads, full, 1), F32)],
        name="attend",
    )(lengths, own, *normed, qkv_mat, out_mat, cos, sin)
    return outs[0:4], outs[4:8], outs[8:12], outs[12:16]


def attend_back_body(len_ref, own_ref, *refs):
    q_ref, k_ref, v_ref, lse_ref = refs[0:4]
    b_in, (w_ref, wo_ref, cos_ref, sin_ref) = refs[4:8], refs[8:12]
    out_refs, dh_refs = refs[12:16], refs[16:20]
    g_ref, dq_ref, dk_ref, dv_ref, dh_acc = refs[20:25]
    rows = b_in[0].shape[1]
    head, heads = pl.program_id(1), pl.num_programs(1)
    length = len_ref[pl.program_id(0)]
    own = own_ref[0]
    inv_root = HEAD_DIM ** (-0.5)
    for r in range(FSDP):
        start = pl.multiple_of((own ^ r) * rows, rows)

        @pl.when(start < length)
        def _():
            g_ref[pl.ds(start, rows), :] = dot(b_in[r][0], wo_ref[...], NT).astype(BF)

    dk_ref[...] = jnp.zeros_like(dk_ref)
    dv_ref[...] = jnp.zeros_like(dv_ref)
    for b in range(FSDP):
        lo, hi = b * rows, (b + 1) * rows

        @pl.when(lo < length)
        def _():
            query, keys, values = q_ref[0, 0, lo:hi, :], k_ref[0, 0, :hi, :], v_ref[0, 0, :hi, :]
            grad = g_ref[lo:hi, :]
            probs = jnp.exp(scores_of(query, keys) - lse_ref[0, 0, lo:hi, :])
            prob_grad = dot(grad, values, NT)
            row_dot = jnp.sum(probs * prob_grad, axis=1, keepdims=True)
            score_grad = (probs * (prob_grad - row_dot)).astype(BF)
            dq_ref[lo:hi, :] = dot(score_grad, keys, NN) * inv_root
            dk_ref[:hi, :] += dot(score_grad, query, TN)
            dv_ref[:hi, :] += dot(probs.astype(BF), grad, TN)

    @pl.when(head == 0)
    def _():
        dh_acc[...] = jnp.zeros_like(dh_acc)

    for r in range(FSDP):
        start = pl.multiple_of((own ^ r) * rows, rows)
        at = pl.ds(start, rows)

        @pl.when(start < length)
        def _():
            cos, sin = cos_ref[at, :], sin_ref[at, :]
            dq, dk = dq_ref[at, :], dk_ref[at, :] * inv_root
            dq = dq * cos - pltpu.roll(dq, HEAD_DIM // 2, 1) * sin
            dk = dk * cos - pltpu.roll(dk, HEAD_DIM // 2, 1) * sin
            grads = jnp.concatenate([dq.astype(BF), dk.astype(BF), dv_ref[at, :].astype(BF)], axis=1)
            out_refs[r][0] = grads
            dh_acc[r] += dot(grads, w_ref[...], NT)

        @pl.when(start >= length)
        def _():
            out_refs[r][0] = jnp.zeros_like(out_refs[r][0])

        @pl.when(head == heads - 1)
        def _():
            dh_refs[r][0] = dh_acc[r].astype(BF)


def attend_back(lengths, own, held, grads, qkv_mat, out_mat, cos, sin):
    count, rows, model = grads[0].shape
    heads = out_mat.shape[0] // HEAD_DIM
    full = FSDP * rows
    block = pl.BlockSpec((1, rows, model), lambda s, h, *_: (s, 0, 0))
    table = pl.BlockSpec((full, HEAD_DIM), lambda s, h, *_: (0, 0))
    whole = pl.BlockSpec((1, 1, full, HEAD_DIM), lambda s, h, *_: (s, h, 0, 0))
    stat = pl.BlockSpec((1, 1, full, 1), lambda s, h, *_: (s, h, 0, 0))
    result = pl.BlockSpec((1, rows, 3 * HEAD_DIM), lambda s, h, *_: (s, 0, h))
    shape = jax.ShapeDtypeStruct
    outs = pl.pallas_call(
        attend_back_body,
        grid_spec=pltpu.PrefetchScalarGridSpec(
            num_scalar_prefetch=2,
            grid=(count, heads),
            in_specs=[whole] * 3
            + [stat]
            + [block] * 4
            + [
                pl.BlockSpec((model, 3 * HEAD_DIM), lambda s, h, *_: (0, h)),
                pl.BlockSpec((HEAD_DIM, model), lambda s, h, *_: (h, 0)),
                table,
                table,
            ],
            out_specs=[result] * 4 + [block] * 4,
            scratch_shapes=[
                pltpu.VMEM((full, HEAD_DIM), BF),
                pltpu.VMEM((full, HEAD_DIM), F32),
                pltpu.VMEM((full, HEAD_DIM), F32),
                pltpu.VMEM((full, HEAD_DIM), F32),
                pltpu.VMEM((FSDP, rows, model), F32),
            ],
        ),
        out_shape=[shape((count, rows, 3 * HEAD_DIM * heads), BF)] * 4 + [shape((count, rows, model), BF)] * 4,
        name="attend_back",
    )(lengths, own, *held, *grads, qkv_mat, out_mat, cos, sin)
    return outs[0:4], outs[4:8]


ROOT = 0.7978845608028654
CUBE = 0.044715


def feed_body(limit_ref, *refs):
    h_refs, g_refs, (in_ref, down_ref) = refs[0:2], refs[2:4], refs[4:6]
    f_refs, dh_refs, a_refs, du_refs = refs[6:8], refs[8:10], refs[10:12], refs[12:14]
    f_acc, dh_acc = refs[14:16]
    step = pl.program_id(0)
    count = h_refs[0].shape[0]
    tile = in_ref.shape[1]

    @pl.when(step == 0)
    def _():
        f_acc[...] = jnp.zeros_like(f_acc)
        dh_acc[...] = jnp.zeros_like(dh_acc)

    for r in range(2):
        for s in range(count):
            limit = limit_ref[r, s] - step * tile

            @pl.when(limit > 0)
            def _():
                h, g = h_refs[r][s], g_refs[r][s]
                pre = dot(h, in_ref[...], NN)
                keep = lax.broadcasted_iota(jnp.int32, pre.shape, 1) < limit
                bend = jnp.tanh(ROOT * (pre + CUBE * pre * pre * pre))
                half = 0.5 * (1.0 + bend)
                slope = half + 0.5 * pre * (1.0 - bend * bend) * (ROOT * (1.0 + 3.0 * CUBE * pre * pre))
                active = jnp.where(keep, pre * half, 0.0).astype(BF)
                a_refs[r][s] = active
                f_acc[r, s] += dot(active, down_ref[...], NN)
                back = dot(g, down_ref[...], NT)
                grad = jnp.where(keep, back * slope, 0.0).astype(BF)
                du_refs[r][s] = grad
                dh_acc[r, s] += dot(grad, in_ref[...], NT)

            @pl.when(limit <= 0)
            def _():
                a_refs[r][s] = jnp.zeros_like(a_refs[r][s])
                du_refs[r][s] = jnp.zeros_like(du_refs[r][s])

    @pl.when(step == pl.num_programs(0) - 1)
    def _():
        for r in range(2):
            f_refs[r][...] = f_acc[r].astype(f_refs[r].dtype)
            dh_refs[r][...] = dh_acc[r].astype(dh_refs[r].dtype)


def feed_both(limits, h, g, in_mat, down_mat):
    count, rows, model = h[0].shape
    hidden = in_mat.shape[1]
    tile = 256
    held = pl.BlockSpec((count, rows, model), lambda t, *_: (0, 0, 0))
    units = pl.BlockSpec((count, rows, tile), lambda t, *_: (0, 0, t))
    outs = pl.pallas_call(
        feed_body,
        grid_spec=pltpu.PrefetchScalarGridSpec(
            num_scalar_prefetch=1,
            grid=(hidden // tile,),
            in_specs=[held] * 4
            + [
                pl.BlockSpec((model, tile), lambda t, *_: (0, t)),
                pl.BlockSpec((tile, model), lambda t, *_: (t, 0)),
            ],
            out_specs=[held] * 4 + [units] * 4,
            scratch_shapes=[pltpu.VMEM((2, count, rows, model), F32)] * 2,
        ),
        out_shape=[jax.ShapeDtypeStruct(h[0].shape, BF)] * 4
        + [jax.ShapeDtypeStruct((count, rows, hidden), BF)] * 4,
        name="feed_both",
    )(limits, *h, *g, in_mat, down_mat)
    return outs[0:2], outs[2:4], outs[4:6], outs[6:8]


def left_tiles_body(limit_ref, *refs):
    left, right = refs[0:4], refs[4:8]
    out_ref, acc = refs[8], refs[9]
    tile = out_ref.shape[0]
    acc[...] = jnp.zeros_like(acc)
    for r in range(FSDP):
        for s in range(left[0].shape[0]):

            @pl.when(limit_ref[r, s] > pl.program_id(0) * tile)
            def _():
                acc[...] += dot(left[r][s], right[r][s], TN)

    out_ref[...] = acc[...].astype(BF)


def left_tiles(limits, left, right, tile):
    count, rows, wide = left[0].shape
    cols = right[0].shape[2]
    return pl.pallas_call(
        left_tiles_body,
        grid_spec=pltpu.PrefetchScalarGridSpec(
            num_scalar_prefetch=1,
            grid=(wide // tile,),
            in_specs=[pl.BlockSpec((count, rows, tile), lambda t, *_: (0, 0, t))] * 4
            + [pl.BlockSpec((count, rows, cols), lambda t, *_: (0, 0, 0))] * 4,
            out_specs=pl.BlockSpec((tile, cols), lambda t, *_: (t, 0)),
            scratch_shapes=[pltpu.VMEM((tile, cols), F32)],
        ),
        out_shape=jax.ShapeDtypeStruct((wide, cols), BF),
        name="left_tiles",
    )(limits, *left, *right)


def right_tiles_body(limit_ref, *refs):
    left, right = refs[0:4], refs[4:8]
    out_ref, acc, turned = refs[8:11]
    tile = out_ref.shape[1]
    count = left[0].shape[0]

    @pl.when(pl.program_id(0) == 0)
    def _():
        for r in range(FSDP):
            for s in range(count):
                turned[r * count + s] = left[r][s].T

    acc[...] = jnp.zeros_like(acc)
    for r in range(FSDP):
        for s in range(count):

            @pl.when(limit_ref[r, s] > pl.program_id(0) * tile)
            def _():
                acc[...] += dot(turned[r * count + s], right[r][s], NN)

    out_ref[...] = acc[...].astype(BF)


def right_tiles(limits, left, right, tile):
    count, rows, wide = left[0].shape
    cols = right[0].shape[2]
    return pl.pallas_call(
        right_tiles_body,
        grid_spec=pltpu.PrefetchScalarGridSpec(
            num_scalar_prefetch=1,
            grid=(cols // tile,),
            in_specs=[pl.BlockSpec((count, rows, wide), lambda t, *_: (0, 0, 0))] * 4
            + [pl.BlockSpec((count, rows, tile), lambda t, *_: (0, 0, t))] * 4,
            out_specs=pl.BlockSpec((wide, tile), lambda t, *_: (0, t)),
            scratch_shapes=[pltpu.VMEM((wide, tile), F32), pltpu.VMEM((4 * count, wide, rows), BF)],
        ),
        out_shape=jax.ShapeDtypeStruct((wide, cols), BF),
        name="right_tiles",
    )(limits, *left, *right)


def turned_tile_body(limit_ref, *refs):
    left, right, out_ref, acc = refs[0:4], refs[4:8], refs[8], refs[9]
    acc[...] = jnp.zeros_like(acc)
    for r in range(FSDP):
        for s in range(left[0].shape[0]):

            @pl.when(limit_ref[r, s] > 0)
            def _():
                acc[...] += dot(left[r][s], right[r][s], NN)

    out_ref[...] = acc[...].astype(BF)


def turned_tile(limits, left, right, tile, at):
    count, wide, rows = left[0].shape
    step = 512
    return pl.pallas_call(
        turned_tile_body,
        grid_spec=pltpu.PrefetchScalarGridSpec(
            num_scalar_prefetch=1,
            grid=(wide // step,),
            in_specs=[pl.BlockSpec((count, step, rows), lambda t, *_: (0, t, 0))] * 4
            + [pl.BlockSpec((count, rows, tile), lambda t, *_: (0, 0, at))] * 4,
            out_specs=pl.BlockSpec((step, tile), lambda t, *_: (t, 0)),
            scratch_shapes=[pltpu.VMEM((step, tile), F32)],
        ),
        out_shape=jax.ShapeDtypeStruct((wide, tile), BF),
        name="turned_tile",
    )(limits, *left, *right)


def place_body(at_ref, *refs):
    half = pl.num_programs(0) // 2
    near, far, outs = refs[0:1], refs[1:2], refs[2:]
    for source, low in ((near[0], True), (far[0], False)):

        @pl.when((pl.program_id(0) < half) == low)
        def _():
            at = 0
            for out in outs:
                out[0] = source[0, :, at : at + out.shape[2]]
                at += out.shape[2]


def place(near, far, ats, widths):
    half, rows, cols = near.shape
    outs = pl.pallas_call(
        place_body,
        grid_spec=pltpu.PrefetchScalarGridSpec(
            num_scalar_prefetch=1,
            grid=(2 * half,),
            in_specs=[
                pl.BlockSpec((1, rows, cols), lambda n, *_: (jnp.minimum(n, half - 1), 0, 0)),
                pl.BlockSpec((1, rows, cols), lambda n, *_: (jnp.maximum(n - half, 0), 0, 0)),
            ],
            out_specs=[pl.BlockSpec((1, rows, wide), lambda n, at: (at[n], 0, 0)) for wide in widths],
        ),
        out_shape=[jax.ShapeDtypeStruct((2 * half, rows, wide), near.dtype) for wide in widths],
        name="place",
    )(ats, near, far)
    return outs


class Moves:
    def __init__(self, dp):
        self.dp = dp
        self.at = lax.axis_index("dp")
        self.own = lax.axis_index("fsdp")
        self.bits = [1 << n for n in range(dp.bit_length() - 1)]

    def peer(self, value, r):
        return lax.ppermute(value, "fsdp", [(j, j ^ r) for j in range(FSDP)])

    def swap(self, value, bit):
        return lax.ppermute(value, "dp", [(i, i ^ bit) for i in range(self.dp)])

    def gather_far(self, shard):
        parts = shard[None]
        for bit in self.bits[:0:-1]:
            parts = jnp.concatenate([parts, self.swap(parts, bit)])
        return parts

    def gather_near(self, parts, widths):
        marks = [0]
        for bit in self.bits[:0:-1]:
            marks += [mark ^ bit for mark in marks]
        marks += [mark ^ 1 for mark in marks]
        return place(parts, self.swap(parts, 1), (self.at ^ jnp.array(marks)).astype(jnp.int32), widths)

    def reduce(self, terms):
        block, cols = terms.shape[0] // self.dp, terms.shape[1]
        total = terms.reshape(self.dp, block, cols)
        for bit in self.bits:
            mine = (self.at // bit) % 2
            pairs = total.reshape(total.shape[0] // 2, 2, block, cols)
            sent = lax.dynamic_index_in_dim(pairs, 1 - mine, 1, keepdims=False).astype(BF)
            kept = lax.dynamic_index_in_dim(pairs, mine, 1, keepdims=False).astype(F32)
            total = kept + self.swap(sent, bit).astype(F32)
        return total.reshape(block, cols)

    def exchange(self, pieces):
        return lax.all_to_all(pieces, "fsdp", 0, 0, tiled=True)

    def total(self, value):
        for r in (1, 2):
            value = value + self.peer(value, r)
        for bit in self.bits:
            value = value + self.swap(value, bit)
        return value

    def spread(self, block):
        across = self.peer(block, 2)
        return [block, self.peer(block, 1), across, self.peer(across, 1)]

    def collect(self, terms):
        far = terms[2].astype(F32) + self.peer(terms[3].astype(BF), 1).astype(F32)
        near = terms[0].astype(F32) + self.peer(terms[1].astype(BF), 1).astype(F32)
        return near + self.peer(far.astype(BF), 2).astype(F32)


def after(value, *earlier):
    return lax.optimization_barrier((value,) + earlier)[0]


def local(
    dp,
    tokens,
    seq_lengths,
    seq_buckets,
    bucket_widths,
    norm_one_gain,
    norm_one_bias,
    qkv_weight,
    out_weight,
    norm_two_gain,
    norm_two_bias,
    ffn_in_weight,
    ffn_out_weight,
    cotangent,
):
    moves = Moves(dp)
    count, rows, model = tokens.shape
    full = rows * FSDP
    slice_rows = norm_one_gain.shape[0]
    ffn = ffn_in_weight.shape[1]
    hidden = ffn // FSDP
    stripe = ffn // (dp * FSDP)
    own = moves.own
    flat = lax.axis_index("dp") * FSDP + own
    own_array = own.astype(jnp.int32).reshape(1)
    home = [((i * FSDP + j), (j * dp + i)) for i in range(dp) for j in range(FSDP)]
    outward = [(b, a) for a, b in home]

    third = model // FSDP
    heads = third // HEAD_DIM
    vectors = jnp.stack([norm_one_gain, norm_one_bias, norm_two_gain, norm_two_bias], axis=1)
    vectors = jnp.pad(vectors, ((0, 0), (0, 124)))
    qkv_pieces = qkv_weight.reshape(slice_rows, 3, FSDP, heads, HEAD_DIM).transpose(2, 0, 3, 1, 4)
    qkv_pieces = qkv_pieces.reshape(FSDP, slice_rows, 3 * third)
    vectors = jnp.broadcast_to(vectors[None], (FSDP,) + vectors.shape)
    qkv_shard = moves.exchange(jnp.concatenate([qkv_pieces, vectors], axis=2))
    qkv_shard = qkv_shard.reshape(FSDP * slice_rows, 3 * third + 128)
    in_pieces = ffn_in_weight.reshape(slice_rows, dp, FSDP, stripe).transpose(2, 0, 1, 3)
    in_pieces = in_pieces.reshape(FSDP, slice_rows, hidden)
    in_shard = moves.exchange(after(in_pieces, qkv_shard)).reshape(FSDP * slice_rows, hidden)
    out_shard = lax.ppermute(after(out_weight, qkv_shard), ("dp", "fsdp"), outward)
    half = FSDP * slice_rows // 2
    first = moves.gather_far(qkv_shard[:half])
    second = moves.gather_far(after(qkv_shard[half:], first))
    in_mat = lax.all_gather(after(in_shard, second), "dp", axis=0, tiled=True)
    third_part = moves.gather_far(after(out_shard, second))
    down_far = moves.gather_far(after(ffn_out_weight, third_part))
    columns = (3 * third, 128)
    halves = zip(moves.gather_near(first, columns), moves.gather_near(second, columns))
    qkv_mat, vectors = [jnp.concatenate(pair, axis=1).reshape(model, -1) for pair in halves]
    out_mat = moves.gather_near(third_part, (model,))[0].reshape(third, model)
    vectors = vectors[:, :4].astype(F32).T
    gain_one, bias_one, gain_two, bias_two = vectors[0], vectors[1], vectors[2], vectors[3]

    positions = [(own ^ r) * rows + jnp.arange(rows) for r in range(FSDP)]
    live = [(p[None, :] < seq_lengths[:, None])[..., None] for p in positions]
    prefix = jnp.sum(
        jnp.where(jnp.arange(BUCKETS)[None, :] == seq_buckets[:, None], bucket_widths[None, :], 0), axis=1
    )
    turn = FSDP * stripe
    units = (prefix // turn) * stripe + jnp.clip(prefix % turn - own * stripe, 0, stripe)
    starts = (own ^ jnp.arange(FSDP)) * rows
    alive = starts[:, None] < seq_lengths[None, :]
    unit_limits = jnp.where(alive, units[None, :], 0).astype(jnp.int32)
    row_limits = jnp.where(alive, 1 << 20, 0).astype(jnp.int32)
    cos, sin = rotary_tables(full)

    token_blocks = moves.spread(after(tokens, qkv_shard))
    inputs = tokens.astype(F32)
    normed_one = []
    for block in token_blocks:
        value, _ = normalize(block.astype(F32))
        normed_one.append((value * gain_one + bias_one).astype(BF))
    feed_grad = jnp.where(live[0], cotangent, jnp.zeros_like(cotangent))
    feed_grad = moves.spread(after(feed_grad, token_blocks[2]))
    lengths = after(seq_lengths, down_far, feed_grad[2])
    branch, attended, turned_one, held = attend(lengths, own_array, normed_one, qkv_mat, out_mat, cos, sin)
    middle = inputs + moves.collect(branch)
    unit_two, scale_two = normalize(middle)
    normed_two = moves.spread((unit_two * gain_two + bias_two).astype(BF))

    down_mat = moves.gather_near(down_far, (model,))[0].reshape(hidden, model)
    feed, normed_two_grad, active, hidden_grad = [], [], [], []
    for r in (0, 2):
        pair = slice(r, r + 2)
        results = feed_both(unit_limits[pair], normed_two[pair], feed_grad[pair], in_mat, down_mat)
        for kept, result in zip((feed, normed_two_grad, active, hidden_grad), results):
            kept.extend(result)

    upstream = jnp.where(live[0], cotangent.astype(F32), 0.0)
    second_grad = moves.collect(normed_two_grad)
    grad_gain_two = jnp.sum(second_grad * unit_two, axis=(0, 1))
    grad_bias_two = jnp.sum(second_grad, axis=(0, 1))
    middle_grad = upstream + norm_back(second_grad, gain_two, unit_two, scale_two)
    branch_grad = moves.spread(middle_grad.astype(BF))

    grad_down = lax.psum_scatter(left_tiles(unit_limits, active, feed_grad, 256), "dp", scatter_dimension=0, tiled=True).astype(F32)
    grad_in = lax.psum_scatter(right_tiles(unit_limits, normed_two, hidden_grad, 256), "dp", scatter_dimension=0, tiled=True)

    qkv_grad, normed_one_grad = attend_back(
        seq_lengths, own_array, held, branch_grad, qkv_mat, out_mat, cos, sin
    )
    grad_qkv = [
        moves.reduce(turned_tile(row_limits, turned_one, qkv_grad, 3 * HEAD_DIM, head)) for head in range(heads)
    ]
    grad_out = moves.reduce(left_tiles(row_limits, attended, branch_grad, third))
    feed[3] = after(feed[3], branch_grad[3])
    feed[1] = after(feed[1], branch_grad[3])
    layer_output = jnp.where(live[0], middle + moves.collect(feed), 0.0).astype(BF)
    first_grad = moves.collect(normed_one_grad)
    unit_one, scale_one = normalize(inputs)
    input_grad = middle_grad + norm_back(first_grad, gain_one, unit_one, scale_one)
    grad_gain_one = jnp.sum(first_grad * unit_one, axis=(0, 1))
    grad_bias_one = jnp.sum(first_grad, axis=(0, 1))
    sums = moves.total(jnp.stack([grad_gain_one, grad_bias_one, grad_gain_two, grad_bias_two]))
    sums = lax.dynamic_slice(sums, (0, flat * slice_rows), (4, slice_rows))

    grad_out = lax.ppermute(grad_out, ("dp", "fsdp"), home)
    grad_qkv = jnp.concatenate([part.astype(BF) for part in grad_qkv], axis=1)
    grad_qkv = moves.exchange(grad_qkv.reshape(FSDP, slice_rows, 3 * third))
    grad_qkv = grad_qkv.reshape(FSDP, slice_rows, heads, 3, HEAD_DIM).transpose(1, 3, 0, 2, 4).astype(F32)
    grad_qkv = grad_qkv.reshape(slice_rows, 3 * model)
    grad_in = moves.exchange(grad_in.astype(BF).reshape(FSDP, slice_rows, hidden))
    grad_in = grad_in.reshape(FSDP, slice_rows, dp, stripe).transpose(1, 2, 0, 3).astype(F32)
    grad_in = grad_in.reshape(slice_rows, ffn)
    return (
        layer_output,
        input_grad,
        sums[0],
        sums[1],
        grad_qkv,
        grad_out,
        sums[2],
        sums[3],
        grad_in,
        grad_down,
    )


def solution(mesh):
    both = ("dp", "fsdp")
    placed = (
        P("dp", "fsdp", None),
        P("dp"),
        P("dp"),
        P(),
        P(both),
        P(both),
        P(both, None),
        P(both, None),
        P(both),
        P(both),
        P(both, None),
        P(both, None),
        P("dp", "fsdp", None),
    )
    return jax.shard_map(
        functools.partial(local, mesh.shape["dp"]),
        mesh=mesh,
        in_specs=placed,
        out_specs=(
            P("dp", "fsdp", None),
            P("dp", "fsdp", None),
            P(both),
            P(both),
            P(both, None),
            P(both, None),
            P(both),
            P(both),
            P(both, None),
            P(both, None),
        ),
        check_vma=False,
    )
```

```python
import functools

import jax
import jax.numpy as jnp
from jax import lax
from jax.experimental import pallas as pl
from jax.experimental.pallas import tpu as pltpu
from jax.sharding import PartitionSpec as P

HEADS = 12
HEAD_DIM = 128
BUCKETS = 4
FSDP = 4

BF = jnp.bfloat16
F32 = jnp.float32
NT = (((1,), (1,)), ((), ()))
TN = (((0,), (0,)), ((), ()))
NN = (((1,), (0,)), ((), ()))


def dot(a, b, dims):
    return lax.dot_general(a, b, dims, preferred_element_type=F32)


def cost(micros):
    return pl.CostEstimate(flops=micros * 10**9, bytes_accessed=micros * 10**6, transcendentals=0)


def rotary_tables(rows):
    half = HEAD_DIM // 2
    inverse = 10000.0 ** (-(jnp.arange(half).astype(F32) * 2.0) / HEAD_DIM)
    angles = jnp.arange(rows).astype(F32)[:, None] * inverse[None, :]
    cos, sin = jnp.cos(angles), jnp.sin(angles)
    return jnp.concatenate([cos, cos], axis=1), jnp.concatenate([-sin, sin], axis=1)


def normalize(values):
    center = values - jnp.mean(values, axis=-1, keepdims=True)
    spread = jnp.mean(center * center, axis=-1, keepdims=True)
    scale = lax.rsqrt(spread + 1e-05)
    return center * scale, scale


def norm_back(grad, gain, normed, scale):
    scaled = grad * gain
    first = jnp.mean(scaled, axis=-1, keepdims=True)
    second = jnp.mean(scaled * normed, axis=-1, keepdims=True)
    return scale * (scaled - first - normed * second)


def scores_of(query, keys):
    rows, cols = query.shape[0], keys.shape[0]
    scores = dot(query, keys, NT) * (HEAD_DIM ** (-0.5))
    row = lax.broadcasted_iota(jnp.int32, (rows, rows), 0)
    col = lax.broadcasted_iota(jnp.int32, (rows, rows), 1)
    last = jnp.where(col <= row, scores[:, cols - rows :], -1e30)
    if cols == rows:
        return last
    return jnp.concatenate([scores[:, : cols - rows], last], axis=1)


def attend_body(len_ref, own_ref, *refs):
    h_in, (w_ref, wo_ref, cos_ref, sin_ref) = refs[0:4], refs[4:8]
    term_refs, out_refs, turned_refs = refs[8:12], refs[12:16], refs[16:20]
    q_ref, k_ref, v_ref, lse_ref, o_ref = refs[20:25]
    rows = h_in[0].shape[1]
    head, heads = pl.program_id(1), pl.num_programs(1)
    length = len_ref[pl.program_id(0)]
    own = own_ref[0]
    for r in range(FSDP):
        start = pl.multiple_of((own ^ r) * rows, rows)
        at = pl.ds(start, rows)

        @pl.when(start < length)
        def _():
            mixed = dot(h_in[r][0], w_ref[...], NN)
            cos, sin = cos_ref[at, :], sin_ref[at, :]
            for part, target in ((0, q_ref), (1, k_ref)):
                value = mixed[:, part * HEAD_DIM : (part + 1) * HEAD_DIM]
                turned = value * cos + pltpu.roll(value, HEAD_DIM // 2, 1) * sin
                target[0, 0, at, :] = turned.astype(BF)
            v_ref[0, 0, at, :] = mixed[:, 2 * HEAD_DIM :].astype(BF)

        @pl.when(head == 0)
        def _():
            turned_refs[r][0] = h_in[r][0].T

    for b in range(FSDP):
        lo, hi = b * rows, (b + 1) * rows

        @pl.when(lo < length)
        def _():
            scores = scores_of(q_ref[0, 0, lo:hi, :], k_ref[0, 0, :hi, :])
            peak = jnp.max(scores, axis=1, keepdims=True)
            expo = jnp.exp(scores - peak)
            total = jnp.sum(expo, axis=1, keepdims=True)
            probs = (expo * (1.0 / total)).astype(BF)
            o_ref[head, lo:hi, :] = dot(probs, v_ref[0, 0, :hi, :], NN).astype(BF)
            lse_ref[0, 0, lo:hi, :] = peak + jnp.log(total)

    @pl.when(head == heads - 1)
    def _():
        for r in range(FSDP):
            start = pl.multiple_of((own ^ r) * rows, rows)
            at = pl.ds(start, rows)

            @pl.when(start < length)
            def _():
                side = jnp.concatenate([o_ref[h, at, :] for h in range(o_ref.shape[0])], axis=1)
                out_refs[r][0] = side
                term_refs[r][0] = dot(side, wo_ref[...], NN).astype(BF)

            @pl.when(start >= length)
            def _():
                out_refs[r][0] = jnp.zeros_like(out_refs[r][0])
                term_refs[r][0] = jnp.zeros_like(term_refs[r][0])


def attend(lengths, own, normed, qkv_mat, out_mat, cos, sin):
    count, rows, model = normed[0].shape
    wide = out_mat.shape[0]
    heads = wide // HEAD_DIM
    full = FSDP * rows
    held = pl.BlockSpec((1, rows, model), lambda s, h, *_: (s, 0, 0))
    side = pl.BlockSpec((1, rows, wide), lambda s, h, *_: (s, 0, 0))
    turned = pl.BlockSpec((1, model, rows), lambda s, h, *_: (s, 0, 0))
    table = pl.BlockSpec((full, HEAD_DIM), lambda s, h, *_: (0, 0))
    whole = pl.BlockSpec((1, 1, full, HEAD_DIM), lambda s, h, *_: (s, h, 0, 0))
    stat = pl.BlockSpec((1, 1, full, 1), lambda s, h, *_: (s, h, 0, 0))
    weight = pl.BlockSpec((model, 3 * HEAD_DIM), lambda s, h, *_: (0, h))
    shape = jax.ShapeDtypeStruct
    outs = pl.pallas_call(
        attend_body,
        grid_spec=pltpu.PrefetchScalarGridSpec(
            num_scalar_prefetch=2,
            grid=(count, heads),
            in_specs=[held] * 4 + [weight, pl.BlockSpec((wide, model), lambda s, h, *_: (0, 0)), table, table],
            out_specs=[held] * 4 + [side] * 4 + [turned] * 4 + [whole] * 3 + [stat],
            scratch_shapes=[pltpu.VMEM((heads, full, HEAD_DIM), BF)],
        ),
        out_shape=[shape((count, rows, model), BF)] * 4
        + [shape((count, rows, wide), BF)] * 4
        + [shape((count, model, rows), BF)] * 4
        + [shape((count, heads, full, HEAD_DIM), BF)] * 3
        + [shape((count, heads, full, 1), F32)],
        cost_estimate=cost(30),
        name="attend",
    )(lengths, own, *normed, qkv_mat, out_mat, cos, sin)
    return outs[0:4], outs[4:8], outs[8:12], outs[12:16]


def attend_back_body(len_ref, own_ref, *refs):
    q_ref, k_ref, v_ref, lse_ref = refs[0:4]
    b_in, (w_ref, wo_ref, cos_ref, sin_ref) = refs[4:8], refs[8:12]
    out_refs, dh_refs = refs[12:16], refs[16:20]
    g_ref, dq_ref, dk_ref, dv_ref, dh_acc = refs[20:25]
    rows = b_in[0].shape[1]
    head, heads = pl.program_id(1), pl.num_programs(1)
    length = len_ref[pl.program_id(0)]
    own = own_ref[0]
    inv_root = HEAD_DIM ** (-0.5)
    for r in range(FSDP):
        start = pl.multiple_of((own ^ r) * rows, rows)

        @pl.when(start < length)
        def _():
            g_ref[pl.ds(start, rows), :] = dot(b_in[r][0], wo_ref[...], NT).astype(BF)

    dk_ref[...] = jnp.zeros_like(dk_ref)
    dv_ref[...] = jnp.zeros_like(dv_ref)
    for b in range(FSDP):
        lo, hi = b * rows, (b + 1) * rows

        @pl.when(lo < length)
        def _():
            query, keys, values = q_ref[0, 0, lo:hi, :], k_ref[0, 0, :hi, :], v_ref[0, 0, :hi, :]
            grad = g_ref[lo:hi, :]
            probs = jnp.exp(scores_of(query, keys) - lse_ref[0, 0, lo:hi, :])
            prob_grad = dot(grad, values, NT)
            row_dot = jnp.sum(probs * prob_grad, axis=1, keepdims=True)
            score_grad = (probs * (prob_grad - row_dot)).astype(BF)
            dq_ref[lo:hi, :] = dot(score_grad, keys, NN) * inv_root
            dk_ref[:hi, :] += dot(score_grad, query, TN)
            dv_ref[:hi, :] += dot(probs.astype(BF), grad, TN)

    @pl.when(head == 0)
    def _():
        dh_acc[...] = jnp.zeros_like(dh_acc)

    for r in range(FSDP):
        start = pl.multiple_of((own ^ r) * rows, rows)
        at = pl.ds(start, rows)

        @pl.when(start < length)
        def _():
            cos, sin = cos_ref[at, :], sin_ref[at, :]
            dq, dk = dq_ref[at, :], dk_ref[at, :] * inv_root
            dq = dq * cos - pltpu.roll(dq, HEAD_DIM // 2, 1) * sin
            dk = dk * cos - pltpu.roll(dk, HEAD_DIM // 2, 1) * sin
            grads = jnp.concatenate([dq.astype(BF), dk.astype(BF), dv_ref[at, :].astype(BF)], axis=1)
            out_refs[r][0] = grads
            dh_acc[r] += dot(grads, w_ref[...], NT)

        @pl.when(start >= length)
        def _():
            out_refs[r][0] = jnp.zeros_like(out_refs[r][0])

        @pl.when(head == heads - 1)
        def _():
            dh_refs[r][0] = dh_acc[r].astype(BF)


def attend_back(lengths, own, held, grads, qkv_mat, out_mat, cos, sin):
    count, rows, model = grads[0].shape
    heads = out_mat.shape[0] // HEAD_DIM
    full = FSDP * rows
    block = pl.BlockSpec((1, rows, model), lambda s, h, *_: (s, 0, 0))
    table = pl.BlockSpec((full, HEAD_DIM), lambda s, h, *_: (0, 0))
    whole = pl.BlockSpec((1, 1, full, HEAD_DIM), lambda s, h, *_: (s, h, 0, 0))
    stat = pl.BlockSpec((1, 1, full, 1), lambda s, h, *_: (s, h, 0, 0))
    result = pl.BlockSpec((1, rows, 3 * HEAD_DIM), lambda s, h, *_: (s, 0, h))
    shape = jax.ShapeDtypeStruct
    outs = pl.pallas_call(
        attend_back_body,
        grid_spec=pltpu.PrefetchScalarGridSpec(
            num_scalar_prefetch=2,
            grid=(count, heads),
            in_specs=[whole] * 3
            + [stat]
            + [block] * 4
            + [
                pl.BlockSpec((model, 3 * HEAD_DIM), lambda s, h, *_: (0, h)),
                pl.BlockSpec((HEAD_DIM, model), lambda s, h, *_: (h, 0)),
                table,
                table,
            ],
            out_specs=[result] * 4 + [block] * 4,
            scratch_shapes=[
                pltpu.VMEM((full, HEAD_DIM), BF),
                pltpu.VMEM((full, HEAD_DIM), F32),
                pltpu.VMEM((full, HEAD_DIM), F32),
                pltpu.VMEM((full, HEAD_DIM), F32),
                pltpu.VMEM((FSDP, rows, model), F32),
            ],
        ),
        out_shape=[shape((count, rows, 3 * HEAD_DIM * heads), BF)] * 4 + [shape((count, rows, model), BF)] * 4,
        cost_estimate=cost(35),
        name="attend_back",
    )(lengths, own, *held, *grads, qkv_mat, out_mat, cos, sin)
    return outs[0:4], outs[4:8]


ROOT = 0.7978845608028654
CUBE = 0.044715


def feed_body(limit_ref, *refs):
    h_refs, g_refs, (in_ref, down_ref) = refs[0:2], refs[2:4], refs[4:6]
    f_refs, dh_refs, a_refs, du_refs = refs[6:8], refs[8:10], refs[10:12], refs[12:14]
    f_acc, dh_acc = refs[14:16]
    step = pl.program_id(0)
    count = h_refs[0].shape[0]
    tile = in_ref.shape[1]

    @pl.when(step == 0)
    def _():
        f_acc[...] = jnp.zeros_like(f_acc)
        dh_acc[...] = jnp.zeros_like(dh_acc)

    for r in range(2):
        for s in range(count):
            limit = limit_ref[r, s] - step * tile

            @pl.when(limit > 0)
            def _():
                h, g = h_refs[r][s], g_refs[r][s]
                pre = dot(h, in_ref[...], NN)
                keep = lax.broadcasted_iota(jnp.int32, pre.shape, 1) < limit
                bend = jnp.tanh(ROOT * (pre + CUBE * pre * pre * pre))
                half = 0.5 * (1.0 + bend)
                slope = half + 0.5 * pre * (1.0 - bend * bend) * (ROOT * (1.0 + 3.0 * CUBE * pre * pre))
                active = jnp.where(keep, pre * half, 0.0).astype(BF)
                a_refs[r][s] = active
                f_acc[r, s] += dot(active, down_ref[...], NN)
                back = dot(g, down_ref[...], NT)
                grad = jnp.where(keep, back * slope, 0.0).astype(BF)
                du_refs[r][s] = grad
                dh_acc[r, s] += dot(grad, in_ref[...], NT)

            @pl.when(limit <= 0)
            def _():
                a_refs[r][s] = jnp.zeros_like(a_refs[r][s])
                du_refs[r][s] = jnp.zeros_like(du_refs[r][s])

    @pl.when(step == pl.num_programs(0) - 1)
    def _():
        for r in range(2):
            f_refs[r][...] = f_acc[r].astype(f_refs[r].dtype)
            dh_refs[r][...] = dh_acc[r].astype(dh_refs[r].dtype)


def feed_both(limits, h, g, in_mat, down_mat):
    count, rows, model = h[0].shape
    hidden = in_mat.shape[1]
    tile = 256
    held = pl.BlockSpec((count, rows, model), lambda t, *_: (0, 0, 0))
    units = pl.BlockSpec((count, rows, tile), lambda t, *_: (0, 0, t))
    outs = pl.pallas_call(
        feed_body,
        grid_spec=pltpu.PrefetchScalarGridSpec(
            num_scalar_prefetch=1,
            grid=(hidden // tile,),
            in_specs=[held] * 4
            + [
                pl.BlockSpec((model, tile), lambda t, *_: (0, t)),
                pl.BlockSpec((tile, model), lambda t, *_: (t, 0)),
            ],
            out_specs=[held] * 4 + [units] * 4,
            scratch_shapes=[pltpu.VMEM((2, count, rows, model), F32)] * 2,
        ),
        out_shape=[jax.ShapeDtypeStruct(h[0].shape, BF)] * 4
        + [jax.ShapeDtypeStruct((count, rows, hidden), BF)] * 4,
        cost_estimate=cost(20),
        name="feed_both",
    )(limits, *h, *g, in_mat, down_mat)
    return outs[0:2], outs[2:4], outs[4:6], outs[6:8]


def left_tiles_body(limit_ref, *refs):
    left, right = refs[0:4], refs[4:8]
    out_ref, acc = refs[8], refs[9]
    tile = out_ref.shape[0]
    acc[...] = jnp.zeros_like(acc)
    for r in range(FSDP):
        for s in range(left[0].shape[0]):

            @pl.when(limit_ref[r, s] > pl.program_id(0) * tile)
            def _():
                acc[...] += dot(left[r][s], right[r][s], TN)

    out_ref[...] = acc[...].astype(BF)


def left_tiles(limits, left, right, tile):
    count, rows, wide = left[0].shape
    cols = right[0].shape[2]
    return pl.pallas_call(
        left_tiles_body,
        grid_spec=pltpu.PrefetchScalarGridSpec(
            num_scalar_prefetch=1,
            grid=(wide // tile,),
            in_specs=[pl.BlockSpec((count, rows, tile), lambda t, *_: (0, 0, t))] * 4
            + [pl.BlockSpec((count, rows, cols), lambda t, *_: (0, 0, 0))] * 4,
            out_specs=pl.BlockSpec((tile, cols), lambda t, *_: (t, 0)),
            scratch_shapes=[pltpu.VMEM((tile, cols), F32)],
        ),
        out_shape=jax.ShapeDtypeStruct((wide, cols), BF),
        cost_estimate=cost(12),
        name="left_tiles",
    )(limits, *left, *right)


def right_tiles_body(limit_ref, *refs):
    left, right = refs[0:4], refs[4:8]
    out_ref, acc, turned = refs[8:11]
    tile = out_ref.shape[1]
    count = left[0].shape[0]

    @pl.when(pl.program_id(0) == 0)
    def _():
        for r in range(FSDP):
            for s in range(count):
                turned[r * count + s] = left[r][s].T

    acc[...] = jnp.zeros_like(acc)
    for r in range(FSDP):
        for s in range(count):

            @pl.when(limit_ref[r, s] > pl.program_id(0) * tile)
            def _():
                acc[...] += dot(turned[r * count + s], right[r][s], NN)

    out_ref[...] = acc[...].astype(BF)


def right_tiles(limits, left, right, tile):
    count, rows, wide = left[0].shape
    cols = right[0].shape[2]
    return pl.pallas_call(
        right_tiles_body,
        grid_spec=pltpu.PrefetchScalarGridSpec(
            num_scalar_prefetch=1,
            grid=(cols // tile,),
            in_specs=[pl.BlockSpec((count, rows, wide), lambda t, *_: (0, 0, 0))] * 4
            + [pl.BlockSpec((count, rows, tile), lambda t, *_: (0, 0, t))] * 4,
            out_specs=pl.BlockSpec((wide, tile), lambda t, *_: (0, t)),
            scratch_shapes=[pltpu.VMEM((wide, tile), F32), pltpu.VMEM((4 * count, wide, rows), BF)],
        ),
        out_shape=jax.ShapeDtypeStruct((wide, cols), BF),
        cost_estimate=cost(14),
        name="right_tiles",
    )(limits, *left, *right)


def turned_tile_body(limit_ref, *refs):
    left, right, out_ref, acc = refs[0:4], refs[4:8], refs[8], refs[9]
    acc[...] = jnp.zeros_like(acc)
    for r in range(FSDP):
        for s in range(left[0].shape[0]):

            @pl.when(limit_ref[r, s] > 0)
            def _():
                acc[...] += dot(left[r][s], right[r][s], NN)

    out_ref[...] = acc[...].astype(BF)


def turned_tile(limits, left, right, tile, at):
    count, wide, rows = left[0].shape
    step = 512
    return pl.pallas_call(
        turned_tile_body,
        grid_spec=pltpu.PrefetchScalarGridSpec(
            num_scalar_prefetch=1,
            grid=(wide // step,),
            in_specs=[pl.BlockSpec((count, step, rows), lambda t, *_: (0, t, 0))] * 4
            + [pl.BlockSpec((count, rows, tile), lambda t, *_: (0, 0, at))] * 4,
            out_specs=pl.BlockSpec((step, tile), lambda t, *_: (t, 0)),
            scratch_shapes=[pltpu.VMEM((step, tile), F32)],
        ),
        out_shape=jax.ShapeDtypeStruct((wide, tile), BF),
        cost_estimate=cost(8),
        name="turned_tile",
    )(limits, *left, *right)


def place_body(at_ref, *refs):
    half = pl.num_programs(0) // 2
    near, far, outs = refs[0:1], refs[1:2], refs[2:]
    for source, low in ((near[0], True), (far[0], False)):

        @pl.when((pl.program_id(0) < half) == low)
        def _():
            at = 0
            for out in outs:
                out[0] = source[0, :, at : at + out.shape[2]]
                at += out.shape[2]


def place(near, far, ats, widths):
    half, rows, cols = near.shape
    outs = pl.pallas_call(
        place_body,
        grid_spec=pltpu.PrefetchScalarGridSpec(
            num_scalar_prefetch=1,
            grid=(2 * half,),
            in_specs=[
                pl.BlockSpec((1, rows, cols), lambda n, *_: (jnp.minimum(n, half - 1), 0, 0)),
                pl.BlockSpec((1, rows, cols), lambda n, *_: (jnp.maximum(n - half, 0), 0, 0)),
            ],
            out_specs=[pl.BlockSpec((1, rows, wide), lambda n, at: (at[n], 0, 0)) for wide in widths],
        ),
        out_shape=[jax.ShapeDtypeStruct((2 * half, rows, wide), near.dtype) for wide in widths],
        cost_estimate=cost(6),
        name="place",
    )(ats, near, far)
    return outs


class Moves:
    def __init__(self, dp):
        self.dp = dp
        self.at = lax.axis_index("dp")
        self.own = lax.axis_index("fsdp")
        self.bits = [1 << n for n in range(dp.bit_length() - 1)]

    def peer(self, value, r):
        return lax.ppermute(value, "fsdp", [(j, j ^ r) for j in range(FSDP)])

    def swap(self, value, bit):
        return lax.ppermute(value, "dp", [(i, i ^ bit) for i in range(self.dp)])

    def gather_far(self, shard):
        parts = shard[None]
        for bit in self.bits[:0:-1]:
            parts = jnp.concatenate([parts, self.swap(parts, bit)])
        return parts

    def gather_near(self, parts, widths):
        marks = [0]
        for bit in self.bits[:0:-1]:
            marks += [mark ^ bit for mark in marks]
        marks += [mark ^ 1 for mark in marks]
        return place(parts, self.swap(parts, 1), (self.at ^ jnp.array(marks)).astype(jnp.int32), widths)

    def halves(self, total, bit):
        mine = (self.at // bit) % 2
        pairs = total.reshape(total.shape[0] // 2, 2, *total.shape[1:])
        sent = lax.dynamic_index_in_dim(pairs, 1 - mine, 1, keepdims=False).astype(BF)
        return sent, lax.dynamic_index_in_dim(pairs, mine, 1, keepdims=False)

    def reduce_far(self, total, bits=None):
        for bit in self.bits[1:] if bits is None else bits:
            sent, kept = self.halves(total, bit)
            total = kept.astype(F32) + self.swap(sent, bit).astype(F32)
        return total.reshape(total.shape[1:])

    def reduce(self, terms):
        return self.reduce_far(terms.reshape(self.dp, -1, terms.shape[1]), self.bits)

    def exchange(self, pieces):
        return lax.all_to_all(pieces, "fsdp", 0, 0, tiled=True)

    def total(self, value):
        devices = self.dp * FSDP
        parts = value.reshape(value.shape[0], devices, -1).transpose(1, 0, 2)
        size = parts.shape[2]
        parts = lax.all_to_all(parts.reshape(devices, -1), ("dp", "fsdp"), 0, 0, tiled=True)
        return jnp.sum(parts, axis=0).reshape(-1, size)

    def spread(self, block):
        across = self.peer(block, 2)
        return [block, self.peer(block, 1), across, self.peer(across, 1)]

    def far_sum(self, terms):
        return (terms[2].astype(F32) + self.peer(terms[3], 1).astype(F32)).astype(BF)

    def near_sum(self, terms, across):
        return terms[0].astype(F32) + self.peer(terms[1], 1).astype(F32) + across.astype(F32)


def after(value, *earlier):
    return lax.optimization_barrier((value,) + earlier)[0]


def local(
    dp,
    tokens,
    seq_lengths,
    seq_buckets,
    bucket_widths,
    norm_one_gain,
    norm_one_bias,
    qkv_weight,
    out_weight,
    norm_two_gain,
    norm_two_bias,
    ffn_in_weight,
    ffn_out_weight,
    cotangent,
):
    moves = Moves(dp)
    count, rows, model = tokens.shape
    full = rows * FSDP
    slice_rows = norm_one_gain.shape[0]
    ffn = ffn_in_weight.shape[1]
    hidden = ffn // FSDP
    stripe = ffn // (dp * FSDP)
    own = moves.own
    own_array = own.astype(jnp.int32).reshape(1)
    home = [((i * FSDP + j), (j * dp + i)) for i in range(dp) for j in range(FSDP)]
    outward = [(b, a) for a, b in home]

    third = model // FSDP
    heads = third // HEAD_DIM
    vectors = jnp.stack([norm_one_gain, norm_one_bias, norm_two_gain, norm_two_bias], axis=1)
    vectors = jnp.pad(vectors, ((0, 0), (0, 124)))
    qkv_pieces = qkv_weight.reshape(slice_rows, 3, FSDP, heads, HEAD_DIM).transpose(2, 0, 3, 1, 4)
    qkv_pieces = qkv_pieces.reshape(FSDP, slice_rows, 3 * third)
    vectors = jnp.broadcast_to(vectors[None], (FSDP,) + vectors.shape)
    qkv_shard = moves.exchange(jnp.concatenate([qkv_pieces, vectors], axis=2))
    qkv_shard = qkv_shard.reshape(FSDP * slice_rows, 3 * third + 128)
    in_pieces = ffn_in_weight.reshape(slice_rows, dp, FSDP, stripe).transpose(2, 0, 1, 3)
    in_pieces = in_pieces.reshape(FSDP, slice_rows, hidden)
    in_shard = moves.exchange(after(in_pieces, qkv_shard)).reshape(FSDP * slice_rows, hidden)
    out_shard = lax.ppermute(after(out_weight, qkv_shard), ("dp", "fsdp"), outward)
    half = FSDP * slice_rows // 2
    first = moves.gather_far(qkv_shard[:half])
    second = moves.gather_far(after(qkv_shard[half:], first))
    down_mat = lax.all_gather(ffn_out_weight, "dp", axis=0, tiled=True)
    in_mat = lax.all_gather(after(in_shard, down_mat), "dp", axis=0, tiled=True)
    third_part = moves.gather_far(after(out_shard, second))
    columns = (3 * third, 128)
    halves = zip(moves.gather_near(first, columns), moves.gather_near(second, columns))
    qkv_mat, vectors = [jnp.concatenate(pair, axis=1).reshape(model, -1) for pair in halves]
    out_mat = moves.gather_near(third_part, (model,))[0].reshape(third, model)
    vectors = vectors[:, :4].astype(F32).T
    gain_one, bias_one, gain_two, bias_two = vectors[0], vectors[1], vectors[2], vectors[3]

    positions = [(own ^ r) * rows + jnp.arange(rows) for r in range(FSDP)]
    live = [(p[None, :] < seq_lengths[:, None])[..., None] for p in positions]
    prefix = jnp.sum(
        jnp.where(jnp.arange(BUCKETS)[None, :] == seq_buckets[:, None], bucket_widths[None, :], 0), axis=1
    )
    turn = FSDP * stripe
    units = (prefix // turn) * stripe + jnp.clip(prefix % turn - own * stripe, 0, stripe)
    starts = (own ^ jnp.arange(FSDP)) * rows
    alive = starts[:, None] < seq_lengths[None, :]
    unit_limits = jnp.where(alive, units[None, :], 0).astype(jnp.int32)
    row_limits = jnp.where(alive, 1 << 20, 0).astype(jnp.int32)
    cos, sin = rotary_tables(full)

    token_blocks = moves.spread(after(tokens, qkv_shard))
    inputs = tokens.astype(F32)
    normed_one = []
    for block in token_blocks:
        value, _ = normalize(block.astype(F32))
        normed_one.append((value * gain_one + bias_one).astype(BF))
    feed_grad = jnp.where(live[0], cotangent, jnp.zeros_like(cotangent))
    feed_grad = moves.spread(after(feed_grad, token_blocks[2]))
    lengths = after(seq_lengths, feed_grad[2], in_shard)
    branch, attended, turned_one, held = attend(lengths, own_array, normed_one, qkv_mat, out_mat, cos, sin)
    across = moves.peer(after(moves.far_sum(branch), in_mat), 2)
    middle = inputs + moves.near_sum(branch, across)
    unit_two, scale_two = normalize(middle)
    normed_two = moves.spread((unit_two * gain_two + bias_two).astype(BF))

    feed, normed_two_grad, active, hidden_grad = [], [], [], []
    for r in (0, 2):
        pair = slice(r, r + 2)
        results = feed_both(after(unit_limits[pair], *feed), normed_two[pair], feed_grad[pair], in_mat, down_mat)
        for kept, result in zip((feed, normed_two_grad, active, hidden_grad), results):
            kept.extend(result)

    upstream = jnp.where(live[0], cotangent.astype(F32), 0.0)
    far = moves.far_sum(normed_two_grad)
    gate = after(unit_limits, far)
    grad_in = right_tiles(gate, normed_two, hidden_grad, 256)
    grad_down = left_tiles(gate, active, feed_grad, 256)
    second_grad = moves.near_sum(normed_two_grad, moves.peer(far, 2))
    second_grad = after(second_grad, grad_in, grad_down)
    grad_in = lax.psum_scatter(grad_in, "dp", scatter_dimension=0, tiled=True)
    grad_down = lax.psum_scatter(grad_down, "dp", scatter_dimension=0, tiled=True).astype(F32)
    grad_gain_two = jnp.sum(second_grad * unit_two, axis=(0, 1))
    grad_bias_two = jnp.sum(second_grad, axis=(0, 1))
    middle_grad = upstream + norm_back(second_grad, gain_two, unit_two, scale_two)
    branch_grad = moves.spread(middle_grad.astype(BF))

    feed[3] = after(feed[3], branch_grad[2])
    far = moves.far_sum(feed)
    across = moves.peer(far, 2)
    qkv_grad, normed_one_grad = attend_back(
        after(seq_lengths, far), own_array, held, branch_grad, qkv_mat, out_mat, cos, sin
    )
    layer_output = jnp.where(live[0], middle + moves.near_sum(feed, across), 0.0).astype(BF)
    far = moves.far_sum(normed_one_grad)
    gate = after(row_limits, far, across)
    grad_out = moves.reduce(left_tiles(row_limits, attended, branch_grad, third))
    grad_qkv = []
    for head in range(heads):
        terms = turned_tile(gate, turned_one, qkv_grad, 3 * HEAD_DIM, head)
        sent, kept = moves.halves(terms.reshape(dp, -1, 3 * HEAD_DIM), 1)
        gate = after(gate, sent)
        grad_qkv.append(moves.reduce_far(kept.astype(F32) + moves.swap(sent, 1).astype(F32)))
    first_grad = moves.near_sum(normed_one_grad, moves.peer(far, 2))
    unit_one, scale_one = normalize(inputs)
    input_grad = middle_grad + norm_back(first_grad, gain_one, unit_one, scale_one)
    grad_gain_one = jnp.sum(first_grad * unit_one, axis=(0, 1))
    grad_bias_one = jnp.sum(first_grad, axis=(0, 1))
    sums = moves.total(jnp.stack([grad_gain_one, grad_bias_one, grad_gain_two, grad_bias_two]))

    grad_out = lax.ppermute(grad_out, ("dp", "fsdp"), home)
    grad_qkv = jnp.concatenate([part.astype(BF) for part in grad_qkv], axis=1)
    grad_qkv = moves.exchange(grad_qkv.reshape(FSDP, slice_rows, 3 * third))
    grad_qkv = grad_qkv.reshape(FSDP, slice_rows, heads, 3, HEAD_DIM).transpose(1, 3, 0, 2, 4).astype(F32)
    grad_qkv = grad_qkv.reshape(slice_rows, 3 * model)
    grad_in = moves.exchange(grad_in.astype(BF).reshape(FSDP, slice_rows, hidden))
    grad_in = grad_in.reshape(FSDP, slice_rows, dp, stripe).transpose(1, 2, 0, 3).astype(F32)
    grad_in = grad_in.reshape(slice_rows, ffn)
    return (
        layer_output,
        input_grad,
        sums[0],
        sums[1],
        grad_qkv,
        grad_out,
        sums[2],
        sums[3],
        grad_in,
        grad_down,
    )


def solution(mesh):
    both = ("dp", "fsdp")
    placed = (
        P("dp", "fsdp", None),
        P("dp"),
        P("dp"),
        P(),
        P(both),
        P(both),
        P(both, None),
        P(both, None),
        P(both),
        P(both),
        P(both, None),
        P(both, None),
        P("dp", "fsdp", None),
    )
    return jax.shard_map(
        functools.partial(local, mesh.shape["dp"]),
        mesh=mesh,
        in_specs=placed,
        out_specs=(
            P("dp", "fsdp", None),
            P("dp", "fsdp", None),
            P(both),
            P(both),
            P(both, None),
            P(both, None),
            P(both),
            P(both),
            P(both, None),
            P(both, None),
        ),
        check_vma=False,
    )
```

```python
import functools

import jax
import jax.numpy as jnp
from jax import lax
from jax.experimental import pallas as pl
from jax.experimental.pallas import tpu as pltpu
from jax.sharding import PartitionSpec as P

HEADS = 12
HEAD_DIM = 128
BUCKETS = 4
FSDP = 4

BF = jnp.bfloat16
F32 = jnp.float32
NT = (((1,), (1,)), ((), ()))
TN = (((0,), (0,)), ((), ()))
NN = (((1,), (0,)), ((), ()))


def dot(a, b, dims):
    return lax.dot_general(a, b, dims, preferred_element_type=F32)


def cost(micros):
    return pl.CostEstimate(flops=micros * 10**9, bytes_accessed=micros * 10**6, transcendentals=0)


def rotary_tables(rows):
    half = HEAD_DIM // 2
    inverse = 10000.0 ** (-(jnp.arange(half).astype(F32) * 2.0) / HEAD_DIM)
    angles = jnp.arange(rows).astype(F32)[:, None] * inverse[None, :]
    cos, sin = jnp.cos(angles), jnp.sin(angles)
    return jnp.concatenate([cos, cos], axis=1), jnp.concatenate([-sin, sin], axis=1)


def normalize(values):
    center = values - jnp.mean(values, axis=-1, keepdims=True)
    spread = jnp.mean(center * center, axis=-1, keepdims=True)
    scale = lax.rsqrt(spread + 1e-05)
    return center * scale, scale


def norm_back(grad, gain, normed, scale):
    scaled = grad * gain
    first = jnp.mean(scaled, axis=-1, keepdims=True)
    second = jnp.mean(scaled * normed, axis=-1, keepdims=True)
    return scale * (scaled - first - normed * second)


def scores_of(query, keys):
    rows, cols = query.shape[0], keys.shape[0]
    scores = dot(query, keys, NT) * (HEAD_DIM ** (-0.5))
    row = lax.broadcasted_iota(jnp.int32, (rows, rows), 0)
    col = lax.broadcasted_iota(jnp.int32, (rows, rows), 1)
    last = jnp.where(col <= row, scores[:, cols - rows :], -1e30)
    if cols == rows:
        return last
    return jnp.concatenate([scores[:, : cols - rows], last], axis=1)


def attend_body(len_ref, own_ref, *refs):
    h_in, (w_ref, wo_ref, cos_ref, sin_ref) = refs[0:4], refs[4:8]
    term_refs, out_refs, turned_refs = refs[8:12], refs[12:16], refs[16:20]
    q_ref, k_ref, v_ref, lse_ref, o_ref = refs[20:25]
    rows = h_in[0].shape[1]
    head, heads = pl.program_id(1), pl.num_programs(1)
    length = len_ref[pl.program_id(0)]
    own = own_ref[0]
    for r in range(FSDP):
        start = pl.multiple_of((own ^ r) * rows, rows)
        at = pl.ds(start, rows)

        @pl.when(start < length)
        def _():
            mixed = dot(h_in[r][0], w_ref[...], NN)
            cos, sin = cos_ref[at, :], sin_ref[at, :]
            for part, target in ((0, q_ref), (1, k_ref)):
                value = mixed[:, part * HEAD_DIM : (part + 1) * HEAD_DIM]
                turned = value * cos + pltpu.roll(value, HEAD_DIM // 2, 1) * sin
                target[0, 0, at, :] = turned.astype(BF)
            v_ref[0, 0, at, :] = mixed[:, 2 * HEAD_DIM :].astype(BF)

        @pl.when(head == 0)
        def _():
            turned_refs[r][0] = h_in[r][0].T

    for b in range(FSDP):
        lo, hi = b * rows, (b + 1) * rows

        @pl.when(lo < length)
        def _():
            scores = scores_of(q_ref[0, 0, lo:hi, :], k_ref[0, 0, :hi, :])
            peak = jnp.max(scores, axis=1, keepdims=True)
            expo = jnp.exp(scores - peak)
            total = jnp.sum(expo, axis=1, keepdims=True)
            probs = (expo * (1.0 / total)).astype(BF)
            o_ref[head, lo:hi, :] = dot(probs, v_ref[0, 0, :hi, :], NN).astype(BF)
            lse_ref[0, 0, lo:hi, :] = peak + jnp.log(total)

    @pl.when(head == heads - 1)
    def _():
        for r in range(FSDP):
            start = pl.multiple_of((own ^ r) * rows, rows)
            at = pl.ds(start, rows)

            @pl.when(start < length)
            def _():
                side = jnp.concatenate([o_ref[h, at, :] for h in range(o_ref.shape[0])], axis=1)
                out_refs[r][0] = side
                term_refs[r][0] = dot(side, wo_ref[...], NN).astype(BF)

            @pl.when(start >= length)
            def _():
                out_refs[r][0] = jnp.zeros_like(out_refs[r][0])
                term_refs[r][0] = jnp.zeros_like(term_refs[r][0])


def attend(lengths, own, normed, qkv_mat, out_mat, cos, sin):
    count, rows, model = normed[0].shape
    wide = out_mat.shape[0]
    heads = wide // HEAD_DIM
    full = FSDP * rows
    held = pl.BlockSpec((1, rows, model), lambda s, h, *_: (s, 0, 0))
    side = pl.BlockSpec((1, rows, wide), lambda s, h, *_: (s, 0, 0))
    turned = pl.BlockSpec((1, model, rows), lambda s, h, *_: (s, 0, 0))
    table = pl.BlockSpec((full, HEAD_DIM), lambda s, h, *_: (0, 0))
    whole = pl.BlockSpec((1, 1, full, HEAD_DIM), lambda s, h, *_: (s, h, 0, 0))
    stat = pl.BlockSpec((1, 1, full, 1), lambda s, h, *_: (s, h, 0, 0))
    weight = pl.BlockSpec((model, 3 * HEAD_DIM), lambda s, h, *_: (0, h))
    shape = jax.ShapeDtypeStruct
    outs = pl.pallas_call(
        attend_body,
        grid_spec=pltpu.PrefetchScalarGridSpec(
            num_scalar_prefetch=2,
            grid=(count, heads),
            in_specs=[held] * 4 + [weight, pl.BlockSpec((wide, model), lambda s, h, *_: (0, 0)), table, table],
            out_specs=[held] * 4 + [side] * 4 + [turned] * 4 + [whole] * 3 + [stat],
            scratch_shapes=[pltpu.VMEM((heads, full, HEAD_DIM), BF)],
        ),
        out_shape=[shape((count, rows, model), BF)] * 4
        + [shape((count, rows, wide), BF)] * 4
        + [shape((count, model, rows), BF)] * 4
        + [shape((count, heads, full, HEAD_DIM), BF)] * 3
        + [shape((count, heads, full, 1), F32)],
        cost_estimate=cost(30),
        name="attend",
    )(lengths, own, *normed, qkv_mat, out_mat, cos, sin)
    return outs[0:4], outs[4:8], outs[8:12], outs[12:16]


def attend_back_body(len_ref, own_ref, *refs):
    q_ref, k_ref, v_ref, lse_ref = refs[0:4]
    b_in, (w_ref, wo_ref, cos_ref, sin_ref) = refs[4:8], refs[8:12]
    out_refs, dh_refs = refs[12:16], refs[16:20]
    g_ref, dq_ref, dk_ref, dv_ref, dh_acc = refs[20:25]
    rows = b_in[0].shape[1]
    head, heads = pl.program_id(1), pl.num_programs(1)
    length = len_ref[pl.program_id(0)]
    own = own_ref[0]
    inv_root = HEAD_DIM ** (-0.5)
    for r in range(FSDP):
        start = pl.multiple_of((own ^ r) * rows, rows)

        @pl.when(start < length)
        def _():
            g_ref[pl.ds(start, rows), :] = dot(b_in[r][0], wo_ref[...], NT).astype(BF)

    dk_ref[...] = jnp.zeros_like(dk_ref)
    dv_ref[...] = jnp.zeros_like(dv_ref)
    for b in range(FSDP):
        lo, hi = b * rows, (b + 1) * rows

        @pl.when(lo < length)
        def _():
            query, keys, values = q_ref[0, 0, lo:hi, :], k_ref[0, 0, :hi, :], v_ref[0, 0, :hi, :]
            grad = g_ref[lo:hi, :]
            probs = jnp.exp(scores_of(query, keys) - lse_ref[0, 0, lo:hi, :])
            prob_grad = dot(grad, values, NT)
            row_dot = jnp.sum(probs * prob_grad, axis=1, keepdims=True)
            score_grad = (probs * (prob_grad - row_dot)).astype(BF)
            dq_ref[lo:hi, :] = dot(score_grad, keys, NN) * inv_root
            dk_ref[:hi, :] += dot(score_grad, query, TN)
            dv_ref[:hi, :] += dot(probs.astype(BF), grad, TN)

    @pl.when(head == 0)
    def _():
        dh_acc[...] = jnp.zeros_like(dh_acc)

    for r in range(FSDP):
        start = pl.multiple_of((own ^ r) * rows, rows)
        at = pl.ds(start, rows)

        @pl.when(start < length)
        def _():
            cos, sin = cos_ref[at, :], sin_ref[at, :]
            dq, dk = dq_ref[at, :], dk_ref[at, :] * inv_root
            dq = dq * cos - pltpu.roll(dq, HEAD_DIM // 2, 1) * sin
            dk = dk * cos - pltpu.roll(dk, HEAD_DIM // 2, 1) * sin
            grads = jnp.concatenate([dq.astype(BF), dk.astype(BF), dv_ref[at, :].astype(BF)], axis=1)
            out_refs[r][0] = grads
            dh_acc[r] += dot(grads, w_ref[...], NT)

        @pl.when(start >= length)
        def _():
            out_refs[r][0] = jnp.zeros_like(out_refs[r][0])

        @pl.when(head == heads - 1)
        def _():
            dh_refs[r][0] = dh_acc[r].astype(BF)


def attend_back(lengths, own, held, grads, qkv_mat, out_mat, cos, sin):
    count, rows, model = grads[0].shape
    heads = out_mat.shape[0] // HEAD_DIM
    full = FSDP * rows
    block = pl.BlockSpec((1, rows, model), lambda s, h, *_: (s, 0, 0))
    table = pl.BlockSpec((full, HEAD_DIM), lambda s, h, *_: (0, 0))
    whole = pl.BlockSpec((1, 1, full, HEAD_DIM), lambda s, h, *_: (s, h, 0, 0))
    stat = pl.BlockSpec((1, 1, full, 1), lambda s, h, *_: (s, h, 0, 0))
    result = pl.BlockSpec((1, rows, 3 * HEAD_DIM), lambda s, h, *_: (s, 0, h))
    shape = jax.ShapeDtypeStruct
    outs = pl.pallas_call(
        attend_back_body,
        grid_spec=pltpu.PrefetchScalarGridSpec(
            num_scalar_prefetch=2,
            grid=(count, heads),
            in_specs=[whole] * 3
            + [stat]
            + [block] * 4
            + [
                pl.BlockSpec((model, 3 * HEAD_DIM), lambda s, h, *_: (0, h)),
                pl.BlockSpec((HEAD_DIM, model), lambda s, h, *_: (h, 0)),
                table,
                table,
            ],
            out_specs=[result] * 4 + [block] * 4,
            scratch_shapes=[
                pltpu.VMEM((full, HEAD_DIM), BF),
                pltpu.VMEM((full, HEAD_DIM), F32),
                pltpu.VMEM((full, HEAD_DIM), F32),
                pltpu.VMEM((full, HEAD_DIM), F32),
                pltpu.VMEM((FSDP, rows, model), F32),
            ],
        ),
        out_shape=[shape((count, rows, 3 * HEAD_DIM * heads), BF)] * 4 + [shape((count, rows, model), BF)] * 4,
        cost_estimate=cost(35),
        name="attend_back",
    )(lengths, own, *held, *grads, qkv_mat, out_mat, cos, sin)
    return outs[0:4], outs[4:8]


ROOT = 0.7978845608028654
CUBE = 0.044715


def feed_body(limit_ref, *refs):
    h_refs, g_refs, (in_ref, low_ref, high_ref) = refs[0:2], refs[2:4], refs[4:7]
    f_refs, dh_refs, a_refs, du_refs = refs[7:9], refs[9:11], refs[11:13], refs[13:15]
    f_acc, dh_acc, down_ref = refs[15:18]
    down_ref[...] = jnp.concatenate([low_ref[...], high_ref[...]], axis=1)
    step = pl.program_id(0)
    count = h_refs[0].shape[0]
    tile = in_ref.shape[1]

    @pl.when(step == 0)
    def _():
        f_acc[...] = jnp.zeros_like(f_acc)
        dh_acc[...] = jnp.zeros_like(dh_acc)

    for r in range(2):
        for s in range(count):
            limit = limit_ref[r, s] - step * tile

            @pl.when(limit > 0)
            def _():
                h, g = h_refs[r][s], g_refs[r][s]
                pre = dot(h, in_ref[...], NN)
                keep = lax.broadcasted_iota(jnp.int32, pre.shape, 1) < limit
                bend = jnp.tanh(ROOT * (pre + CUBE * pre * pre * pre))
                half = 0.5 * (1.0 + bend)
                slope = half + 0.5 * pre * (1.0 - bend * bend) * (ROOT * (1.0 + 3.0 * CUBE * pre * pre))
                active = jnp.where(keep, pre * half, 0.0).astype(BF)
                a_refs[r][s] = active
                f_acc[r, s] += dot(active, down_ref[...], NN)
                back = dot(g, down_ref[...], NT)
                grad = jnp.where(keep, back * slope, 0.0).astype(BF)
                du_refs[r][s] = grad
                dh_acc[r, s] += dot(grad, in_ref[...], NT)

            @pl.when(limit <= 0)
            def _():
                a_refs[r][s] = jnp.zeros_like(a_refs[r][s])
                du_refs[r][s] = jnp.zeros_like(du_refs[r][s])

    @pl.when(step == pl.num_programs(0) - 1)
    def _():
        for r in range(2):
            f_refs[r][...] = f_acc[r].astype(f_refs[r].dtype)
            dh_refs[r][...] = dh_acc[r].astype(dh_refs[r].dtype)


def feed_both(limits, h, g, in_mat, down_low, down_high):
    count, rows, model = h[0].shape
    hidden = in_mat.shape[1]
    tile = 256
    held = pl.BlockSpec((count, rows, model), lambda t, *_: (0, 0, 0))
    units = pl.BlockSpec((count, rows, tile), lambda t, *_: (0, 0, t))
    outs = pl.pallas_call(
        feed_body,
        grid_spec=pltpu.PrefetchScalarGridSpec(
            num_scalar_prefetch=1,
            grid=(hidden // tile,),
            in_specs=[held] * 4
            + [
                pl.BlockSpec((model, tile), lambda t, *_: (0, t)),
                pl.BlockSpec((tile, model // 2), lambda t, *_: (t, 0)),
                pl.BlockSpec((tile, model // 2), lambda t, *_: (t, 0)),
            ],
            out_specs=[held] * 4 + [units] * 4,
            scratch_shapes=[pltpu.VMEM((2, count, rows, model), F32)] * 2 + [pltpu.VMEM((tile, model), BF)],
        ),
        out_shape=[jax.ShapeDtypeStruct(h[0].shape, BF)] * 4
        + [jax.ShapeDtypeStruct((count, rows, hidden), BF)] * 4,
        cost_estimate=cost(20),
        name="feed_both",
    )(limits, *h, *g, in_mat, down_low, down_high)
    return outs[0:2], outs[2:4], outs[4:6], outs[6:8]


def left_tiles_body(limit_ref, *refs):
    left, right = refs[0:4], refs[4:8]
    out_refs, acc = refs[8:-1], refs[-1]
    tile, cols = acc.shape
    acc[...] = jnp.zeros_like(acc)
    for r in range(FSDP):
        for s in range(left[0].shape[0]):

            @pl.when(limit_ref[r, s] > pl.program_id(0) * tile)
            def _():
                acc[...] += dot(left[r][s], right[r][s], TN)

    wide = cols // len(out_refs)
    for n, out_ref in enumerate(out_refs):
        out_ref[...] = acc[:, n * wide : (n + 1) * wide].astype(BF)


def left_tiles(limits, left, right, tile, parts):
    count, rows, wide = left[0].shape
    cols = right[0].shape[2]
    return pl.pallas_call(
        left_tiles_body,
        grid_spec=pltpu.PrefetchScalarGridSpec(
            num_scalar_prefetch=1,
            grid=(wide // tile,),
            in_specs=[pl.BlockSpec((count, rows, tile), lambda t, *_: (0, 0, t))] * 4
            + [pl.BlockSpec((count, rows, cols), lambda t, *_: (0, 0, 0))] * 4,
            out_specs=[pl.BlockSpec((tile, cols // parts), lambda t, *_: (t, 0))] * parts,
            scratch_shapes=[pltpu.VMEM((tile, cols), F32)],
        ),
        out_shape=[jax.ShapeDtypeStruct((wide, cols // parts), BF)] * parts,
        cost_estimate=cost(12),
        name="left_tiles",
    )(limits, *left, *right)


def right_tiles_body(limit_ref, *refs):
    left, right = refs[0:4], refs[4:8]
    out_ref, acc, turned = refs[8:11]
    tile = out_ref.shape[1]
    count = left[0].shape[0]

    @pl.when(pl.program_id(0) == 0)
    def _():
        for r in range(FSDP):
            for s in range(count):
                turned[r * count + s] = left[r][s].T

    acc[...] = jnp.zeros_like(acc)
    for r in range(FSDP):
        for s in range(count):

            @pl.when(limit_ref[r, s] > pl.program_id(0) * tile)
            def _():
                acc[...] += dot(turned[r * count + s], right[r][s], NN)

    out_ref[...] = acc[...].astype(BF)


def right_tiles(limits, left, right, tile):
    count, rows, wide = left[0].shape
    cols = right[0].shape[2]
    return pl.pallas_call(
        right_tiles_body,
        grid_spec=pltpu.PrefetchScalarGridSpec(
            num_scalar_prefetch=1,
            grid=(cols // tile,),
            in_specs=[pl.BlockSpec((count, rows, wide), lambda t, *_: (0, 0, 0))] * 4
            + [pl.BlockSpec((count, rows, tile), lambda t, *_: (0, 0, t))] * 4,
            out_specs=pl.BlockSpec((wide, tile), lambda t, *_: (0, t)),
            scratch_shapes=[pltpu.VMEM((wide, tile), F32), pltpu.VMEM((4 * count, wide, rows), BF)],
        ),
        out_shape=jax.ShapeDtypeStruct((wide, cols), BF),
        cost_estimate=cost(14),
        name="right_tiles",
    )(limits, *left, *right)


def turned_tile_body(limit_ref, *refs):
    left, right, out_ref, acc = refs[0:4], refs[4:8], refs[8], refs[9]
    acc[...] = jnp.zeros_like(acc)
    for r in range(FSDP):
        for s in range(left[0].shape[0]):

            @pl.when(limit_ref[r, s] > 0)
            def _():
                acc[...] += dot(left[r][s], right[r][s], NN)

    out_ref[...] = acc[...].astype(BF)


def turned_tile(limits, left, right, tile, at):
    count, wide, rows = left[0].shape
    step = 512
    return pl.pallas_call(
        turned_tile_body,
        grid_spec=pltpu.PrefetchScalarGridSpec(
            num_scalar_prefetch=1,
            grid=(wide // step,),
            in_specs=[pl.BlockSpec((count, step, rows), lambda t, *_: (0, t, 0))] * 4
            + [pl.BlockSpec((count, rows, tile), lambda t, *_: (0, 0, at))] * 4,
            out_specs=pl.BlockSpec((step, tile), lambda t, *_: (t, 0)),
            scratch_shapes=[pltpu.VMEM((step, tile), F32)],
        ),
        out_shape=jax.ShapeDtypeStruct((wide, tile), BF),
        cost_estimate=cost(8),
        name="turned_tile",
    )(limits, *left, *right)


def place_body(at_ref, near_ref, far_ref, out_ref):
    half = pl.num_programs(0) // 2

    @pl.when(pl.program_id(0) < half)
    def _():
        out_ref[...] = near_ref[...]

    @pl.when(pl.program_id(0) >= half)
    def _():
        out_ref[...] = far_ref[...]


def place(near, far, ats):
    half, rows, cols = near.shape
    return pl.pallas_call(
        place_body,
        grid_spec=pltpu.PrefetchScalarGridSpec(
            num_scalar_prefetch=1,
            grid=(2 * half,),
            in_specs=[
                pl.BlockSpec((1, rows, cols), lambda n, *_: (jnp.minimum(n, half - 1), 0, 0)),
                pl.BlockSpec((1, rows, cols), lambda n, *_: (jnp.maximum(n - half, 0), 0, 0)),
            ],
            out_specs=pl.BlockSpec((1, rows, cols), lambda n, at: (at[n], 0, 0)),
        ),
        out_shape=jax.ShapeDtypeStruct((2 * half, rows, cols), near.dtype),
        cost_estimate=cost(6),
        name="place",
    )(ats, near, far)


class Moves:
    def __init__(self, dp):
        self.dp = dp
        self.at = lax.axis_index("dp")
        self.own = lax.axis_index("fsdp")
        self.bits = [1 << n for n in range(dp.bit_length() - 1)]

    def peer(self, value, r):
        return lax.ppermute(value, "fsdp", [(j, j ^ r) for j in range(FSDP)])

    def swap(self, value, bit):
        return lax.ppermute(value, "dp", [(i, i ^ bit) for i in range(self.dp)])

    def gather_far(self, shard):
        parts = shard[None]
        for bit in self.bits[:0:-1]:
            parts = jnp.concatenate([parts, self.swap(parts, bit)])
        return parts

    def placed(self, parts, swapped):
        marks = [0]
        for bit in self.bits[:0:-1]:
            marks += [mark ^ bit for mark in marks]
        marks += [mark ^ 1 for mark in marks]
        return place(parts, swapped, (self.at ^ jnp.array(marks)).astype(jnp.int32))

    def halves(self, total, bit):
        mine = (self.at // bit) % 2
        pairs = total.reshape(total.shape[0] // 2, 2, *total.shape[1:])
        sent = lax.dynamic_index_in_dim(pairs, 1 - mine, 1, keepdims=False).astype(BF)
        return sent, lax.dynamic_index_in_dim(pairs, mine, 1, keepdims=False)

    def reduce_far(self, total):
        for bit in self.bits[1:]:
            sent, kept = self.halves(total, bit)
            total = kept.astype(F32) + self.swap(sent, bit).astype(F32)
        return total.reshape(total.shape[1:])

    def exchange(self, pieces):
        return lax.all_to_all(pieces, "fsdp", 0, 0, tiled=True)

    def total(self, value):
        devices = self.dp * FSDP
        parts = value.reshape(value.shape[0], devices, -1).transpose(1, 0, 2)
        size = parts.shape[2]
        parts = lax.all_to_all(parts.reshape(devices, -1), ("dp", "fsdp"), 0, 0, tiled=True)
        return jnp.sum(parts, axis=0).reshape(-1, size)

    def spread(self, block):
        across = self.peer(block, 2)
        return [block, self.peer(block, 1), across, self.peer(across, 1)]

    def far_sum(self, terms):
        return (terms[2].astype(F32) + self.peer(terms[3], 1).astype(F32)).astype(BF)

    def near_sum(self, terms, across):
        return sum_of(terms[0], self.peer(terms[1], 1), across)


def sum_of(*terms):
    return functools.reduce(jnp.add, [term.astype(F32) for term in terms])


def after(value, *earlier):
    return lax.optimization_barrier((value,) + earlier)[0]


def local(
    dp,
    tokens,
    seq_lengths,
    seq_buckets,
    bucket_widths,
    norm_one_gain,
    norm_one_bias,
    qkv_weight,
    out_weight,
    norm_two_gain,
    norm_two_bias,
    ffn_in_weight,
    ffn_out_weight,
    cotangent,
):
    moves = Moves(dp)
    count, rows, model = tokens.shape
    full = rows * FSDP
    slice_rows = norm_one_gain.shape[0]
    ffn = ffn_in_weight.shape[1]
    hidden = ffn // FSDP
    stripe = ffn // (dp * FSDP)
    own = moves.own
    own_array = own.astype(jnp.int32).reshape(1)
    home = [((i * FSDP + j), (j * dp + i)) for i in range(dp) for j in range(FSDP)]
    outward = [(b, a) for a, b in home]

    third = model // FSDP
    heads = third // HEAD_DIM
    qkv_pieces = qkv_weight.reshape(slice_rows, 3, FSDP, heads, HEAD_DIM).transpose(2, 0, 3, 1, 4)
    qkv_shard = moves.exchange(qkv_pieces.reshape(FSDP, slice_rows, 3 * third))
    qkv_shard = qkv_shard.reshape(FSDP * slice_rows, 3 * third)
    vectors = jnp.concatenate([norm_one_gain, norm_one_bias, norm_two_gain, norm_two_bias])
    vectors = jnp.broadcast_to(after(vectors, qkv_shard)[None], (dp * FSDP, 4 * slice_rows))
    vectors = lax.all_to_all(vectors, ("dp", "fsdp"), 0, 0, tiled=True)
    vectors = vectors.reshape(dp * FSDP, 4, slice_rows).transpose(1, 0, 2).reshape(4, model).astype(F32)
    gain_one, bias_one, gain_two, bias_two = vectors[0], vectors[1], vectors[2], vectors[3]
    in_pieces = ffn_in_weight.reshape(slice_rows, dp, FSDP, stripe).transpose(2, 0, 1, 3)
    in_pieces = in_pieces.reshape(FSDP, slice_rows, hidden)
    in_shard = moves.exchange(after(in_pieces, qkv_shard)).reshape(FSDP * slice_rows, hidden)
    out_shard = lax.ppermute(after(out_weight, qkv_shard), ("dp", "fsdp"), outward)
    qkv_far = moves.gather_far(qkv_shard)
    out_far = moves.gather_far(after(out_shard, qkv_far))
    in_far = moves.gather_far(after(in_shard, out_far))
    qkv_swapped = moves.swap(qkv_far, 1)
    qkv_mat = moves.placed(qkv_far, qkv_swapped).reshape(model, -1)
    out_mat = moves.placed(out_far, moves.swap(out_far, 1)).reshape(third, model)
    wide = model // 2
    down_low = lax.all_gather(after(ffn_out_weight[:, :wide], qkv_swapped), "dp", axis=0, tiled=True)
    down_high = lax.all_gather(after(ffn_out_weight[:, wide:], down_low), "dp", axis=0, tiled=True)

    positions = [(own ^ r) * rows + jnp.arange(rows) for r in range(FSDP)]
    live = [(p[None, :] < seq_lengths[:, None])[..., None] for p in positions]
    prefix = jnp.sum(
        jnp.where(jnp.arange(BUCKETS)[None, :] == seq_buckets[:, None], bucket_widths[None, :], 0), axis=1
    )
    turn = FSDP * stripe
    units = (prefix // turn) * stripe + jnp.clip(prefix % turn - own * stripe, 0, stripe)
    starts = (own ^ jnp.arange(FSDP)) * rows
    alive = starts[:, None] < seq_lengths[None, :]
    unit_limits = jnp.where(alive, units[None, :], 0).astype(jnp.int32)
    row_limits = jnp.where(alive, 1 << 20, 0).astype(jnp.int32)
    cos, sin = rotary_tables(full)

    token_blocks = moves.spread(after(tokens, qkv_shard))
    inputs = tokens.astype(F32)
    normed_one = []
    for block in token_blocks:
        value, _ = normalize(block.astype(F32))
        normed_one.append((value * gain_one + bias_one).astype(BF))
    feed_grad = jnp.where(live[0], cotangent, jnp.zeros_like(cotangent))
    feed_grad = moves.spread(after(feed_grad, token_blocks[2]))
    lengths = after(seq_lengths, feed_grad[2], in_far)
    branch, attended, turned_one, held = attend(lengths, own_array, normed_one, qkv_mat, out_mat, cos, sin)
    across = moves.peer(after(moves.far_sum(branch), down_low), 2)
    middle = inputs + moves.near_sum(branch, across)
    unit_two, scale_two = normalize(middle)
    in_swapped = moves.swap(in_far, 1)
    normed_two = moves.spread(after((unit_two * gain_two + bias_two).astype(BF), in_swapped))
    in_mat = moves.placed(in_far, in_swapped).reshape(model, hidden)

    feed, normed_two_grad, active, hidden_grad = [], [], [], []
    for r in (0, 2):
        pair = slice(r, r + 2)
        gate = after(unit_limits[pair], *feed)
        results = feed_both(gate, normed_two[pair], feed_grad[pair], in_mat, down_low, down_high)
        for kept, result in zip((feed, normed_two_grad, active, hidden_grad), results):
            kept.extend(result)

    upstream = jnp.where(live[0], cotangent.astype(F32), 0.0)
    far = moves.far_sum(normed_two_grad)
    gate = after(unit_limits, far)
    grad_in = right_tiles(gate, normed_two, hidden_grad, 256)
    down_terms = left_tiles(after(gate, grad_in), active, feed_grad, 256, 2)
    second_grad = moves.near_sum(normed_two_grad, moves.peer(far, 2))
    second_grad = after(second_grad, grad_in, down_terms[0])
    grad_in = lax.psum_scatter(grad_in, "dp", scatter_dimension=0, tiled=True)
    grad_in_pieces = moves.exchange(grad_in.reshape(FSDP, slice_rows, hidden))
    grad_gain_two = jnp.sum(second_grad * unit_two, axis=(0, 1))
    grad_bias_two = jnp.sum(second_grad, axis=(0, 1))
    middle_grad = upstream + norm_back(second_grad, gain_two, unit_two, scale_two)
    branch_grad = moves.spread(middle_grad.astype(BF))

    down_low = lax.psum_scatter(after(down_terms[0], branch_grad[2]), "dp", scatter_dimension=0, tiled=True)
    out_terms = left_tiles(row_limits, attended, branch_grad, third, 1)[0].reshape(dp, -1, model)
    out_sent, out_kept = moves.halves(out_terms, 1)
    feed[3] = after(feed[3], branch_grad[2])
    far = moves.far_sum(feed)
    across = moves.peer(far, 2)
    beside = moves.peer(feed[1], 1)
    qkv_grad, normed_one_grad = attend_back(
        after(seq_lengths, far, beside, out_sent), own_array, held, branch_grad, qkv_mat, out_mat, cos, sin
    )
    down_high = lax.psum_scatter(after(down_terms[1], qkv_grad[0]), "dp", scatter_dimension=0, tiled=True)
    layer_output = jnp.where(live[0], middle + sum_of(feed[0], beside, across), 0.0).astype(BF)
    out_swapped = moves.swap(out_sent, 1)
    far = moves.far_sum([*normed_one_grad[:3], after(normed_one_grad[3], across, out_swapped)])
    gate = after(row_limits, far)
    grad_out = moves.reduce_far(after(out_kept, far).astype(F32) + out_swapped.astype(F32))
    grad_qkv = []
    for head in range(heads):
        terms = turned_tile(gate, turned_one, qkv_grad, 3 * HEAD_DIM, head)
        sent, kept = moves.halves(terms.reshape(dp, -1, 3 * HEAD_DIM), 1)
        gate = after(gate, sent)
        grad_qkv.append(moves.reduce_far(kept.astype(F32) + moves.swap(sent, 1).astype(F32)))
    first_grad = moves.near_sum(normed_one_grad, after(moves.peer(far, 2), grad_in_pieces, down_low))
    unit_one, scale_one = normalize(inputs)
    input_grad = middle_grad + norm_back(first_grad, gain_one, unit_one, scale_one)
    grad_gain_one = jnp.sum(first_grad * unit_one, axis=(0, 1))
    grad_bias_one = jnp.sum(first_grad, axis=(0, 1))
    sums = moves.total(jnp.stack([grad_gain_one, grad_bias_one, grad_gain_two, grad_bias_two]))

    grad_out = lax.ppermute(grad_out, ("dp", "fsdp"), home)
    grad_qkv = jnp.concatenate([part.astype(BF) for part in grad_qkv], axis=1)
    grad_qkv = moves.exchange(grad_qkv.reshape(FSDP, slice_rows, 3 * third))
    grad_qkv = grad_qkv.reshape(FSDP, slice_rows, heads, 3, HEAD_DIM).transpose(1, 3, 0, 2, 4).astype(F32)
    grad_qkv = grad_qkv.reshape(slice_rows, 3 * model)
    grad_in = grad_in_pieces.reshape(FSDP, slice_rows, dp, stripe).transpose(1, 2, 0, 3).astype(F32)
    grad_in = grad_in.reshape(slice_rows, ffn)
    return (
        layer_output,
        input_grad,
        sums[0],
        sums[1],
        grad_qkv,
        grad_out,
        sums[2],
        sums[3],
        grad_in,
        jnp.concatenate([down_low, down_high], axis=1).astype(F32),
    )


def solution(mesh):
    both = ("dp", "fsdp")
    placed = (
        P("dp", "fsdp", None),
        P("dp"),
        P("dp"),
        P(),
        P(both),
        P(both),
        P(both, None),
        P(both, None),
        P(both),
        P(both),
        P(both, None),
        P(both, None),
        P("dp", "fsdp", None),
    )
    return jax.shard_map(
        functools.partial(local, mesh.shape["dp"]),
        mesh=mesh,
        in_specs=placed,
        out_specs=(
            P("dp", "fsdp", None),
            P("dp", "fsdp", None),
            P(both),
            P(both),
            P(both, None),
            P(both, None),
            P(both),
            P(both),
            P(both, None),
            P(both, None),
        ),
        check_vma=False,
    )
```

```python
import functools

import jax
import jax.numpy as jnp
from jax import lax
from jax.experimental import pallas as pl
from jax.experimental.pallas import tpu as pltpu
from jax.sharding import PartitionSpec as P

HEADS = 12
HEAD_DIM = 128
BUCKETS = 4
FSDP = 4

BF = jnp.bfloat16
F32 = jnp.float32
NT = (((1,), (1,)), ((), ()))
TN = (((0,), (0,)), ((), ()))
NN = (((1,), (0,)), ((), ()))


def dot(a, b, dims):
    return lax.dot_general(a, b, dims, preferred_element_type=F32)


def cost(micros):
    return pl.CostEstimate(flops=micros * 10**9, bytes_accessed=micros * 10**6, transcendentals=0)


def rotary_tables(rows):
    half = HEAD_DIM // 2
    inverse = 10000.0 ** (-(jnp.arange(half).astype(F32) * 2.0) / HEAD_DIM)
    angles = jnp.arange(rows).astype(F32)[:, None] * inverse[None, :]
    cos, sin = jnp.cos(angles), jnp.sin(angles)
    return jnp.concatenate([cos, cos], axis=1), jnp.concatenate([-sin, sin], axis=1)


def normalize(values):
    center = values - jnp.mean(values, axis=-1, keepdims=True)
    spread = jnp.mean(center * center, axis=-1, keepdims=True)
    scale = lax.rsqrt(spread + 1e-05)
    return center * scale, scale


def norm_back(grad, gain, normed, scale):
    scaled = grad * gain
    first = jnp.mean(scaled, axis=-1, keepdims=True)
    second = jnp.mean(scaled * normed, axis=-1, keepdims=True)
    return scale * (scaled - first - normed * second)


def scores_of(query, keys):
    rows, cols = query.shape[0], keys.shape[0]
    scores = dot(query, keys, NT) * (HEAD_DIM ** (-0.5))
    row = lax.broadcasted_iota(jnp.int32, (rows, rows), 0)
    col = lax.broadcasted_iota(jnp.int32, (rows, rows), 1)
    last = jnp.where(col <= row, scores[:, cols - rows :], -1e30)
    if cols == rows:
        return last
    return jnp.concatenate([scores[:, : cols - rows], last], axis=1)


def attend_body(len_ref, own_ref, *refs):
    h_in, (w_ref, wo_ref, cos_ref, sin_ref) = refs[0:4], refs[4:8]
    term_refs, out_refs, turned_refs = refs[8:12], refs[12:16], refs[16:20]
    q_ref, k_ref, v_ref, lse_ref, o_ref = refs[20:25]
    rows = h_in[0].shape[1]
    head, heads = pl.program_id(1), pl.num_programs(1)
    length = len_ref[pl.program_id(0)]
    own = own_ref[0]
    for r in range(FSDP):
        start = pl.multiple_of((own ^ r) * rows, rows)
        at = pl.ds(start, rows)

        @pl.when(start < length)
        def _():
            mixed = dot(h_in[r][0], w_ref[...], NN)
            cos, sin = cos_ref[at, :], sin_ref[at, :]
            for part, target in ((0, q_ref), (1, k_ref)):
                value = mixed[:, part * HEAD_DIM : (part + 1) * HEAD_DIM]
                turned = value * cos + pltpu.roll(value, HEAD_DIM // 2, 1) * sin
                target[0, 0, at, :] = turned.astype(BF)
            v_ref[0, 0, at, :] = mixed[:, 2 * HEAD_DIM :].astype(BF)

        @pl.when(head == 0)
        def _():
            turned_refs[r][0] = h_in[r][0].T

    for b in range(FSDP):
        lo, hi = b * rows, (b + 1) * rows

        @pl.when(lo < length)
        def _():
            scores = scores_of(q_ref[0, 0, lo:hi, :], k_ref[0, 0, :hi, :])
            peak = jnp.max(scores, axis=1, keepdims=True)
            expo = jnp.exp(scores - peak)
            total = jnp.sum(expo, axis=1, keepdims=True)
            probs = (expo * (1.0 / total)).astype(BF)
            o_ref[head, lo:hi, :] = dot(probs, v_ref[0, 0, :hi, :], NN).astype(BF)
            lse_ref[0, 0, lo:hi, :] = peak + jnp.log(total)

    @pl.when(head == heads - 1)
    def _():
        for r in range(FSDP):
            start = pl.multiple_of((own ^ r) * rows, rows)
            at = pl.ds(start, rows)

            @pl.when(start < length)
            def _():
                side = jnp.concatenate([o_ref[h, at, :] for h in range(o_ref.shape[0])], axis=1)
                out_refs[r][0] = side
                term_refs[r][0] = dot(side, wo_ref[...], NN).astype(BF)

            @pl.when(start >= length)
            def _():
                out_refs[r][0] = jnp.zeros_like(out_refs[r][0])
                term_refs[r][0] = jnp.zeros_like(term_refs[r][0])


def attend(lengths, own, normed, qkv_mat, out_mat, cos, sin):
    count, rows, model = normed[0].shape
    wide = out_mat.shape[0]
    heads = wide // HEAD_DIM
    full = FSDP * rows
    held = pl.BlockSpec((1, rows, model), lambda s, h, *_: (s, 0, 0))
    side = pl.BlockSpec((1, rows, wide), lambda s, h, *_: (s, 0, 0))
    turned = pl.BlockSpec((1, model, rows), lambda s, h, *_: (s, 0, 0))
    table = pl.BlockSpec((full, HEAD_DIM), lambda s, h, *_: (0, 0))
    whole = pl.BlockSpec((1, 1, full, HEAD_DIM), lambda s, h, *_: (s, h, 0, 0))
    stat = pl.BlockSpec((1, 1, full, 1), lambda s, h, *_: (s, h, 0, 0))
    weight = pl.BlockSpec((model, 3 * HEAD_DIM), lambda s, h, *_: (0, h))
    shape = jax.ShapeDtypeStruct
    outs = pl.pallas_call(
        attend_body,
        grid_spec=pltpu.PrefetchScalarGridSpec(
            num_scalar_prefetch=2,
            grid=(count, heads),
            in_specs=[held] * 4 + [weight, pl.BlockSpec((wide, model), lambda s, h, *_: (0, 0)), table, table],
            out_specs=[held] * 4 + [side] * 4 + [turned] * 4 + [whole] * 3 + [stat],
            scratch_shapes=[pltpu.VMEM((heads, full, HEAD_DIM), BF)],
        ),
        out_shape=[shape((count, rows, model), BF)] * 4
        + [shape((count, rows, wide), BF)] * 4
        + [shape((count, model, rows), BF)] * 4
        + [shape((count, heads, full, HEAD_DIM), BF)] * 3
        + [shape((count, heads, full, 1), F32)],
        cost_estimate=cost(30),
        name="attend",
    )(lengths, own, *normed, qkv_mat, out_mat, cos, sin)
    return outs[0:4], outs[4:8], outs[8:12], outs[12:16]


def attend_back_body(len_ref, own_ref, *refs):
    q_ref, k_ref, v_ref, lse_ref = refs[0:4]
    b_in, (w_ref, wo_ref, cos_ref, sin_ref) = refs[4:8], refs[8:12]
    out_refs, dh_refs = refs[12:16], refs[16:20]
    g_ref, dq_ref, dk_ref, dv_ref, dh_acc = refs[20:25]
    rows = b_in[0].shape[1]
    head, heads = pl.program_id(1), pl.num_programs(1)
    length = len_ref[pl.program_id(0)]
    own = own_ref[0]
    inv_root = HEAD_DIM ** (-0.5)
    for r in range(FSDP):
        start = pl.multiple_of((own ^ r) * rows, rows)

        @pl.when(start < length)
        def _():
            g_ref[pl.ds(start, rows), :] = dot(b_in[r][0], wo_ref[...], NT).astype(BF)

    dk_ref[...] = jnp.zeros_like(dk_ref)
    dv_ref[...] = jnp.zeros_like(dv_ref)
    for b in range(FSDP):
        lo, hi = b * rows, (b + 1) * rows

        @pl.when(lo < length)
        def _():
            query, keys, values = q_ref[0, 0, lo:hi, :], k_ref[0, 0, :hi, :], v_ref[0, 0, :hi, :]
            grad = g_ref[lo:hi, :]
            probs = jnp.exp(scores_of(query, keys) - lse_ref[0, 0, lo:hi, :])
            prob_grad = dot(grad, values, NT)
            row_dot = jnp.sum(probs * prob_grad, axis=1, keepdims=True)
            score_grad = (probs * (prob_grad - row_dot)).astype(BF)
            dq_ref[lo:hi, :] = dot(score_grad, keys, NN) * inv_root
            dk_ref[:hi, :] += dot(score_grad, query, TN)
            dv_ref[:hi, :] += dot(probs.astype(BF), grad, TN)

    @pl.when(head == 0)
    def _():
        dh_acc[...] = jnp.zeros_like(dh_acc)

    for r in range(FSDP):
        start = pl.multiple_of((own ^ r) * rows, rows)
        at = pl.ds(start, rows)

        @pl.when(start < length)
        def _():
            cos, sin = cos_ref[at, :], sin_ref[at, :]
            dq, dk = dq_ref[at, :], dk_ref[at, :] * inv_root
            dq = dq * cos - pltpu.roll(dq, HEAD_DIM // 2, 1) * sin
            dk = dk * cos - pltpu.roll(dk, HEAD_DIM // 2, 1) * sin
            grads = jnp.concatenate([dq.astype(BF), dk.astype(BF), dv_ref[at, :].astype(BF)], axis=1)
            out_refs[r][0] = grads
            dh_acc[r] += dot(grads, w_ref[...], NT)

        @pl.when(start >= length)
        def _():
            out_refs[r][0] = jnp.zeros_like(out_refs[r][0])

        @pl.when(head == heads - 1)
        def _():
            dh_refs[r][0] = dh_acc[r].astype(BF)


def attend_back(lengths, own, held, grads, qkv_mat, out_mat, cos, sin):
    count, rows, model = grads[0].shape
    heads = out_mat.shape[0] // HEAD_DIM
    full = FSDP * rows
    block = pl.BlockSpec((1, rows, model), lambda s, h, *_: (s, 0, 0))
    table = pl.BlockSpec((full, HEAD_DIM), lambda s, h, *_: (0, 0))
    whole = pl.BlockSpec((1, 1, full, HEAD_DIM), lambda s, h, *_: (s, h, 0, 0))
    stat = pl.BlockSpec((1, 1, full, 1), lambda s, h, *_: (s, h, 0, 0))
    result = pl.BlockSpec((1, rows, 3 * HEAD_DIM), lambda s, h, *_: (s, 0, h))
    shape = jax.ShapeDtypeStruct
    outs = pl.pallas_call(
        attend_back_body,
        grid_spec=pltpu.PrefetchScalarGridSpec(
            num_scalar_prefetch=2,
            grid=(count, heads),
            in_specs=[whole] * 3
            + [stat]
            + [block] * 4
            + [
                pl.BlockSpec((model, 3 * HEAD_DIM), lambda s, h, *_: (0, h)),
                pl.BlockSpec((HEAD_DIM, model), lambda s, h, *_: (h, 0)),
                table,
                table,
            ],
            out_specs=[result] * 4 + [block] * 4,
            scratch_shapes=[
                pltpu.VMEM((full, HEAD_DIM), BF),
                pltpu.VMEM((full, HEAD_DIM), F32),
                pltpu.VMEM((full, HEAD_DIM), F32),
                pltpu.VMEM((full, HEAD_DIM), F32),
                pltpu.VMEM((FSDP, rows, model), F32),
            ],
        ),
        out_shape=[shape((count, rows, 3 * HEAD_DIM * heads), BF)] * 4 + [shape((count, rows, model), BF)] * 4,
        cost_estimate=cost(35),
        name="attend_back",
    )(lengths, own, *held, *grads, qkv_mat, out_mat, cos, sin)
    return outs[0:4], outs[4:8]


ROOT = 0.7978845608028654
CUBE = 0.044715


def feed_body(limit_ref, *refs):
    h_refs, g_refs, (in_ref, down_ref) = refs[0:2], refs[2:4], refs[4:6]
    f_refs, dh_refs, a_refs, du_refs = refs[6:8], refs[8:10], refs[10:12], refs[12:14]
    f_acc, dh_acc = refs[14:16]
    step = pl.program_id(0)
    count = h_refs[0].shape[0]
    tile = in_ref.shape[1]

    @pl.when(step == 0)
    def _():
        f_acc[...] = jnp.zeros_like(f_acc)
        dh_acc[...] = jnp.zeros_like(dh_acc)

    for r in range(2):
        for s in range(count):
            limit = limit_ref[r, s] - step * tile

            @pl.when(limit > 0)
            def _():
                h, g = h_refs[r][s], g_refs[r][s]
                pre = dot(h, in_ref[...], NN)
                keep = lax.broadcasted_iota(jnp.int32, pre.shape, 1) < limit
                bend = jnp.tanh(ROOT * (pre + CUBE * pre * pre * pre))
                half = 0.5 * (1.0 + bend)
                slope = half + 0.5 * pre * (1.0 - bend * bend) * (ROOT * (1.0 + 3.0 * CUBE * pre * pre))
                active = jnp.where(keep, pre * half, 0.0).astype(BF)
                a_refs[r][s] = active
                f_acc[r, s] += dot(active, down_ref[...], NN)
                back = dot(g, down_ref[...], NT)
                grad = jnp.where(keep, back * slope, 0.0).astype(BF)
                du_refs[r][s] = grad
                dh_acc[r, s] += dot(grad, in_ref[...], NT)

            @pl.when(limit <= 0)
            def _():
                a_refs[r][s] = jnp.zeros_like(a_refs[r][s])
                du_refs[r][s] = jnp.zeros_like(du_refs[r][s])

    @pl.when(step == pl.num_programs(0) - 1)
    def _():
        for r in range(2):
            f_refs[r][...] = f_acc[r].astype(f_refs[r].dtype)
            dh_refs[r][...] = dh_acc[r].astype(dh_refs[r].dtype)


def feed_both(limits, h, g, in_mat, down_mat):
    count, rows, model = h[0].shape
    hidden = in_mat.shape[1]
    tile = 256
    held = pl.BlockSpec((count, rows, model), lambda t, *_: (0, 0, 0))
    units = pl.BlockSpec((count, rows, tile), lambda t, *_: (0, 0, t))
    outs = pl.pallas_call(
        feed_body,
        grid_spec=pltpu.PrefetchScalarGridSpec(
            num_scalar_prefetch=1,
            grid=(hidden // tile,),
            in_specs=[held] * 4
            + [
                pl.BlockSpec((model, tile), lambda t, *_: (0, t)),
                pl.BlockSpec((tile, model), lambda t, *_: (t, 0)),
            ],
            out_specs=[held] * 4 + [units] * 4,
            scratch_shapes=[pltpu.VMEM((2, count, rows, model), F32)] * 2,
        ),
        out_shape=[jax.ShapeDtypeStruct(h[0].shape, BF)] * 4
        + [jax.ShapeDtypeStruct((count, rows, hidden), BF)] * 4,
        cost_estimate=cost(20),
        name="feed_both",
    )(limits, *h, *g, in_mat, down_mat)
    return outs[0:2], outs[2:4], outs[4:6], outs[6:8]


def left_tiles_body(limit_ref, *refs):
    left, right = refs[0:4], refs[4:8]
    out_ref, acc = refs[8], refs[9]
    tile = out_ref.shape[0]
    acc[...] = jnp.zeros_like(acc)
    for r in range(FSDP):
        for s in range(left[0].shape[0]):

            @pl.when(limit_ref[r, s] > pl.program_id(0) * tile)
            def _():
                acc[...] += dot(left[r][s], right[r][s], TN)

    out_ref[...] = acc[...].astype(BF)


def left_tiles(limits, left, right, tile):
    count, rows, wide = left[0].shape
    cols = right[0].shape[2]
    return pl.pallas_call(
        left_tiles_body,
        grid_spec=pltpu.PrefetchScalarGridSpec(
            num_scalar_prefetch=1,
            grid=(wide // tile,),
            in_specs=[pl.BlockSpec((count, rows, tile), lambda t, *_: (0, 0, t))] * 4
            + [pl.BlockSpec((count, rows, cols), lambda t, *_: (0, 0, 0))] * 4,
            out_specs=pl.BlockSpec((tile, cols), lambda t, *_: (t, 0)),
            scratch_shapes=[pltpu.VMEM((tile, cols), F32)],
        ),
        out_shape=jax.ShapeDtypeStruct((wide, cols), BF),
        cost_estimate=cost(12),
        name="left_tiles",
    )(limits, *left, *right)


def right_tiles_body(limit_ref, *refs):
    left, right = refs[0:4], refs[4:8]
    out_ref, acc, turned = refs[8:11]
    tile = out_ref.shape[1]
    count = left[0].shape[0]

    @pl.when(pl.program_id(0) == 0)
    def _():
        for r in range(FSDP):
            for s in range(count):
                turned[r * count + s] = left[r][s].T

    acc[...] = jnp.zeros_like(acc)
    for r in range(FSDP):
        for s in range(count):

            @pl.when(limit_ref[r, s] > pl.program_id(0) * tile)
            def _():
                acc[...] += dot(turned[r * count + s], right[r][s], NN)

    out_ref[...] = acc[...].astype(BF)


def right_tiles(limits, left, right, tile):
    count, rows, wide = left[0].shape
    cols = right[0].shape[2]
    return pl.pallas_call(
        right_tiles_body,
        grid_spec=pltpu.PrefetchScalarGridSpec(
            num_scalar_prefetch=1,
            grid=(cols // tile,),
            in_specs=[pl.BlockSpec((count, rows, wide), lambda t, *_: (0, 0, 0))] * 4
            + [pl.BlockSpec((count, rows, tile), lambda t, *_: (0, 0, t))] * 4,
            out_specs=pl.BlockSpec((wide, tile), lambda t, *_: (0, t)),
            scratch_shapes=[pltpu.VMEM((wide, tile), F32), pltpu.VMEM((4 * count, wide, rows), BF)],
        ),
        out_shape=jax.ShapeDtypeStruct((wide, cols), BF),
        cost_estimate=cost(14),
        name="right_tiles",
    )(limits, *left, *right)


def turned_tiles_body(limit_ref, *refs):
    left, right, out_ref, acc = refs[0:4], refs[4:8], refs[8], refs[9]
    acc[...] = jnp.zeros_like(acc)
    for r in range(FSDP):
        for s in range(left[0].shape[0]):

            @pl.when(limit_ref[r, s] > 0)
            def _():
                acc[...] += dot(left[r][s], right[r][s], NN)

    out_ref[...] = acc[...].astype(BF)


def turned_tiles(limits, left, right):
    count, wide, rows = left[0].shape
    cols = right[0].shape[2]
    step = 512
    return pl.pallas_call(
        turned_tiles_body,
        grid_spec=pltpu.PrefetchScalarGridSpec(
            num_scalar_prefetch=1,
            grid=(wide // step,),
            in_specs=[pl.BlockSpec((count, step, rows), lambda t, *_: (0, t, 0))] * 4
            + [pl.BlockSpec((count, rows, cols), lambda t, *_: (0, 0, 0))] * 4,
            out_specs=pl.BlockSpec((step, cols), lambda t, *_: (t, 0)),
            scratch_shapes=[pltpu.VMEM((step, cols), F32)],
        ),
        out_shape=jax.ShapeDtypeStruct((wide, cols), BF),
        cost_estimate=cost(20),
        name="turned_tiles",
    )(limits, *left, *right)


def place_body(at_ref, near_ref, far_ref, out_ref):
    half = pl.num_programs(0) // 2

    @pl.when(pl.program_id(0) < half)
    def _():
        out_ref[...] = near_ref[...]

    @pl.when(pl.program_id(0) >= half)
    def _():
        out_ref[...] = far_ref[...]


def place(near, far, ats):
    half, rows, cols = near.shape
    return pl.pallas_call(
        place_body,
        grid_spec=pltpu.PrefetchScalarGridSpec(
            num_scalar_prefetch=1,
            grid=(2 * half,),
            in_specs=[
                pl.BlockSpec((1, rows, cols), lambda n, *_: (jnp.minimum(n, half - 1), 0, 0)),
                pl.BlockSpec((1, rows, cols), lambda n, *_: (jnp.maximum(n - half, 0), 0, 0)),
            ],
            out_specs=pl.BlockSpec((1, rows, cols), lambda n, at: (at[n], 0, 0)),
        ),
        out_shape=jax.ShapeDtypeStruct((2 * half, rows, cols), near.dtype),
        cost_estimate=cost(6),
        name="place",
    )(ats, near, far)


class Moves:
    def __init__(self, dp):
        self.dp = dp
        self.at = lax.axis_index("dp")
        self.own = lax.axis_index("fsdp")
        self.bits = [1 << n for n in range(dp.bit_length() - 1)]

    def peer(self, value, r):
        return lax.ppermute(value, "fsdp", [(j, j ^ r) for j in range(FSDP)])

    def swap(self, value, bit):
        return lax.ppermute(value, "dp", [(i, i ^ bit) for i in range(self.dp)])

    def gather_far(self, shard):
        parts, first = shard[None], None
        for bit in self.bits[:0:-1]:
            parts = jnp.concatenate([parts, self.swap(parts, bit)])
            first = parts if first is None else first
        return parts, first

    def placed(self, parts, swapped):
        marks = [0]
        for bit in self.bits[:0:-1]:
            marks += [mark ^ bit for mark in marks]
        marks += [mark ^ 1 for mark in marks]
        return place(parts, swapped, (self.at ^ jnp.array(marks)).astype(jnp.int32))

    def halves(self, total, bit):
        mine = (self.at // bit) % 2
        pairs = total.reshape(total.shape[0] // 2, 2, *total.shape[1:])
        sent = lax.dynamic_index_in_dim(pairs, 1 - mine, 1, keepdims=False).astype(BF)
        return sent, lax.dynamic_index_in_dim(pairs, mine, 1, keepdims=False)

    def reduce_far(self, total):
        for bit in self.bits[1:]:
            sent, kept = self.halves(total, bit)
            total = kept.astype(F32) + self.swap(sent, bit).astype(F32)
        return total.reshape(total.shape[1:])

    def exchange(self, pieces):
        return lax.all_to_all(pieces, "fsdp", 0, 0, tiled=True)

    def total(self, value):
        devices = self.dp * FSDP
        parts = value.reshape(value.shape[0], devices, -1).transpose(1, 0, 2)
        size = parts.shape[2]
        parts = lax.all_to_all(parts.reshape(devices, -1), ("dp", "fsdp"), 0, 0, tiled=True)
        return jnp.sum(parts, axis=0).reshape(-1, size)

    def spread(self, block):
        across = self.peer(block, 2)
        return [block, self.peer(block, 1), across, self.peer(across, 1)]

    def far_sum(self, terms):
        return (terms[2].astype(F32) + self.peer(terms[3], 1).astype(F32)).astype(BF)

    def near_sum(self, terms, across):
        return sum_of(terms[0], self.peer(terms[1], 1), across)


def sum_of(*terms):
    return functools.reduce(jnp.add, [term.astype(F32) for term in terms])


def after(value, *earlier):
    return lax.optimization_barrier((value,) + earlier)[0]


def local(
    dp,
    tokens,
    seq_lengths,
    seq_buckets,
    bucket_widths,
    norm_one_gain,
    norm_one_bias,
    qkv_weight,
    out_weight,
    norm_two_gain,
    norm_two_bias,
    ffn_in_weight,
    ffn_out_weight,
    cotangent,
):
    moves = Moves(dp)
    count, rows, model = tokens.shape
    full = rows * FSDP
    slice_rows = norm_one_gain.shape[0]
    ffn = ffn_in_weight.shape[1]
    hidden = ffn // FSDP
    stripe = ffn // (dp * FSDP)
    own = moves.own
    own_array = own.astype(jnp.int32).reshape(1)
    home = [((i * FSDP + j), (j * dp + i)) for i in range(dp) for j in range(FSDP)]
    outward = [(b, a) for a, b in home]

    third = model // FSDP
    heads = third // HEAD_DIM
    qkv_pieces = qkv_weight.reshape(slice_rows, 3, FSDP, heads, HEAD_DIM).transpose(2, 0, 3, 1, 4)
    qkv_shard = moves.exchange(qkv_pieces.reshape(FSDP, slice_rows, 3 * third))
    qkv_shard = qkv_shard.reshape(FSDP * slice_rows, 3 * third)
    vectors = jnp.concatenate([norm_one_gain, norm_one_bias, norm_two_gain, norm_two_bias])
    vectors = jnp.broadcast_to(after(vectors, qkv_shard)[None], (dp * FSDP, 4 * slice_rows))
    vectors = lax.all_to_all(vectors, ("dp", "fsdp"), 0, 0, tiled=True)
    vectors = vectors.reshape(dp * FSDP, 4, slice_rows).transpose(1, 0, 2).reshape(4, model).astype(F32)
    gain_one, bias_one, gain_two, bias_two = vectors[0], vectors[1], vectors[2], vectors[3]
    in_pieces = ffn_in_weight.reshape(slice_rows, dp, FSDP, stripe).transpose(2, 0, 1, 3)
    in_pieces = in_pieces.reshape(FSDP, slice_rows, hidden)
    in_shard = moves.exchange(after(in_pieces, qkv_shard)).reshape(FSDP * slice_rows, hidden)
    out_shard = lax.ppermute(after(out_weight, qkv_shard), ("dp", "fsdp"), outward)
    qkv_far, qkv_first = moves.gather_far(qkv_shard)
    down_mat = lax.all_gather(after(ffn_out_weight, qkv_first), "dp", axis=0, tiled=True)
    in_mat = lax.all_gather(after(in_shard, down_mat), "dp", axis=0, tiled=True)
    out_far, _ = moves.gather_far(after(out_shard, qkv_far))
    qkv_mat = moves.placed(qkv_far, moves.swap(qkv_far, 1)).reshape(model, -1)
    out_mat = moves.placed(out_far, moves.swap(out_far, 1)).reshape(third, model)

    positions = [(own ^ r) * rows + jnp.arange(rows) for r in range(FSDP)]
    live = [(p[None, :] < seq_lengths[:, None])[..., None] for p in positions]
    prefix = jnp.sum(
        jnp.where(jnp.arange(BUCKETS)[None, :] == seq_buckets[:, None], bucket_widths[None, :], 0), axis=1
    )
    turn = FSDP * stripe
    units = (prefix // turn) * stripe + jnp.clip(prefix % turn - own * stripe, 0, stripe)
    starts = (own ^ jnp.arange(FSDP)) * rows
    alive = starts[:, None] < seq_lengths[None, :]
    unit_limits = jnp.where(alive, units[None, :], 0).astype(jnp.int32)
    row_limits = jnp.where(alive, 1 << 20, 0).astype(jnp.int32)
    cos, sin = rotary_tables(full)

    token_blocks = moves.spread(after(tokens, qkv_shard))
    inputs = tokens.astype(F32)
    normed_one = []
    for block in token_blocks:
        value, _ = normalize(block.astype(F32))
        normed_one.append((value * gain_one + bias_one).astype(BF))
    feed_grad = jnp.where(live[0], cotangent, jnp.zeros_like(cotangent))
    feed_grad = moves.spread(after(feed_grad, token_blocks[2]))
    lengths = after(seq_lengths, feed_grad[2], in_shard)
    branch, attended, turned_one, held = attend(lengths, own_array, normed_one, qkv_mat, out_mat, cos, sin)
    across = moves.peer(after(moves.far_sum(branch), down_mat), 2)
    middle = inputs + moves.near_sum(branch, across)
    unit_two, scale_two = normalize(middle)
    normed_two = moves.spread((unit_two * gain_two + bias_two).astype(BF))

    feed, normed_two_grad, active, hidden_grad = [], [], [], []
    for r in (0, 2):
        pair = slice(r, r + 2)
        gate = after(unit_limits[pair], *feed)
        results = feed_both(gate, normed_two[pair], feed_grad[pair], in_mat, down_mat)
        for kept, result in zip((feed, normed_two_grad, active, hidden_grad), results):
            kept.extend(result)

    upstream = jnp.where(live[0], cotangent.astype(F32), 0.0)
    far = moves.far_sum(normed_two_grad)
    gate = after(unit_limits, far)
    grad_in = right_tiles(gate, normed_two, hidden_grad, 256)
    grad_down = left_tiles(after(gate, grad_in), active, feed_grad, 256)
    second_grad = moves.near_sum(normed_two_grad, moves.peer(far, 2))
    second_grad = after(second_grad, grad_in, grad_down)
    grad_in = lax.psum_scatter(grad_in, "dp", scatter_dimension=0, tiled=True)
    grad_in_pieces = moves.exchange(grad_in.reshape(FSDP, slice_rows, hidden))
    grad_gain_two = jnp.sum(second_grad * unit_two, axis=(0, 1))
    grad_bias_two = jnp.sum(second_grad, axis=(0, 1))
    middle_grad = upstream + norm_back(second_grad, gain_two, unit_two, scale_two)
    branch_grad = moves.spread(middle_grad.astype(BF))

    grad_down = lax.psum_scatter(after(grad_down, branch_grad[2]), "dp", scatter_dimension=0, tiled=True)
    out_terms = left_tiles(row_limits, attended, branch_grad, third).reshape(dp, -1, model)
    out_sent, out_kept = moves.halves(out_terms, 1)
    feed[3] = after(feed[3], branch_grad[2])
    far = moves.far_sum(feed)
    across = moves.peer(far, 2)
    beside = moves.peer(feed[1], 1)
    qkv_grad, normed_one_grad = attend_back(
        after(seq_lengths, far, beside, out_sent), own_array, held, branch_grad, qkv_mat, out_mat, cos, sin
    )
    layer_output = jnp.where(live[0], middle + sum_of(feed[0], beside, across), 0.0).astype(BF)
    out_swapped = moves.swap(out_sent, 1)
    far = moves.far_sum([*normed_one_grad[:3], after(normed_one_grad[3], across, out_swapped)])
    gate = after(row_limits, far)
    grad_out = moves.reduce_far(after(out_kept, far).astype(F32) + out_swapped.astype(F32))
    across = moves.peer(far, 2)
    sent, kept = moves.halves(turned_tiles(gate, turned_one, qkv_grad).reshape(dp, -1, 3 * third), 1)
    kept = after(kept, across, grad_in_pieces)
    grad_qkv = moves.reduce_far(kept.astype(F32) + moves.swap(sent, 1).astype(F32))
    first_grad = moves.near_sum(normed_one_grad, across)
    unit_one, scale_one = normalize(inputs)
    input_grad = middle_grad + norm_back(first_grad, gain_one, unit_one, scale_one)
    grad_gain_one = jnp.sum(first_grad * unit_one, axis=(0, 1))
    grad_bias_one = jnp.sum(first_grad, axis=(0, 1))
    sums = moves.total(jnp.stack([grad_gain_one, grad_bias_one, grad_gain_two, grad_bias_two]))

    grad_out = lax.ppermute(grad_out, ("dp", "fsdp"), home)
    grad_qkv = moves.exchange(grad_qkv.astype(BF).reshape(FSDP, slice_rows, 3 * third))
    grad_qkv = grad_qkv.reshape(FSDP, slice_rows, heads, 3, HEAD_DIM).transpose(1, 3, 0, 2, 4).astype(F32)
    grad_qkv = grad_qkv.reshape(slice_rows, 3 * model)
    grad_in = grad_in_pieces.reshape(FSDP, slice_rows, dp, stripe).transpose(1, 2, 0, 3).astype(F32)
    grad_in = grad_in.reshape(slice_rows, ffn)
    return (
        layer_output,
        input_grad,
        sums[0],
        sums[1],
        grad_qkv,
        grad_out,
        sums[2],
        sums[3],
        grad_in,
        grad_down.astype(F32),
    )


def solution(mesh):
    both = ("dp", "fsdp")
    placed = (
        P("dp", "fsdp", None),
        P("dp"),
        P("dp"),
        P(),
        P(both),
        P(both),
        P(both, None),
        P(both, None),
        P(both),
        P(both),
        P(both, None),
        P(both, None),
        P("dp", "fsdp", None),
    )
    return jax.shard_map(
        functools.partial(local, mesh.shape["dp"]),
        mesh=mesh,
        in_specs=placed,
        out_specs=(
            P("dp", "fsdp", None),
            P("dp", "fsdp", None),
            P(both),
            P(both),
            P(both, None),
            P(both, None),
            P(both),
            P(both),
            P(both, None),
            P(both, None),
        ),
        check_vma=False,
    )
```

```python
import functools

import jax
import jax.numpy as jnp
from jax import lax
from jax.experimental import pallas as pl
from jax.experimental.pallas import tpu as pltpu
from jax.sharding import PartitionSpec as P

HEADS = 12
HEAD_DIM = 128
BUCKETS = 4
FSDP = 4

BF = jnp.bfloat16
F32 = jnp.float32
NT = (((1,), (1,)), ((), ()))
TN = (((0,), (0,)), ((), ()))
NN = (((1,), (0,)), ((), ()))


def dot(a, b, dims):
    return lax.dot_general(a, b, dims, preferred_element_type=F32)


def cost(micros):
    return pl.CostEstimate(flops=micros * 10**9, bytes_accessed=micros * 10**6, transcendentals=0)


def rotary_tables(rows):
    half = HEAD_DIM // 2
    inverse = 10000.0 ** (-(jnp.arange(half).astype(F32) * 2.0) / HEAD_DIM)
    angles = jnp.arange(rows).astype(F32)[:, None] * inverse[None, :]
    cos, sin = jnp.cos(angles), jnp.sin(angles)
    return jnp.concatenate([cos, cos], axis=1), jnp.concatenate([-sin, sin], axis=1)


def normalize(values):
    center = values - jnp.mean(values, axis=-1, keepdims=True)
    spread = jnp.mean(center * center, axis=-1, keepdims=True)
    scale = lax.rsqrt(spread + 1e-05)
    return center * scale, scale


def norm_back(grad, gain, normed, scale):
    scaled = grad * gain
    first = jnp.mean(scaled, axis=-1, keepdims=True)
    second = jnp.mean(scaled * normed, axis=-1, keepdims=True)
    return scale * (scaled - first - normed * second)


def scores_of(query, keys):
    rows, cols = query.shape[0], keys.shape[0]
    scores = dot(query, keys, NT) * (HEAD_DIM ** (-0.5))
    row = lax.broadcasted_iota(jnp.int32, (rows, rows), 0)
    col = lax.broadcasted_iota(jnp.int32, (rows, rows), 1)
    last = jnp.where(col <= row, scores[:, cols - rows :], -1e30)
    if cols == rows:
        return last
    return jnp.concatenate([scores[:, : cols - rows], last], axis=1)


def attend_body(len_ref, own_ref, *refs):
    h_in, (w_ref, wo_ref, cos_ref, sin_ref) = refs[0:4], refs[4:8]
    term_refs, out_refs, turned_refs = refs[8:12], refs[12:16], refs[16:20]
    q_ref, k_ref, v_ref, lse_ref, o_ref = refs[20:25]
    rows = h_in[0].shape[1]
    head, heads = pl.program_id(1), pl.num_programs(1)
    length = len_ref[pl.program_id(0)]
    own = own_ref[0]
    for r in range(FSDP):
        start = pl.multiple_of((own ^ r) * rows, rows)
        at = pl.ds(start, rows)

        @pl.when(start < length)
        def _():
            mixed = dot(h_in[r][0], w_ref[...], NN)
            cos, sin = cos_ref[at, :], sin_ref[at, :]
            for part, target in ((0, q_ref), (1, k_ref)):
                value = mixed[:, part * HEAD_DIM : (part + 1) * HEAD_DIM]
                turned = value * cos + pltpu.roll(value, HEAD_DIM // 2, 1) * sin
                target[0, 0, at, :] = turned.astype(BF)
            v_ref[0, 0, at, :] = mixed[:, 2 * HEAD_DIM :].astype(BF)

        @pl.when(head == 0)
        def _():
            turned_refs[r][0] = h_in[r][0].T

    for b in range(FSDP):
        lo, hi = b * rows, (b + 1) * rows

        @pl.when(lo < length)
        def _():
            scores = scores_of(q_ref[0, 0, lo:hi, :], k_ref[0, 0, :hi, :])
            peak = jnp.max(scores, axis=1, keepdims=True)
            expo = jnp.exp(scores - peak)
            total = jnp.sum(expo, axis=1, keepdims=True)
            probs = (expo * (1.0 / total)).astype(BF)
            o_ref[head, lo:hi, :] = dot(probs, v_ref[0, 0, :hi, :], NN).astype(BF)
            lse_ref[0, 0, lo:hi, :] = peak + jnp.log(total)

    @pl.when(head == heads - 1)
    def _():
        for r in range(FSDP):
            start = pl.multiple_of((own ^ r) * rows, rows)
            at = pl.ds(start, rows)

            @pl.when(start < length)
            def _():
                side = jnp.concatenate([o_ref[h, at, :] for h in range(o_ref.shape[0])], axis=1)
                out_refs[r][0] = side
                term_refs[r][0] = dot(side, wo_ref[...], NN).astype(BF)

            @pl.when(start >= length)
            def _():
                out_refs[r][0] = jnp.zeros_like(out_refs[r][0])
                term_refs[r][0] = jnp.zeros_like(term_refs[r][0])


def attend(lengths, own, normed, qkv_mat, out_mat, cos, sin):
    count, rows, model = normed[0].shape
    wide = out_mat.shape[0]
    heads = wide // HEAD_DIM
    full = FSDP * rows
    held = pl.BlockSpec((1, rows, model), lambda s, h, *_: (s, 0, 0))
    side = pl.BlockSpec((1, rows, wide), lambda s, h, *_: (s, 0, 0))
    turned = pl.BlockSpec((1, model, rows), lambda s, h, *_: (s, 0, 0))
    table = pl.BlockSpec((full, HEAD_DIM), lambda s, h, *_: (0, 0))
    whole = pl.BlockSpec((1, 1, full, HEAD_DIM), lambda s, h, *_: (s, h, 0, 0))
    stat = pl.BlockSpec((1, 1, full, 1), lambda s, h, *_: (s, h, 0, 0))
    weight = pl.BlockSpec((model, 3 * HEAD_DIM), lambda s, h, *_: (0, h))
    shape = jax.ShapeDtypeStruct
    outs = pl.pallas_call(
        attend_body,
        grid_spec=pltpu.PrefetchScalarGridSpec(
            num_scalar_prefetch=2,
            grid=(count, heads),
            in_specs=[held] * 4 + [weight, pl.BlockSpec((wide, model), lambda s, h, *_: (0, 0)), table, table],
            out_specs=[held] * 4 + [side] * 4 + [turned] * 4 + [whole] * 3 + [stat],
            scratch_shapes=[pltpu.VMEM((heads, full, HEAD_DIM), BF)],
        ),
        out_shape=[shape((count, rows, model), BF)] * 4
        + [shape((count, rows, wide), BF)] * 4
        + [shape((count, model, rows), BF)] * 4
        + [shape((count, heads, full, HEAD_DIM), BF)] * 3
        + [shape((count, heads, full, 1), F32)],
        cost_estimate=cost(30),
        name="attend",
    )(lengths, own, *normed, qkv_mat, out_mat, cos, sin)
    return outs[0:4], outs[4:8], outs[8:12], outs[12:16]


def attend_back_body(len_ref, own_ref, *refs):
    q_ref, k_ref, v_ref, lse_ref = refs[0:4]
    b_in, (w_ref, wo_ref, cos_ref, sin_ref) = refs[4:8], refs[8:12]
    out_refs, dh_refs = refs[12:16], refs[16:20]
    g_ref, dq_ref, dk_ref, dv_ref, dh_acc = refs[20:25]
    rows = b_in[0].shape[1]
    head, heads = pl.program_id(1), pl.num_programs(1)
    length = len_ref[pl.program_id(0)]
    own = own_ref[0]
    inv_root = HEAD_DIM ** (-0.5)
    for r in range(FSDP):
        start = pl.multiple_of((own ^ r) * rows, rows)

        @pl.when(start < length)
        def _():
            g_ref[pl.ds(start, rows), :] = dot(b_in[r][0], wo_ref[...], NT).astype(BF)

    dk_ref[...] = jnp.zeros_like(dk_ref)
    dv_ref[...] = jnp.zeros_like(dv_ref)
    for b in range(FSDP):
        lo, hi = b * rows, (b + 1) * rows

        @pl.when(lo < length)
        def _():
            query, keys, values = q_ref[0, 0, lo:hi, :], k_ref[0, 0, :hi, :], v_ref[0, 0, :hi, :]
            grad = g_ref[lo:hi, :]
            probs = jnp.exp(scores_of(query, keys) - lse_ref[0, 0, lo:hi, :])
            prob_grad = dot(grad, values, NT)
            row_dot = jnp.sum(probs * prob_grad, axis=1, keepdims=True)
            score_grad = (probs * (prob_grad - row_dot)).astype(BF)
            dq_ref[lo:hi, :] = dot(score_grad, keys, NN) * inv_root
            dk_ref[:hi, :] += dot(score_grad, query, TN)
            dv_ref[:hi, :] += dot(probs.astype(BF), grad, TN)

    @pl.when(head == 0)
    def _():
        dh_acc[...] = jnp.zeros_like(dh_acc)

    for r in range(FSDP):
        start = pl.multiple_of((own ^ r) * rows, rows)
        at = pl.ds(start, rows)

        @pl.when(start < length)
        def _():
            cos, sin = cos_ref[at, :], sin_ref[at, :]
            dq, dk = dq_ref[at, :], dk_ref[at, :] * inv_root
            dq = dq * cos - pltpu.roll(dq, HEAD_DIM // 2, 1) * sin
            dk = dk * cos - pltpu.roll(dk, HEAD_DIM // 2, 1) * sin
            grads = jnp.concatenate([dq.astype(BF), dk.astype(BF), dv_ref[at, :].astype(BF)], axis=1)
            out_refs[r][0] = grads
            dh_acc[r] += dot(grads, w_ref[...], NT)

        @pl.when(start >= length)
        def _():
            out_refs[r][0] = jnp.zeros_like(out_refs[r][0])

        @pl.when(head == heads - 1)
        def _():
            dh_refs[r][0] = dh_acc[r].astype(BF)


def attend_back(lengths, own, held, grads, qkv_mat, out_mat, cos, sin):
    count, rows, model = grads[0].shape
    heads = out_mat.shape[0] // HEAD_DIM
    full = FSDP * rows
    block = pl.BlockSpec((1, rows, model), lambda s, h, *_: (s, 0, 0))
    table = pl.BlockSpec((full, HEAD_DIM), lambda s, h, *_: (0, 0))
    whole = pl.BlockSpec((1, 1, full, HEAD_DIM), lambda s, h, *_: (s, h, 0, 0))
    stat = pl.BlockSpec((1, 1, full, 1), lambda s, h, *_: (s, h, 0, 0))
    result = pl.BlockSpec((1, rows, 3 * HEAD_DIM), lambda s, h, *_: (s, 0, h))
    shape = jax.ShapeDtypeStruct
    outs = pl.pallas_call(
        attend_back_body,
        grid_spec=pltpu.PrefetchScalarGridSpec(
            num_scalar_prefetch=2,
            grid=(count, heads),
            in_specs=[whole] * 3
            + [stat]
            + [block] * 4
            + [
                pl.BlockSpec((model, 3 * HEAD_DIM), lambda s, h, *_: (0, h)),
                pl.BlockSpec((HEAD_DIM, model), lambda s, h, *_: (h, 0)),
                table,
                table,
            ],
            out_specs=[result] * 4 + [block] * 4,
            scratch_shapes=[
                pltpu.VMEM((full, HEAD_DIM), BF),
                pltpu.VMEM((full, HEAD_DIM), F32),
                pltpu.VMEM((full, HEAD_DIM), F32),
                pltpu.VMEM((full, HEAD_DIM), F32),
                pltpu.VMEM((FSDP, rows, model), F32),
            ],
        ),
        out_shape=[shape((count, rows, 3 * HEAD_DIM * heads), BF)] * 4 + [shape((count, rows, model), BF)] * 4,
        cost_estimate=cost(35),
        name="attend_back",
    )(lengths, own, *held, *grads, qkv_mat, out_mat, cos, sin)
    return outs[0:4], outs[4:8]


ROOT = 0.7978845608028654
CUBE = 0.044715


def feed_body(limit_ref, *refs):
    h_refs, g_refs, (in_ref, down_ref) = refs[0:2], refs[2:4], refs[4:6]
    f_refs, dh_refs, a_refs, du_refs = refs[6:8], refs[8:10], refs[10:12], refs[12:14]
    f_acc, dh_acc = refs[14:16]
    step = pl.program_id(0)
    count = h_refs[0].shape[0]
    tile = in_ref.shape[1]

    @pl.when(step == 0)
    def _():
        f_acc[...] = jnp.zeros_like(f_acc)
        dh_acc[...] = jnp.zeros_like(dh_acc)

    for r in range(2):
        for s in range(count):
            limit = limit_ref[r, s] - step * tile

            @pl.when(limit > 0)
            def _():
                h, g = h_refs[r][s], g_refs[r][s]
                pre = dot(h, in_ref[...], NN)
                keep = lax.broadcasted_iota(jnp.int32, pre.shape, 1) < limit
                bend = jnp.tanh(ROOT * (pre + CUBE * pre * pre * pre))
                half = 0.5 * (1.0 + bend)
                slope = half + 0.5 * pre * (1.0 - bend * bend) * (ROOT * (1.0 + 3.0 * CUBE * pre * pre))
                active = jnp.where(keep, pre * half, 0.0).astype(BF)
                a_refs[r][s] = active
                f_acc[r, s] += dot(active, down_ref[...], NN)
                back = dot(g, down_ref[...], NT)
                grad = jnp.where(keep, back * slope, 0.0).astype(BF)
                du_refs[r][s] = grad
                dh_acc[r, s] += dot(grad, in_ref[...], NT)

            @pl.when(limit <= 0)
            def _():
                a_refs[r][s] = jnp.zeros_like(a_refs[r][s])
                du_refs[r][s] = jnp.zeros_like(du_refs[r][s])

    @pl.when(step == pl.num_programs(0) - 1)
    def _():
        for r in range(2):
            f_refs[r][...] = f_acc[r].astype(f_refs[r].dtype)
            dh_refs[r][...] = dh_acc[r].astype(dh_refs[r].dtype)


def feed_both(limits, h, g, in_mat, down_mat):
    count, rows, model = h[0].shape
    hidden = in_mat.shape[1]
    tile = 256
    held = pl.BlockSpec((count, rows, model), lambda t, *_: (0, 0, 0))
    units = pl.BlockSpec((count, rows, tile), lambda t, *_: (0, 0, t))
    outs = pl.pallas_call(
        feed_body,
        grid_spec=pltpu.PrefetchScalarGridSpec(
            num_scalar_prefetch=1,
            grid=(hidden // tile,),
            in_specs=[held] * 4
            + [
                pl.BlockSpec((model, tile), lambda t, *_: (0, t)),
                pl.BlockSpec((tile, model), lambda t, *_: (t, 0)),
            ],
            out_specs=[held] * 4 + [units] * 4,
            scratch_shapes=[pltpu.VMEM((2, count, rows, model), F32)] * 2,
        ),
        out_shape=[jax.ShapeDtypeStruct(h[0].shape, BF)] * 4
        + [jax.ShapeDtypeStruct((count, rows, hidden), BF)] * 4,
        cost_estimate=cost(20),
        name="feed_both",
    )(limits, *h, *g, in_mat, down_mat)
    return outs[0:2], outs[2:4], outs[4:6], outs[6:8]


def left_tiles_body(limit_ref, *refs):
    left, right = refs[0:4], refs[4:8]
    out_ref, acc = refs[8], refs[9]
    tile = out_ref.shape[0]
    acc[...] = jnp.zeros_like(acc)
    for r in range(FSDP):
        for s in range(left[0].shape[0]):

            @pl.when(limit_ref[r, s] > pl.program_id(0) * tile)
            def _():
                acc[...] += dot(left[r][s], right[r][s], TN)

    out_ref[...] = acc[...].astype(BF)


def left_tiles(limits, left, right, tile):
    count, rows, wide = left[0].shape
    cols = right[0].shape[2]
    return pl.pallas_call(
        left_tiles_body,
        grid_spec=pltpu.PrefetchScalarGridSpec(
            num_scalar_prefetch=1,
            grid=(wide // tile,),
            in_specs=[pl.BlockSpec((count, rows, tile), lambda t, *_: (0, 0, t))] * 4
            + [pl.BlockSpec((count, rows, cols), lambda t, *_: (0, 0, 0))] * 4,
            out_specs=pl.BlockSpec((tile, cols), lambda t, *_: (t, 0)),
            scratch_shapes=[pltpu.VMEM((tile, cols), F32)],
        ),
        out_shape=jax.ShapeDtypeStruct((wide, cols), BF),
        cost_estimate=cost(12),
        name="left_tiles",
    )(limits, *left, *right)


def right_tiles_body(limit_ref, *refs):
    left, right = refs[0:4], refs[4:8]
    out_ref, acc, turned = refs[8:11]
    tile = out_ref.shape[1]
    count = left[0].shape[0]

    @pl.when(pl.program_id(0) == 0)
    def _():
        for r in range(FSDP):
            for s in range(count):
                turned[r * count + s] = left[r][s].T

    acc[...] = jnp.zeros_like(acc)
    for r in range(FSDP):
        for s in range(count):

            @pl.when(limit_ref[r, s] > pl.program_id(0) * tile)
            def _():
                acc[...] += dot(turned[r * count + s], right[r][s], NN)

    out_ref[...] = acc[...].astype(BF)


def right_tiles(limits, left, right, tile):
    count, rows, wide = left[0].shape
    cols = right[0].shape[2]
    return pl.pallas_call(
        right_tiles_body,
        grid_spec=pltpu.PrefetchScalarGridSpec(
            num_scalar_prefetch=1,
            grid=(cols // tile,),
            in_specs=[pl.BlockSpec((count, rows, wide), lambda t, *_: (0, 0, 0))] * 4
            + [pl.BlockSpec((count, rows, tile), lambda t, *_: (0, 0, t))] * 4,
            out_specs=pl.BlockSpec((wide, tile), lambda t, *_: (0, t)),
            scratch_shapes=[pltpu.VMEM((wide, tile), F32), pltpu.VMEM((4 * count, wide, rows), BF)],
        ),
        out_shape=jax.ShapeDtypeStruct((wide, cols), BF),
        cost_estimate=cost(14),
        name="right_tiles",
    )(limits, *left, *right)


def turned_tiles_body(limit_ref, *refs):
    left, right, out_ref, acc = refs[0:4], refs[4:8], refs[8], refs[9]
    acc[...] = jnp.zeros_like(acc)
    for r in range(FSDP):
        for s in range(left[0].shape[0]):

            @pl.when(limit_ref[r, s] > 0)
            def _():
                acc[...] += dot(left[r][s], right[r][s], NN)

    out_ref[...] = acc[...].astype(BF)


def turned_tiles(limits, left, right):
    count, wide, rows = left[0].shape
    cols = right[0].shape[2]
    step = 512
    return pl.pallas_call(
        turned_tiles_body,
        grid_spec=pltpu.PrefetchScalarGridSpec(
            num_scalar_prefetch=1,
            grid=(wide // step,),
            in_specs=[pl.BlockSpec((count, step, rows), lambda t, *_: (0, t, 0))] * 4
            + [pl.BlockSpec((count, rows, cols), lambda t, *_: (0, 0, 0))] * 4,
            out_specs=pl.BlockSpec((step, cols), lambda t, *_: (t, 0)),
            scratch_shapes=[pltpu.VMEM((step, cols), F32)],
        ),
        out_shape=jax.ShapeDtypeStruct((wide, cols), BF),
        cost_estimate=cost(20),
        name="turned_tiles",
    )(limits, *left, *right)


def place_body(at_ref, near_ref, far_ref, out_ref):
    half = pl.num_programs(0) // 2

    @pl.when(pl.program_id(0) < half)
    def _():
        out_ref[...] = near_ref[...]

    @pl.when(pl.program_id(0) >= half)
    def _():
        out_ref[...] = far_ref[...]


def place(near, far, ats):
    half, rows, cols = near.shape
    return pl.pallas_call(
        place_body,
        grid_spec=pltpu.PrefetchScalarGridSpec(
            num_scalar_prefetch=1,
            grid=(2 * half,),
            in_specs=[
                pl.BlockSpec((1, rows, cols), lambda n, *_: (jnp.minimum(n, half - 1), 0, 0)),
                pl.BlockSpec((1, rows, cols), lambda n, *_: (jnp.maximum(n - half, 0), 0, 0)),
            ],
            out_specs=pl.BlockSpec((1, rows, cols), lambda n, at: (at[n], 0, 0)),
        ),
        out_shape=jax.ShapeDtypeStruct((2 * half, rows, cols), near.dtype),
        cost_estimate=cost(6),
        name="place",
    )(ats, near, far)


class Moves:
    def __init__(self, dp):
        self.dp = dp
        self.at = lax.axis_index("dp")
        self.own = lax.axis_index("fsdp")
        self.bits = [1 << n for n in range(dp.bit_length() - 1)]

    def peer(self, value, r):
        return lax.ppermute(value, "fsdp", [(j, j ^ r) for j in range(FSDP)])

    def swap(self, value, bit):
        return lax.ppermute(value, "dp", [(i, i ^ bit) for i in range(self.dp)])

    def gather_far(self, shard):
        parts = shard[None]
        for bit in self.bits[:0:-1]:
            parts = jnp.concatenate([parts, self.swap(parts, bit)])
        return parts

    def placed(self, parts, swapped):
        marks = [0]
        for bit in self.bits[:0:-1]:
            marks += [mark ^ bit for mark in marks]
        marks += [mark ^ 1 for mark in marks]
        return place(parts, swapped, (self.at ^ jnp.array(marks)).astype(jnp.int32))

    def halves(self, total, bit):
        mine = (self.at // bit) % 2
        pairs = total.reshape(total.shape[0] // 2, 2, *total.shape[1:])
        sent = lax.dynamic_index_in_dim(pairs, 1 - mine, 1, keepdims=False).astype(BF)
        return sent, lax.dynamic_index_in_dim(pairs, mine, 1, keepdims=False)

    def reduce_far(self, total, done, *earlier):
        for bit in self.bits[done:]:
            sent, kept = self.halves(total, bit)
            total = after(kept, *earlier).astype(F32) + self.swap(sent, bit).astype(F32)
        return total.reshape(total.shape[1:])

    def exchange(self, pieces):
        return lax.all_to_all(pieces, "fsdp", 0, 0, tiled=True)

    def total(self, value):
        devices = self.dp * FSDP
        parts = value.reshape(value.shape[0], devices, -1).transpose(1, 0, 2)
        size = parts.shape[2]
        parts = lax.all_to_all(parts.reshape(devices, -1), ("dp", "fsdp"), 0, 0, tiled=True)
        return jnp.sum(parts, axis=0).reshape(-1, size)

    def spread(self, block):
        across = self.peer(block, 2)
        return [block, self.peer(block, 1), across, self.peer(across, 1)]

    def far_sum(self, terms):
        return (terms[2].astype(F32) + self.peer(terms[3], 1).astype(F32)).astype(BF)

    def near_sum(self, terms, across):
        return sum_of(terms[0], self.peer(terms[1], 1), across)


def sum_of(*terms):
    return functools.reduce(jnp.add, [term.astype(F32) for term in terms])


def after(value, *earlier):
    return lax.optimization_barrier((value,) + earlier)[0]


def local(
    dp,
    tokens,
    seq_lengths,
    seq_buckets,
    bucket_widths,
    norm_one_gain,
    norm_one_bias,
    qkv_weight,
    out_weight,
    norm_two_gain,
    norm_two_bias,
    ffn_in_weight,
    ffn_out_weight,
    cotangent,
):
    moves = Moves(dp)
    count, rows, model = tokens.shape
    full = rows * FSDP
    slice_rows = norm_one_gain.shape[0]
    ffn = ffn_in_weight.shape[1]
    hidden = ffn // FSDP
    stripe = ffn // (dp * FSDP)
    own = moves.own
    own_array = own.astype(jnp.int32).reshape(1)
    home = [((i * FSDP + j), (j * dp + i)) for i in range(dp) for j in range(FSDP)]
    outward = [(b, a) for a, b in home]

    third = model // FSDP
    heads = third // HEAD_DIM
    qkv_pieces = qkv_weight.reshape(slice_rows, 3, FSDP, heads, HEAD_DIM).transpose(2, 0, 3, 1, 4)
    qkv_shard = moves.exchange(qkv_pieces.reshape(FSDP, slice_rows, 3 * third))
    qkv_shard = qkv_shard.reshape(FSDP * slice_rows, 3 * third)
    vectors = jnp.concatenate([norm_one_gain, norm_one_bias, norm_two_gain, norm_two_bias])
    vectors = jnp.broadcast_to(after(vectors, qkv_shard)[None], (dp * FSDP, 4 * slice_rows))
    vectors = lax.all_to_all(vectors, ("dp", "fsdp"), 0, 0, tiled=True)
    vectors = vectors.reshape(dp * FSDP, 4, slice_rows).transpose(1, 0, 2).reshape(4, model).astype(F32)
    gain_one, bias_one, gain_two, bias_two = vectors[0], vectors[1], vectors[2], vectors[3]
    in_pieces = ffn_in_weight.reshape(slice_rows, dp, FSDP, stripe).transpose(2, 0, 1, 3)
    in_pieces = in_pieces.reshape(FSDP, slice_rows, hidden)
    in_shard = moves.exchange(after(in_pieces, qkv_shard)).reshape(FSDP * slice_rows, hidden)
    out_shard = lax.ppermute(after(out_weight, qkv_shard), ("dp", "fsdp"), outward)
    qkv_far = moves.gather_far(qkv_shard)
    qkv_swapped = moves.swap(qkv_far, 1)
    down_mat = lax.all_gather(after(ffn_out_weight, qkv_far), "dp", axis=0, tiled=True)
    in_mat = lax.all_gather(after(in_shard, qkv_swapped), "dp", axis=0, tiled=True)
    out_far = moves.gather_far(after(out_shard, qkv_far))
    out_mat = moves.placed(out_far, moves.swap(out_far, 1)).reshape(third, model)

    positions = [(own ^ r) * rows + jnp.arange(rows) for r in range(FSDP)]
    live = [(p[None, :] < seq_lengths[:, None])[..., None] for p in positions]
    prefix = jnp.sum(
        jnp.where(jnp.arange(BUCKETS)[None, :] == seq_buckets[:, None], bucket_widths[None, :], 0), axis=1
    )
    turn = FSDP * stripe
    units = (prefix // turn) * stripe + jnp.clip(prefix % turn - own * stripe, 0, stripe)
    starts = (own ^ jnp.arange(FSDP)) * rows
    alive = starts[:, None] < seq_lengths[None, :]
    unit_limits = jnp.where(alive, units[None, :], 0).astype(jnp.int32)
    row_limits = jnp.where(alive, 1 << 20, 0).astype(jnp.int32)
    cos, sin = rotary_tables(full)

    token_blocks = moves.spread(after(tokens, qkv_shard))
    inputs = tokens.astype(F32)
    normed_one = []
    for block in token_blocks:
        value, _ = normalize(block.astype(F32))
        normed_one.append((value * gain_one + bias_one).astype(BF))
    qkv_mat = moves.placed(qkv_far, after(qkv_swapped, *normed_one)).reshape(model, -1)
    feed_grad = jnp.where(live[0], cotangent, jnp.zeros_like(cotangent))
    feed_grad = moves.spread(after(feed_grad, token_blocks[2]))
    lengths = after(seq_lengths, feed_grad[2], in_shard)
    branch, attended, turned_one, held = attend(lengths, own_array, normed_one, qkv_mat, out_mat, cos, sin)
    across = moves.peer(after(moves.far_sum(branch), down_mat), 2)
    middle = inputs + moves.near_sum(branch, across)
    unit_two, scale_two = normalize(middle)
    normed_two = moves.spread((unit_two * gain_two + bias_two).astype(BF))

    feed, normed_two_grad, active, hidden_grad = [], [], [], []
    for r in (0, 2):
        pair = slice(r, r + 2)
        gate = after(unit_limits[pair], *feed)
        results = feed_both(gate, normed_two[pair], feed_grad[pair], in_mat, down_mat)
        for kept, result in zip((feed, normed_two_grad, active, hidden_grad), results):
            kept.extend(result)

    upstream = jnp.where(live[0], cotangent.astype(F32), 0.0)
    far = moves.far_sum(normed_two_grad)
    gate = after(unit_limits, far)
    grad_down = left_tiles(gate, active, feed_grad, 256)
    grad_in = right_tiles(after(gate, grad_down), normed_two, hidden_grad, 256)
    in_sent, in_kept = moves.halves(grad_in.reshape(dp, -1, hidden), 1)
    in_swapped = moves.swap(in_sent, 1)
    second_grad = moves.near_sum(normed_two_grad, moves.peer(far, 2))
    second_grad = after(second_grad, in_sent)
    grad_gain_two = jnp.sum(second_grad * unit_two, axis=(0, 1))
    grad_bias_two = jnp.sum(second_grad, axis=(0, 1))
    middle_grad = upstream + norm_back(second_grad, gain_two, unit_two, scale_two)
    branch_grad = moves.spread(middle_grad.astype(BF))

    grad_down = lax.psum_scatter(grad_down, "dp", scatter_dimension=0, tiled=True)
    out_terms = left_tiles(row_limits, attended, branch_grad, third).reshape(dp, -1, model)
    out_sent, out_kept = moves.halves(out_terms, 1)
    feed[3] = after(feed[3], branch_grad[2])
    far = moves.far_sum(feed)
    across = moves.peer(far, 2)
    beside = moves.peer(feed[1], 1)
    grad_in = after(in_kept, branch_grad[2]).astype(F32) + in_swapped.astype(F32)
    in_sent, in_kept = moves.halves(grad_in, moves.bits[1])
    in_swapped = moves.swap(in_sent, moves.bits[1])
    qkv_grad, normed_one_grad = attend_back(
        after(seq_lengths, far, beside, out_sent, in_sent), own_array, held, branch_grad, qkv_mat, out_mat, cos, sin
    )
    layer_output = jnp.where(live[0], middle + sum_of(feed[0], beside, across), 0.0).astype(BF)
    out_swapped = moves.swap(out_sent, 1)
    far = moves.far_sum([*normed_one_grad[:3], after(normed_one_grad[3], across, out_swapped, in_swapped)])
    gate = after(row_limits, far)
    grad_out = moves.reduce_far(after(out_kept, far).astype(F32) + out_swapped.astype(F32), 1)
    grad_in = moves.reduce_far(after(in_kept, far).astype(F32) + in_swapped.astype(F32), 2, grad_down)
    grad_in = moves.exchange(grad_in.astype(BF).reshape(FSDP, slice_rows, hidden))
    across = moves.peer(far, 2)
    sent, kept = moves.halves(turned_tiles(gate, turned_one, qkv_grad).reshape(dp, -1, 3 * third), 1)
    kept = after(kept, across)
    grad_qkv = moves.reduce_far(kept.astype(F32) + moves.swap(sent, 1).astype(F32), 1, grad_in)
    first_grad = moves.near_sum(normed_one_grad, across)
    unit_one, scale_one = normalize(inputs)
    input_grad = middle_grad + norm_back(first_grad, gain_one, unit_one, scale_one)
    grad_gain_one = jnp.sum(first_grad * unit_one, axis=(0, 1))
    grad_bias_one = jnp.sum(first_grad, axis=(0, 1))
    sums = moves.total(jnp.stack([grad_gain_one, grad_bias_one, grad_gain_two, grad_bias_two]))

    grad_out = lax.ppermute(grad_out, ("dp", "fsdp"), home)
    grad_qkv = moves.exchange(grad_qkv.astype(BF).reshape(FSDP, slice_rows, 3 * third))
    grad_qkv = grad_qkv.reshape(FSDP, slice_rows, heads, 3, HEAD_DIM).transpose(1, 3, 0, 2, 4).astype(F32)
    grad_qkv = grad_qkv.reshape(slice_rows, 3 * model)
    grad_in = grad_in.reshape(FSDP, slice_rows, dp, stripe).transpose(1, 2, 0, 3).astype(F32)
    grad_in = grad_in.reshape(slice_rows, ffn)
    return (
        layer_output,
        input_grad,
        sums[0],
        sums[1],
        grad_qkv,
        grad_out,
        sums[2],
        sums[3],
        grad_in,
        grad_down.astype(F32),
    )


def solution(mesh):
    both = ("dp", "fsdp")
    placed = (
        P("dp", "fsdp", None),
        P("dp"),
        P("dp"),
        P(),
        P(both),
        P(both),
        P(both, None),
        P(both, None),
        P(both),
        P(both),
        P(both, None),
        P(both, None),
        P("dp", "fsdp", None),
    )
    return jax.shard_map(
        functools.partial(local, mesh.shape["dp"]),
        mesh=mesh,
        in_specs=placed,
        out_specs=(
            P("dp", "fsdp", None),
            P("dp", "fsdp", None),
            P(both),
            P(both),
            P(both, None),
            P(both, None),
            P(both),
            P(both),
            P(both, None),
            P(both, None),
        ),
        check_vma=False,
    )
```

```python
import functools

import jax
import jax.numpy as jnp
from jax import lax
from jax.experimental import pallas as pl
from jax.experimental.pallas import tpu as pltpu
from jax.sharding import PartitionSpec as P

HEADS = 12
HEAD_DIM = 128
BUCKETS = 4
FSDP = 4

BF = jnp.bfloat16
F32 = jnp.float32
NT = (((1,), (1,)), ((), ()))
TN = (((0,), (0,)), ((), ()))
NN = (((1,), (0,)), ((), ()))


def dot(a, b, dims):
    return lax.dot_general(a, b, dims, preferred_element_type=F32)


def cost(micros):
    return pl.CostEstimate(flops=micros * 10**9, bytes_accessed=micros * 10**6, transcendentals=0)


def rotary_tables(rows):
    half = HEAD_DIM // 2
    inverse = 10000.0 ** (-(jnp.arange(half).astype(F32) * 2.0) / HEAD_DIM)
    angles = jnp.arange(rows).astype(F32)[:, None] * inverse[None, :]
    cos, sin = jnp.cos(angles), jnp.sin(angles)
    return jnp.concatenate([cos, cos], axis=1), jnp.concatenate([-sin, sin], axis=1)


def normalize(values):
    center = values - jnp.mean(values, axis=-1, keepdims=True)
    spread = jnp.mean(center * center, axis=-1, keepdims=True)
    scale = lax.rsqrt(spread + 1e-05)
    return center * scale, scale


def norm_back(grad, gain, normed, scale):
    scaled = grad * gain
    first = jnp.mean(scaled, axis=-1, keepdims=True)
    second = jnp.mean(scaled * normed, axis=-1, keepdims=True)
    return scale * (scaled - first - normed * second)


def scores_of(query, keys):
    rows, cols = query.shape[0], keys.shape[0]
    scores = dot(query, keys, NT) * (HEAD_DIM ** (-0.5))
    row = lax.broadcasted_iota(jnp.int32, (rows, rows), 0)
    col = lax.broadcasted_iota(jnp.int32, (rows, rows), 1)
    last = jnp.where(col <= row, scores[:, cols - rows :], -1e30)
    if cols == rows:
        return last
    return jnp.concatenate([scores[:, : cols - rows], last], axis=1)


def attend_body(len_ref, own_ref, *refs):
    h_in, (w_ref, wo_ref, cos_ref, sin_ref) = refs[0:4], refs[4:8]
    term_refs, out_refs, turned_refs = refs[8:12], refs[12:16], refs[16:20]
    q_ref, k_ref, v_ref, lse_ref, o_ref = refs[20:25]
    rows = h_in[0].shape[1]
    head, heads = pl.program_id(1), pl.num_programs(1)
    length = len_ref[pl.program_id(0)]
    own = own_ref[0]
    for r in range(FSDP):
        start = pl.multiple_of((own ^ r) * rows, rows)
        at = pl.ds(start, rows)

        @pl.when(start < length)
        def _():
            mixed = dot(h_in[r][0], w_ref[...], NN)
            cos, sin = cos_ref[at, :], sin_ref[at, :]
            for part, target in ((0, q_ref), (1, k_ref)):
                value = mixed[:, part * HEAD_DIM : (part + 1) * HEAD_DIM]
                turned = value * cos + pltpu.roll(value, HEAD_DIM // 2, 1) * sin
                target[0, 0, at, :] = turned.astype(BF)
            v_ref[0, 0, at, :] = mixed[:, 2 * HEAD_DIM :].astype(BF)

        @pl.when(head == 0)
        def _():
            turned_refs[r][0] = h_in[r][0].T

    for b in range(FSDP):
        lo, hi = b * rows, (b + 1) * rows

        @pl.when(lo < length)
        def _():
            scores = scores_of(q_ref[0, 0, lo:hi, :], k_ref[0, 0, :hi, :])
            peak = jnp.max(scores, axis=1, keepdims=True)
            expo = jnp.exp(scores - peak)
            total = jnp.sum(expo, axis=1, keepdims=True)
            probs = (expo * (1.0 / total)).astype(BF)
            o_ref[head, lo:hi, :] = dot(probs, v_ref[0, 0, :hi, :], NN).astype(BF)
            lse_ref[0, 0, lo:hi, :] = peak + jnp.log(total)

    @pl.when(head == heads - 1)
    def _():
        for r in range(FSDP):
            start = pl.multiple_of((own ^ r) * rows, rows)
            at = pl.ds(start, rows)

            @pl.when(start < length)
            def _():
                side = jnp.concatenate([o_ref[h, at, :] for h in range(o_ref.shape[0])], axis=1)
                out_refs[r][0] = side
                term_refs[r][0] = dot(side, wo_ref[...], NN).astype(BF)

            @pl.when(start >= length)
            def _():
                out_refs[r][0] = jnp.zeros_like(out_refs[r][0])
                term_refs[r][0] = jnp.zeros_like(term_refs[r][0])


def attend(lengths, own, normed, qkv_mat, out_mat, cos, sin):
    count, rows, model = normed[0].shape
    wide = out_mat.shape[0]
    heads = wide // HEAD_DIM
    full = FSDP * rows
    held = pl.BlockSpec((1, rows, model), lambda s, h, *_: (s, 0, 0))
    side = pl.BlockSpec((1, rows, wide), lambda s, h, *_: (s, 0, 0))
    turned = pl.BlockSpec((1, model, rows), lambda s, h, *_: (s, 0, 0))
    table = pl.BlockSpec((full, HEAD_DIM), lambda s, h, *_: (0, 0))
    whole = pl.BlockSpec((1, 1, full, HEAD_DIM), lambda s, h, *_: (s, h, 0, 0))
    stat = pl.BlockSpec((1, 1, full, 1), lambda s, h, *_: (s, h, 0, 0))
    weight = pl.BlockSpec((model, 3 * HEAD_DIM), lambda s, h, *_: (0, h))
    shape = jax.ShapeDtypeStruct
    outs = pl.pallas_call(
        attend_body,
        grid_spec=pltpu.PrefetchScalarGridSpec(
            num_scalar_prefetch=2,
            grid=(count, heads),
            in_specs=[held] * 4 + [weight, pl.BlockSpec((wide, model), lambda s, h, *_: (0, 0)), table, table],
            out_specs=[held] * 4 + [side] * 4 + [turned] * 4 + [whole] * 3 + [stat],
            scratch_shapes=[pltpu.VMEM((heads, full, HEAD_DIM), BF)],
        ),
        out_shape=[shape((count, rows, model), BF)] * 4
        + [shape((count, rows, wide), BF)] * 4
        + [shape((count, model, rows), BF)] * 4
        + [shape((count, heads, full, HEAD_DIM), BF)] * 3
        + [shape((count, heads, full, 1), F32)],
        cost_estimate=cost(30),
        name="attend",
    )(lengths, own, *normed, qkv_mat, out_mat, cos, sin)
    return outs[0:4], outs[4:8], outs[8:12], outs[12:16]


def attend_back_body(len_ref, own_ref, *refs):
    q_ref, k_ref, v_ref, lse_ref = refs[0:4]
    b_in, (w_ref, wo_ref, cos_ref, sin_ref) = refs[4:8], refs[8:12]
    out_refs, dh_refs = refs[12:16], refs[16:20]
    g_ref, dq_ref, dk_ref, dv_ref, dh_acc = refs[20:25]
    rows = b_in[0].shape[1]
    head, heads = pl.program_id(1), pl.num_programs(1)
    length = len_ref[pl.program_id(0)]
    own = own_ref[0]
    inv_root = HEAD_DIM ** (-0.5)
    for r in range(FSDP):
        start = pl.multiple_of((own ^ r) * rows, rows)

        @pl.when(start < length)
        def _():
            g_ref[pl.ds(start, rows), :] = dot(b_in[r][0], wo_ref[...], NT).astype(BF)

    dk_ref[...] = jnp.zeros_like(dk_ref)
    dv_ref[...] = jnp.zeros_like(dv_ref)
    for b in range(FSDP):
        lo, hi = b * rows, (b + 1) * rows

        @pl.when(lo < length)
        def _():
            query, keys, values = q_ref[0, 0, lo:hi, :], k_ref[0, 0, :hi, :], v_ref[0, 0, :hi, :]
            grad = g_ref[lo:hi, :]
            probs = jnp.exp(scores_of(query, keys) - lse_ref[0, 0, lo:hi, :])
            prob_grad = dot(grad, values, NT)
            row_dot = jnp.sum(probs * prob_grad, axis=1, keepdims=True)
            score_grad = (probs * (prob_grad - row_dot)).astype(BF)
            dq_ref[lo:hi, :] = dot(score_grad, keys, NN) * inv_root
            dk_ref[:hi, :] += dot(score_grad, query, TN)
            dv_ref[:hi, :] += dot(probs.astype(BF), grad, TN)

    @pl.when(head == 0)
    def _():
        dh_acc[...] = jnp.zeros_like(dh_acc)

    for r in range(FSDP):
        start = pl.multiple_of((own ^ r) * rows, rows)
        at = pl.ds(start, rows)

        @pl.when(start < length)
        def _():
            cos, sin = cos_ref[at, :], sin_ref[at, :]
            dq, dk = dq_ref[at, :], dk_ref[at, :] * inv_root
            dq = dq * cos - pltpu.roll(dq, HEAD_DIM // 2, 1) * sin
            dk = dk * cos - pltpu.roll(dk, HEAD_DIM // 2, 1) * sin
            grads = jnp.concatenate([dq.astype(BF), dk.astype(BF), dv_ref[at, :].astype(BF)], axis=1)
            out_refs[r][0] = grads
            dh_acc[r] += dot(grads, w_ref[...], NT)

        @pl.when(start >= length)
        def _():
            out_refs[r][0] = jnp.zeros_like(out_refs[r][0])

        @pl.when(head == heads - 1)
        def _():
            dh_refs[r][0] = dh_acc[r].astype(BF)


def attend_back(lengths, own, held, grads, qkv_mat, out_mat, cos, sin):
    count, rows, model = grads[0].shape
    heads = out_mat.shape[0] // HEAD_DIM
    full = FSDP * rows
    block = pl.BlockSpec((1, rows, model), lambda s, h, *_: (s, 0, 0))
    table = pl.BlockSpec((full, HEAD_DIM), lambda s, h, *_: (0, 0))
    whole = pl.BlockSpec((1, 1, full, HEAD_DIM), lambda s, h, *_: (s, h, 0, 0))
    stat = pl.BlockSpec((1, 1, full, 1), lambda s, h, *_: (s, h, 0, 0))
    result = pl.BlockSpec((1, rows, 3 * HEAD_DIM), lambda s, h, *_: (s, 0, h))
    shape = jax.ShapeDtypeStruct
    outs = pl.pallas_call(
        attend_back_body,
        grid_spec=pltpu.PrefetchScalarGridSpec(
            num_scalar_prefetch=2,
            grid=(count, heads),
            in_specs=[whole] * 3
            + [stat]
            + [block] * 4
            + [
                pl.BlockSpec((model, 3 * HEAD_DIM), lambda s, h, *_: (0, h)),
                pl.BlockSpec((HEAD_DIM, model), lambda s, h, *_: (h, 0)),
                table,
                table,
            ],
            out_specs=[result] * 4 + [block] * 4,
            scratch_shapes=[
                pltpu.VMEM((full, HEAD_DIM), BF),
                pltpu.VMEM((full, HEAD_DIM), F32),
                pltpu.VMEM((full, HEAD_DIM), F32),
                pltpu.VMEM((full, HEAD_DIM), F32),
                pltpu.VMEM((FSDP, rows, model), F32),
            ],
        ),
        out_shape=[shape((count, rows, 3 * HEAD_DIM * heads), BF)] * 4 + [shape((count, rows, model), BF)] * 4,
        cost_estimate=cost(35),
        name="attend_back",
    )(lengths, own, *held, *grads, qkv_mat, out_mat, cos, sin)
    return outs[0:4], outs[4:8]


ROOT = 0.7978845608028654
CUBE = 0.044715


def feed_body(limit_ref, *refs):
    h_refs, g_refs, (in_ref, down_ref) = refs[0:2], refs[2:4], refs[4:6]
    f_refs, dh_refs, a_refs, du_refs = refs[6:8], refs[8:10], refs[10:12], refs[12:14]
    f_acc, dh_acc = refs[14:16]
    step = pl.program_id(0)
    count = h_refs[0].shape[0]
    tile = in_ref.shape[1]

    @pl.when(step == 0)
    def _():
        f_acc[...] = jnp.zeros_like(f_acc)
        dh_acc[...] = jnp.zeros_like(dh_acc)

    for r in range(2):
        for s in range(count):
            limit = limit_ref[r, s] - step * tile

            @pl.when(limit > 0)
            def _():
                h, g = h_refs[r][s], g_refs[r][s]
                pre = dot(h, in_ref[...], NN)
                keep = lax.broadcasted_iota(jnp.int32, pre.shape, 1) < limit
                bend = jnp.tanh(ROOT * (pre + CUBE * pre * pre * pre))
                half = 0.5 * (1.0 + bend)
                slope = half + 0.5 * pre * (1.0 - bend * bend) * (ROOT * (1.0 + 3.0 * CUBE * pre * pre))
                active = jnp.where(keep, pre * half, 0.0).astype(BF)
                a_refs[r][s] = active
                f_acc[r, s] += dot(active, down_ref[...], NN)
                back = dot(g, down_ref[...], NT)
                grad = jnp.where(keep, back * slope, 0.0).astype(BF)
                du_refs[r][s] = grad
                dh_acc[r, s] += dot(grad, in_ref[...], NT)

            @pl.when(limit <= 0)
            def _():
                a_refs[r][s] = jnp.zeros_like(a_refs[r][s])
                du_refs[r][s] = jnp.zeros_like(du_refs[r][s])

    @pl.when(step == pl.num_programs(0) - 1)
    def _():
        for r in range(2):
            f_refs[r][...] = f_acc[r].astype(f_refs[r].dtype)
            dh_refs[r][...] = dh_acc[r].astype(dh_refs[r].dtype)


def feed_both(limits, h, g, in_mat, down_mat):
    count, rows, model = h[0].shape
    hidden = in_mat.shape[1]
    tile = 256
    held = pl.BlockSpec((count, rows, model), lambda t, *_: (0, 0, 0))
    units = pl.BlockSpec((count, rows, tile), lambda t, *_: (0, 0, t))
    outs = pl.pallas_call(
        feed_body,
        grid_spec=pltpu.PrefetchScalarGridSpec(
            num_scalar_prefetch=1,
            grid=(hidden // tile,),
            in_specs=[held] * 4
            + [
                pl.BlockSpec((model, tile), lambda t, *_: (0, t)),
                pl.BlockSpec((tile, model), lambda t, *_: (t, 0)),
            ],
            out_specs=[held] * 4 + [units] * 4,
            scratch_shapes=[pltpu.VMEM((2, count, rows, model), F32)] * 2,
        ),
        out_shape=[jax.ShapeDtypeStruct(h[0].shape, BF)] * 4
        + [jax.ShapeDtypeStruct((count, rows, hidden), BF)] * 4,
        cost_estimate=cost(20),
        name="feed_both",
    )(limits, *h, *g, in_mat, down_mat)
    return outs[0:2], outs[2:4], outs[4:6], outs[6:8]


def left_tiles_body(limit_ref, *refs):
    left, right = refs[0:4], refs[4:8]
    out_ref, acc = refs[8], refs[9]
    tile = out_ref.shape[0]
    acc[...] = jnp.zeros_like(acc)
    for r in range(FSDP):
        for s in range(left[0].shape[0]):

            @pl.when(limit_ref[r, s] > pl.program_id(0) * tile)
            def _():
                acc[...] += dot(left[r][s], right[r][s], TN)

    out_ref[...] = acc[...].astype(BF)


def left_tiles(limits, left, right, tile):
    count, rows, wide = left[0].shape
    cols = right[0].shape[2]
    return pl.pallas_call(
        left_tiles_body,
        grid_spec=pltpu.PrefetchScalarGridSpec(
            num_scalar_prefetch=1,
            grid=(wide // tile,),
            in_specs=[pl.BlockSpec((count, rows, tile), lambda t, *_: (0, 0, t))] * 4
            + [pl.BlockSpec((count, rows, cols), lambda t, *_: (0, 0, 0))] * 4,
            out_specs=pl.BlockSpec((tile, cols), lambda t, *_: (t, 0)),
            scratch_shapes=[pltpu.VMEM((tile, cols), F32)],
        ),
        out_shape=jax.ShapeDtypeStruct((wide, cols), BF),
        cost_estimate=cost(12),
        name="left_tiles",
    )(limits, *left, *right)


def right_tiles_body(limit_ref, *refs):
    left, right = refs[0:4], refs[4:8]
    out_ref, acc, turned = refs[8:11]
    tile = out_ref.shape[1]
    count = left[0].shape[0]

    @pl.when(pl.program_id(0) == 0)
    def _():
        for r in range(FSDP):
            for s in range(count):
                turned[r * count + s] = left[r][s].T

    acc[...] = jnp.zeros_like(acc)
    for r in range(FSDP):
        for s in range(count):

            @pl.when(limit_ref[r, s] > pl.program_id(0) * tile)
            def _():
                acc[...] += dot(turned[r * count + s], right[r][s], NN)

    out_ref[...] = acc[...].astype(BF)


def right_tiles(limits, left, right, tile):
    count, rows, wide = left[0].shape
    cols = right[0].shape[2]
    return pl.pallas_call(
        right_tiles_body,
        grid_spec=pltpu.PrefetchScalarGridSpec(
            num_scalar_prefetch=1,
            grid=(cols // tile,),
            in_specs=[pl.BlockSpec((count, rows, wide), lambda t, *_: (0, 0, 0))] * 4
            + [pl.BlockSpec((count, rows, tile), lambda t, *_: (0, 0, t))] * 4,
            out_specs=pl.BlockSpec((wide, tile), lambda t, *_: (0, t)),
            scratch_shapes=[pltpu.VMEM((wide, tile), F32), pltpu.VMEM((4 * count, wide, rows), BF)],
        ),
        out_shape=jax.ShapeDtypeStruct((wide, cols), BF),
        cost_estimate=cost(14),
        name="right_tiles",
    )(limits, *left, *right)


def turned_tiles_body(limit_ref, *refs):
    left, right, out_ref, acc = refs[0:4], refs[4:8], refs[8], refs[9]
    acc[...] = jnp.zeros_like(acc)
    for r in range(FSDP):
        for s in range(left[0].shape[0]):

            @pl.when(limit_ref[r, s] > 0)
            def _():
                acc[...] += dot(left[r][s], right[r][s], NN)

    out_ref[...] = acc[...].astype(BF)


def turned_tiles(limits, left, right):
    count, wide, rows = left[0].shape
    cols = right[0].shape[2]
    step = 512
    return pl.pallas_call(
        turned_tiles_body,
        grid_spec=pltpu.PrefetchScalarGridSpec(
            num_scalar_prefetch=1,
            grid=(wide // step,),
            in_specs=[pl.BlockSpec((count, step, rows), lambda t, *_: (0, t, 0))] * 4
            + [pl.BlockSpec((count, rows, cols), lambda t, *_: (0, 0, 0))] * 4,
            out_specs=pl.BlockSpec((step, cols), lambda t, *_: (t, 0)),
            scratch_shapes=[pltpu.VMEM((step, cols), F32)],
        ),
        out_shape=jax.ShapeDtypeStruct((wide, cols), BF),
        cost_estimate=cost(20),
        name="turned_tiles",
    )(limits, *left, *right)


def place_body(at_ref, near_ref, far_ref, out_ref):
    half = pl.num_programs(0) // 2

    @pl.when(pl.program_id(0) < half)
    def _():
        out_ref[...] = near_ref[...]

    @pl.when(pl.program_id(0) >= half)
    def _():
        out_ref[...] = far_ref[...]


def place(near, far, ats):
    half, rows, cols = near.shape
    return pl.pallas_call(
        place_body,
        grid_spec=pltpu.PrefetchScalarGridSpec(
            num_scalar_prefetch=1,
            grid=(2 * half,),
            in_specs=[
                pl.BlockSpec((1, rows, cols), lambda n, *_: (jnp.minimum(n, half - 1), 0, 0)),
                pl.BlockSpec((1, rows, cols), lambda n, *_: (jnp.maximum(n - half, 0), 0, 0)),
            ],
            out_specs=pl.BlockSpec((1, rows, cols), lambda n, at: (at[n], 0, 0)),
        ),
        out_shape=jax.ShapeDtypeStruct((2 * half, rows, cols), near.dtype),
        cost_estimate=cost(6),
        name="place",
    )(ats, near, far)


class Moves:
    def __init__(self, dp):
        self.dp = dp
        self.at = lax.axis_index("dp")
        self.own = lax.axis_index("fsdp")
        self.bits = [1 << n for n in range(dp.bit_length() - 1)]

    def peer(self, value, r):
        return lax.ppermute(value, "fsdp", [(j, j ^ r) for j in range(FSDP)])

    def swap(self, value, bit):
        return lax.ppermute(value, "dp", [(i, i ^ bit) for i in range(self.dp)])

    def gather_far(self, *shards):
        shards = [shard[None] for shard in shards]
        for bit in self.bits[:0:-1]:
            shards = [jnp.concatenate([parts, self.swap(parts, bit)]) for parts in shards]
            shards[1:] = [after(parts, shards[0]) for parts in shards[1:]]
        return shards

    def placed(self, parts, swapped):
        marks = [0]
        for bit in self.bits[:0:-1]:
            marks += [mark ^ bit for mark in marks]
        marks += [mark ^ 1 for mark in marks]
        return place(parts, swapped, (self.at ^ jnp.array(marks)).astype(jnp.int32))

    def halves(self, total, bit):
        mine = (self.at // bit) % 2
        pairs = total.reshape(total.shape[0] // 2, 2, *total.shape[1:])
        sent = lax.dynamic_index_in_dim(pairs, 1 - mine, 1, keepdims=False).astype(BF)
        return sent, lax.dynamic_index_in_dim(pairs, mine, 1, keepdims=False)

    def reduce_far(self, total, done, *earlier):
        for bit in self.bits[done:]:
            sent, kept = self.halves(total, bit)
            total = after(kept, *earlier).astype(F32) + self.swap(sent, bit).astype(F32)
        return total.reshape(total.shape[1:])

    def exchange(self, pieces):
        return lax.all_to_all(pieces, "fsdp", 0, 0, tiled=True)

    def total(self, value):
        devices = self.dp * FSDP
        parts = value.reshape(value.shape[0], devices, -1).transpose(1, 0, 2)
        size = parts.shape[2]
        parts = lax.all_to_all(parts.reshape(devices, -1), ("dp", "fsdp"), 0, 0, tiled=True)
        return jnp.sum(parts, axis=0).reshape(-1, size)

    def spread(self, block):
        across = self.peer(block, 2)
        return [block, self.peer(block, 1), across, self.peer(across, 1)]

    def far_sum(self, terms):
        return (terms[2].astype(F32) + self.peer(terms[3], 1).astype(F32)).astype(BF)

    def near_sum(self, terms, across):
        return sum_of(terms[0], self.peer(terms[1], 1), across)


def sum_of(*terms):
    return functools.reduce(jnp.add, [term.astype(F32) for term in terms])


def after(value, *earlier):
    return lax.optimization_barrier((value,) + earlier)[0]


def local(
    dp,
    tokens,
    seq_lengths,
    seq_buckets,
    bucket_widths,
    norm_one_gain,
    norm_one_bias,
    qkv_weight,
    out_weight,
    norm_two_gain,
    norm_two_bias,
    ffn_in_weight,
    ffn_out_weight,
    cotangent,
):
    moves = Moves(dp)
    count, rows, model = tokens.shape
    full = rows * FSDP
    slice_rows = norm_one_gain.shape[0]
    ffn = ffn_in_weight.shape[1]
    hidden = ffn // FSDP
    stripe = ffn // (dp * FSDP)
    own = moves.own
    own_array = own.astype(jnp.int32).reshape(1)
    home = [((i * FSDP + j), (j * dp + i)) for i in range(dp) for j in range(FSDP)]
    outward = [(b, a) for a, b in home]

    third = model // FSDP
    heads = third // HEAD_DIM
    qkv_pieces = qkv_weight.reshape(slice_rows, 3, FSDP, heads, HEAD_DIM).transpose(2, 0, 3, 1, 4)
    qkv_shard = moves.exchange(qkv_pieces.reshape(FSDP, slice_rows, 3 * third))
    qkv_shard = qkv_shard.reshape(FSDP * slice_rows, 3 * third)
    vectors = jnp.concatenate([norm_one_gain, norm_one_bias, norm_two_gain, norm_two_bias])
    vectors = jnp.broadcast_to(after(vectors, qkv_shard)[None], (dp * FSDP, 4 * slice_rows))
    parts = lax.all_to_all(vectors, ("dp", "fsdp"), 0, 0, tiled=True)
    vectors = parts.reshape(dp * FSDP, 4, slice_rows).transpose(1, 0, 2).reshape(4, model).astype(F32)
    gain_one, bias_one, gain_two, bias_two = vectors[0], vectors[1], vectors[2], vectors[3]
    in_pieces = ffn_in_weight.reshape(slice_rows, dp, FSDP, stripe).transpose(2, 0, 1, 3)
    in_pieces = in_pieces.reshape(FSDP, slice_rows, hidden)
    in_shard = moves.exchange(after(in_pieces, parts)).reshape(FSDP * slice_rows, hidden)
    out_shard = lax.ppermute(out_weight, ("dp", "fsdp"), outward)
    out_far, qkv_far = moves.gather_far(out_shard, qkv_shard)
    qkv_swapped = moves.swap(qkv_far, 1)
    token_blocks = moves.spread(after(tokens, qkv_shard))
    early = (in_shard, token_blocks[2])
    down_mat = lax.all_gather(after(ffn_out_weight, qkv_far, *early), "dp", axis=0, tiled=True)
    in_mat = lax.all_gather(after(in_shard, qkv_swapped), "dp", axis=0, tiled=True)
    out_mat = moves.placed(out_far, moves.swap(out_far, 1)).reshape(third, model)

    positions = [(own ^ r) * rows + jnp.arange(rows) for r in range(FSDP)]
    live = [(p[None, :] < seq_lengths[:, None])[..., None] for p in positions]
    prefix = jnp.sum(
        jnp.where(jnp.arange(BUCKETS)[None, :] == seq_buckets[:, None], bucket_widths[None, :], 0), axis=1
    )
    turn = FSDP * stripe
    units = (prefix // turn) * stripe + jnp.clip(prefix % turn - own * stripe, 0, stripe)
    starts = (own ^ jnp.arange(FSDP)) * rows
    alive = starts[:, None] < seq_lengths[None, :]
    unit_limits = jnp.where(alive, units[None, :], 0).astype(jnp.int32)
    row_limits = jnp.where(alive, 1 << 20, 0).astype(jnp.int32)
    cos, sin = rotary_tables(full)

    inputs = tokens.astype(F32)
    normed_one = []
    for block in token_blocks:
        value, _ = normalize(block.astype(F32))
        normed_one.append((value * gain_one + bias_one).astype(BF))
    qkv_mat = moves.placed(qkv_far, after(qkv_swapped, *normed_one)).reshape(model, -1)
    feed_grad = jnp.where(live[0], cotangent, jnp.zeros_like(cotangent))
    feed_grad = moves.spread(after(feed_grad, token_blocks[2]))
    lengths = after(seq_lengths, feed_grad[2], in_shard)
    branch, attended, turned_one, held = attend(lengths, own_array, normed_one, qkv_mat, out_mat, cos, sin)
    across = moves.peer(after(moves.far_sum(branch), down_mat), 2)
    middle = inputs + moves.near_sum(branch, across)
    unit_two, scale_two = normalize(middle)
    normed_two = moves.spread((unit_two * gain_two + bias_two).astype(BF))

    feed, normed_two_grad, active, hidden_grad = [], [], [], []
    for r in (0, 2):
        pair = slice(r, r + 2)
        gate = after(unit_limits[pair], *feed)
        results = feed_both(gate, normed_two[pair], feed_grad[pair], in_mat, down_mat)
        for kept, result in zip((feed, normed_two_grad, active, hidden_grad), results):
            kept.extend(result)

    upstream = jnp.where(live[0], cotangent.astype(F32), 0.0)
    far = moves.far_sum(normed_two_grad)
    gate = after(unit_limits, far)
    grad_down = left_tiles(gate, active, feed_grad, 256)
    grad_in = right_tiles(after(gate, grad_down), normed_two, hidden_grad, 256)
    in_sent, in_kept = moves.halves(grad_in.reshape(dp, -1, hidden), 1)
    in_swapped = moves.swap(in_sent, 1)
    second_grad = moves.near_sum(normed_two_grad, moves.peer(far, 2))
    second_grad = after(second_grad, in_sent)
    grad_gain_two = jnp.sum(second_grad * unit_two, axis=(0, 1))
    grad_bias_two = jnp.sum(second_grad, axis=(0, 1))
    middle_grad = upstream + norm_back(second_grad, gain_two, unit_two, scale_two)
    branch_grad = moves.spread(middle_grad.astype(BF))

    grad_down = lax.psum_scatter(grad_down, "dp", scatter_dimension=0, tiled=True)
    out_terms = left_tiles(row_limits, attended, branch_grad, third).reshape(dp, -1, model)
    out_sent, out_kept = moves.halves(out_terms, 1)
    feed[3] = after(feed[3], branch_grad[2])
    far = moves.far_sum(feed)
    across = moves.peer(far, 2)
    beside = moves.peer(feed[1], 1)
    grad_in = after(in_kept, branch_grad[2]).astype(F32) + in_swapped.astype(F32)
    in_sent, in_kept = moves.halves(grad_in, moves.bits[1])
    in_swapped = moves.swap(in_sent, moves.bits[1])
    qkv_grad, normed_one_grad = attend_back(
        after(seq_lengths, far, beside, out_sent, in_sent), own_array, held, branch_grad, qkv_mat, out_mat, cos, sin
    )
    layer_output = jnp.where(live[0], middle + sum_of(feed[0], beside, across), 0.0).astype(BF)
    out_swapped = moves.swap(out_sent, 1)
    far = moves.far_sum([*normed_one_grad[:3], after(normed_one_grad[3], across, out_swapped, in_swapped)])
    gate = after(row_limits, far)
    grad_out = moves.reduce_far(after(out_kept, far).astype(F32) + out_swapped.astype(F32), 1)
    grad_in = moves.reduce_far(after(in_kept, far).astype(F32) + in_swapped.astype(F32), 2, grad_down)
    grad_in = moves.exchange(grad_in.astype(BF).reshape(FSDP, slice_rows, hidden))
    across = moves.peer(far, 2)
    sent, kept = moves.halves(turned_tiles(gate, turned_one, qkv_grad).reshape(dp, -1, 3 * third), 1)
    kept = after(kept, across)
    grad_qkv = moves.reduce_far(kept.astype(F32) + moves.swap(sent, 1).astype(F32), 1, grad_in)
    first_grad = moves.near_sum(normed_one_grad, across)
    unit_one, scale_one = normalize(inputs)
    input_grad = middle_grad + norm_back(first_grad, gain_one, unit_one, scale_one)
    grad_gain_one = jnp.sum(first_grad * unit_one, axis=(0, 1))
    grad_bias_one = jnp.sum(first_grad, axis=(0, 1))
    sums = moves.total(jnp.stack([grad_gain_one, grad_bias_one, grad_gain_two, grad_bias_two]))

    grad_out = lax.ppermute(grad_out, ("dp", "fsdp"), home)
    grad_qkv = moves.exchange(grad_qkv.astype(BF).reshape(FSDP, slice_rows, 3 * third))
    grad_qkv = grad_qkv.reshape(FSDP, slice_rows, heads, 3, HEAD_DIM).transpose(1, 3, 0, 2, 4).astype(F32)
    grad_qkv = grad_qkv.reshape(slice_rows, 3 * model)
    grad_in = grad_in.reshape(FSDP, slice_rows, dp, stripe).transpose(1, 2, 0, 3).astype(F32)
    grad_in = grad_in.reshape(slice_rows, ffn)
    return (
        layer_output,
        input_grad,
        sums[0],
        sums[1],
        grad_qkv,
        grad_out,
        sums[2],
        sums[3],
        grad_in,
        grad_down.astype(F32),
    )


def solution(mesh):
    both = ("dp", "fsdp")
    placed = (
        P("dp", "fsdp", None),
        P("dp"),
        P("dp"),
        P(),
        P(both),
        P(both),
        P(both, None),
        P(both, None),
        P(both),
        P(both),
        P(both, None),
        P(both, None),
        P("dp", "fsdp", None),
    )
    return jax.shard_map(
        functools.partial(local, mesh.shape["dp"]),
        mesh=mesh,
        in_specs=placed,
        out_specs=(
            P("dp", "fsdp", None),
            P("dp", "fsdp", None),
            P(both),
            P(both),
            P(both, None),
            P(both, None),
            P(both),
            P(both),
            P(both, None),
            P(both, None),
        ),
        check_vma=False,
    )
```
